32 devices in a mesh: lat: 4 (over x, core), lon: 8 (over z, y).
Axes of the slice: x: 2, y: 2, z: 4, core: 2. Of those that a mesh axis runs over, the one named last changes fastest.
Arguments:
- source: float32 [1024, 16384], P('lat', 'lon'), may hold values from -80 to 80
- flags: int32 [8, 128], P('lat', 'lon'), may hold values from 0 to 2
Outputs:
- solution: float32 [1024, 16384], P('lat', 'lon')
- residual: float32 [1024, 16384], P('lat', 'lon')
The draws below stay inside these ranges and needn't reach their ends.
All inputs are finite; a program needn't handle non-finite values.
Results may differ from the reference program's by a relative error of at most 0.0001.
Values sent between devices are 32-bit elements; how exact they have to be, the bound alone decides.
No kernel may reach another device: no remote copies, remote signals or barrier semaphores. Data moves between devices by JAX's collectives and lax.ppermute only.
A program may use at most 64 MiB of HBM per device.

```python
import math
import jax
import jax.numpy as jnp

ITERS = 2
NR = 1024
NC = 16384
TR = 8
TC = 128


def draw_source(key, part):
    key_base, key_rough = jax.random.split(key, 2)
    col_pos = jnp.arange(NC, dtype=jnp.float32)[None, :]
    row_pos = jnp.arange(NR, dtype=jnp.float32)[:, None]
    ramp = (1.0 + 2.0 * col_pos / (NC - 1)) * (1.0 + 2.0 * row_pos / (NR - 1))
    rough = jax.random.uniform(key_rough, (NR, NC), jnp.float32, 0.5, 2.0)
    base = jnp.clip(jax.random.normal(key_base, (NR, NC), jnp.float32), -4.0, 4.0)
    return base * rough * ramp


def touch_ends(entries, stream_key, smallest, largest):
    longest = entries.shape.index(max(entries.shape))
    spots = []
    for shift in (0, 1):
        where = [jax.random.randint(jax.random.fold_in(stream_key, axis), (), 0, length) for axis, length in enumerate(entries.shape)]
        where[longest] = (where[longest] + shift) % entries.shape[longest]
        spots.append(tuple(where))
    return entries.at[spots[0]].set(smallest).at[spots[1]].set(largest)


def setup_inputs(seed: int = 0) -> dict:
    seeds = jax.random.split(jax.random.key(seed), 3)
    return {
        "source": draw_source(jax.random.fold_in(seeds[2], 71), 0),
        "flags": touch_ends(jax.random.randint(seeds[1], (TR, TC), 0, 3), jax.random.fold_in(seeds[1], 1), 0, 2).astype(jnp.int32),
    }


ARC_SPAN = 2.0 * math.pi / 3.0


def reference(source, flags):
    row_pos = jnp.arange(NR, dtype=jnp.float32)
    east_west = jnp.cos((row_pos + 0.5) / NR * ARC_SPAN - 0.5 * ARC_SPAN)[:, None]
    upper = jnp.cos(row_pos / NR * ARC_SPAN - 0.5 * ARC_SPAN)[:, None]
    lower = jnp.cos((row_pos + 1.0) / NR * ARC_SPAN - 0.5 * ARC_SPAN)[:, None]
    levels = jnp.repeat(jnp.repeat(flags, 128, axis=0), 128, axis=1)
    screen = jnp.where(levels == 0, 0.05, jnp.where(levels == 1, 0.4, 2.0)).astype(jnp.float32)
    diag = screen + 2.0 * east_west + upper + lower

    def operate(value):
        zero_row = jnp.zeros((1, NC), dtype=value.dtype)
        above = jnp.concatenate([zero_row, value[:-1]], axis=0)
        below = jnp.concatenate([value[1:], zero_row], axis=0)
        east_side = jnp.roll(value, -1, axis=1)
        west_side = jnp.roll(value, 1, axis=1)
        return diag * value - east_west * (east_side + west_side) - upper * above - lower * below

    solution = jnp.zeros_like(source)
    remain = source
    precond = remain / diag
    search = precond
    energy = jnp.sum(remain * precond)
    for step in range(ITERS):
        image = operate(search)
        alpha = energy / jnp.sum(search * image)
        solution = solution + alpha * search
        remain = remain - alpha * image
        precond = remain / diag
        fresh = jnp.sum(remain * precond)
        search = precond + (fresh / energy) * search
        energy = fresh
    return solution, remain
```

```python
import math

import jax
import jax.numpy as jnp
from jax import lax
from jax.sharding import PartitionSpec as P

ARC_SPAN = 2.0 * math.pi / 3.0


def shifted(block, axis, periodic):
    count = lax.axis_size(axis)
    forward = [(i, i + 1) for i in range(count - 1)]
    if periodic:
        forward.append((count - 1, 0))
    backward = [(target, source) for source, target in forward]
    return forward, backward


def halos(value):
    up, down = shifted(value, "lat", False)
    east, west = shifted(value, "lon", True)
    above = lax.ppermute(value[-1:], "lat", up)
    below = lax.ppermute(value[:1], "lat", down)
    cols = value[:, -1].reshape(1, -1), value[:, 0].reshape(1, -1)
    west_side = lax.ppermute(cols[0], "lon", east)
    east_side = lax.ppermute(cols[1], "lon", west)
    return above, below, west_side.reshape(-1, 1), east_side.reshape(-1, 1)


def geometry(start, count, total_rows):
    row_pos = (start + jnp.arange(count, dtype=jnp.int32)).astype(jnp.float32)
    east_west = jnp.cos((row_pos + 0.5) / total_rows * ARC_SPAN - 0.5 * ARC_SPAN)[:, None]
    upper = jnp.cos(row_pos / total_rows * ARC_SPAN - 0.5 * ARC_SPAN)[:, None]
    lower = jnp.cos((row_pos + 1.0) / total_rows * ARC_SPAN - 0.5 * ARC_SPAN)[:, None]
    return east_west, upper, lower


def screen_cells(tiles):
    values = jnp.where(tiles == 0, 0.05, jnp.where(tiles == 1, 0.4, 2.0)).astype(jnp.float32)
    tile_rows, tile_cols = values.shape
    spread = jnp.broadcast_to(values[:, None, :, None], (tile_rows, 128, tile_cols, 128))
    return spread.reshape(tile_rows * 128, tile_cols * 128)


def neighbours(value, coeffs):
    east_west, upper, lower = coeffs
    above, below, west, east = halos(value)
    above = jnp.concatenate([above, value[:-1]], axis=0)
    below = jnp.concatenate([value[1:], below], axis=0)
    west = jnp.concatenate([west, value[:, :-1]], axis=1)
    east = jnp.concatenate([value[:, 1:], east], axis=1)
    return east_west * (east + west) + upper * above + lower * below


def total(parts):
    value = jnp.pad(jnp.stack(parts)[None, :], ((0, 0), (0, 128 - len(parts))))
    for axis in ("lat", "lon"):
        count = lax.axis_size(axis)
        step = 1
        while step < count:
            value = value + lax.ppermute(value, axis, [(i, i ^ step) for i in range(count)])
            step *= 2
    return [value[0, i] for i in range(len(parts))]


def per_device(source, flags):
    band_rows, sector_cols = source.shape
    total_rows = band_rows * lax.axis_size("lat")
    coeffs = geometry(lax.axis_index("lat") * band_rows, band_rows, total_rows)
    east_west, upper, lower = coeffs
    diag = screen_cells(flags) + 2.0 * east_west + upper + lower
    inverse = 1.0 / diag
    base = source * inverse
    first = source - neighbours(base, coeffs)
    scaled = first * inverse
    second = first - neighbours(scaled, coeffs)
    sums = total(
        [
            jnp.sum(source * base),
            jnp.sum(base * first),
            jnp.sum(scaled * first),
            jnp.sum(scaled * second),
        ]
    )
    alpha = sums[0] / sums[1]
    fresh = alpha * alpha * sums[2] - 2.0 * alpha * sums[1] + sums[0]
    grow = 1.0 + fresh / sums[0]
    bend = grow * grow * sums[1] - 2.0 * grow * alpha * sums[2] + alpha * alpha * sums[3]
    beta = fresh / bend
    near, far = alpha + beta * grow, alpha * beta
    return near * base - far * scaled, source - near * first + far * second


def solution(mesh):
    in_specs = (P("lat", "lon"), P("lat", "lon"))
    out_specs = (P("lat", "lon"), P("lat", "lon"))
    return jax.shard_map(
        per_device, mesh=mesh, in_specs=in_specs, out_specs=out_specs, check_vma=False
    )
```

```python
import functools
import math

import jax
import jax.numpy as jnp
from jax import lax
from jax.experimental import pallas as pl
from jax.experimental.pallas import tpu as pltpu
from jax.sharding import PartitionSpec as P

ARC_SPAN = 2.0 * math.pi / 3.0
TILE = 128
SUB = 8
VMEM_SPEC = pl.BlockSpec(memory_space=pltpu.VMEM)
SMEM_SPEC = pl.BlockSpec(memory_space=pltpu.SMEM)
Z0, U0, V0, Z1, U1, V1, I0, I1 = range(8)
EAST_WEST, UPPER, LOWER, INNER = range(4)


def coefficient_table(total_rows):
    row_pos = jnp.arange(total_rows, dtype=jnp.int32).astype(jnp.float32)
    east_west = jnp.cos((row_pos + 0.5) / total_rows * ARC_SPAN - 0.5 * ARC_SPAN)
    upper = jnp.cos(row_pos / total_rows * ARC_SPAN - 0.5 * ARC_SPAN)
    lower = jnp.cos((row_pos + 1.0) / total_rows * ARC_SPAN - 0.5 * ARC_SPAN)
    inner = jnp.where(row_pos == total_rows - 1, 0.0, lower)
    zero = jnp.zeros_like(lower)
    return jnp.stack([east_west, upper, lower, inner, zero, zero, zero, zero])


def fold(row):
    total = row[:, :TILE]
    for start in range(TILE, row.shape[1], TILE):
        total = total + row[:, start : start + TILE]
    return total


def wide(cell, width=TILE):
    return jnp.broadcast_to(cell, (cell.shape[0], width))


def after(row):
    return pltpu.roll(row, row.shape[1] - 1, 1)


def before(row):
    return pltpu.roll(row, 1, 1)


def lane_ids(rows, width=TILE):
    return lax.broadcasted_iota(jnp.int32, (rows, width), 1)


def local_kernel(flags, tabs, src, z, u, w, v, pack, inv, ew_t, up_t, lo_t):
    rows, cols = src.shape
    tiles = cols // TILE
    blocks = TILE // SUB
    start = pl.multiple_of(lax.axis_index("lat") * rows, rows)
    band = jnp.transpose(tabs[:, pl.ds(start, rows)])
    ew = wide(band[:, EAST_WEST : EAST_WEST + 1])
    up = wide(band[:, UPPER : UPPER + 1])
    lo = wide(band[:, LOWER : LOWER + 1])
    ew_t[...] = ew
    up_t[...] = up
    lo_t[...] = lo
    for kind, screen in enumerate((0.05, 0.4, 2.0)):
        inv[kind] = 1.0 / (screen + 2.0 * ew + up + lo)
    nothing = jnp.zeros((SUB, cols), jnp.float32)
    for padded in (z, u):
        padded[:SUB] = nothing
        padded[rows + SUB :] = nothing
    zero = jnp.zeros((SUB, TILE), jnp.float32)
    row_id = lax.broadcasted_iota(jnp.int32, (SUB, TILE), 0)
    lane = lane_ids(SUB)
    kinds = [
        [
            jnp.where(flags[band_row, c] == 0, 0, jnp.where(flags[band_row, c] == 1, 1, 2))
            for c in range(tiles)
        ]
        for band_row in range(rows // TILE)
    ]

    def columns(c):
        return pl.ds(c * TILE, TILE)

    def around(field, at, c, here, west, east, coeffs):
        prev = field[pl.ds(at, SUB), columns(c)]
        later = field[pl.ds(at + 2 * SUB, SUB), columns(c)]
        above = pltpu.roll(jnp.where(row_id == SUB - 1, prev, here), 1, 0)
        below = pltpu.roll(jnp.where(row_id == 0, later, here), SUB - 1, 0)
        right = pltpu.roll(jnp.where(lane == 0, east, here), TILE - 1, 1)
        left = pltpu.roll(jnp.where(lane == TILE - 1, west, here), 1, 1)
        e, a, b = coeffs
        return e * (right + left) + a * above + b * below

    def sweep(body, count):
        sums = (zero,) * count
        for band_row in range(rows // TILE):

            def step(k, carry, band_row=band_row):
                at = pl.multiple_of(band_row * TILE + k * SUB, SUB)
                return body(at, kinds[band_row], carry)

            sums = lax.fori_loop(0, blocks, step, sums)
        return sums

    def first_pass(at, kind, carry):
        (m0,) = carry
        for c in range(tiles):
            b = src[pl.ds(at, SUB), columns(c)]
            value = b * inv[kind[c], pl.ds(at, SUB), :]
            z[pl.ds(at + SUB, SUB), columns(c)] = value
            m0 = m0 + b * value
        return (m0,)

    def second_pass(at, kind, carry):
        m1, m2 = carry
        here_rows = pl.ds(at, SUB)
        coeffs = ew_t[here_rows, :], up_t[here_rows, :], lo_t[here_rows, :]
        line = [zero] + [z[pl.ds(at + SUB, SUB), columns(c)] for c in range(tiles)] + [zero]
        for c in range(tiles):
            here = line[c + 1]
            near = around(z, at, c, here, line[c], line[c + 2], coeffs)
            image = src[here_rows, columns(c)] - near
            scaled = image * inv[kind[c], here_rows, :]
            w[here_rows, columns(c)] = image
            u[pl.ds(at + SUB, SUB), columns(c)] = scaled
            m1 = m1 + here * image
            m2 = m2 + scaled * image
        return m1, m2

    def third_pass(at, kind, carry):
        (m3,) = carry
        here_rows = pl.ds(at, SUB)
        coeffs = ew_t[here_rows, :], up_t[here_rows, :], lo_t[here_rows, :]
        line = [zero] + [u[pl.ds(at + SUB, SUB), columns(c)] for c in range(tiles)] + [zero]
        for c in range(tiles):
            here = line[c + 1]
            near = around(u, at, c, here, line[c], line[c + 2], coeffs)
            image = w[here_rows, columns(c)] - near
            v[here_rows, columns(c)] = image
            m3 = m3 + here * image
        return (m3,)

    (m0,) = sweep(first_pass, 1)
    m1, m2 = sweep(second_pass, 2)
    (m3,) = sweep(third_pass, 1)

    last = rows - 1
    pack[Z0 : Z0 + 1, :cols] = z[SUB : SUB + 1, :]
    pack[U0 : U0 + 1, :cols] = u[SUB : SUB + 1, :]
    pack[V0 : V0 + 1, :cols] = v[:1, :]
    pack[Z1 : Z1 + 1, :cols] = z[last + SUB : last + SUB + 1, :]
    pack[U1 : U1 + 1, :cols] = u[last + SUB : last + SUB + 1, :]
    pack[V1 : V1 + 1, :cols] = v[last:, :]
    for c in range(tiles):
        pack[I0 : I0 + 1, c * TILE : (c + 1) * TILE] = inv[kinds[0][c], :1, :]
        pack[I1 : I1 + 1, c * TILE : (c + 1) * TILE] = inv[kinds[-1][c], last:, :]

    for band_row in range(rows // TILE):
        here_rows = slice(band_row * TILE, (band_row + 1) * TILE)
        inner_rows = slice(band_row * TILE + SUB, (band_row + 1) * TILE + SUB)
        east = slice(cols - TILE, cols)
        ids = lane_ids(TILE)
        mix = inv[kinds[band_row][-1], here_rows, :]
        mix = jnp.where(ids == I0, inv[kinds[band_row][0], here_rows, :], mix)
        mix = jnp.where(ids == V1, pltpu.roll(v[here_rows, east], V1 + 1, 1), mix)
        mix = jnp.where(ids == U1, pltpu.roll(u[inner_rows, east], U1 + 1, 1), mix)
        mix = jnp.where(ids == Z1, pltpu.roll(z[inner_rows, east], Z1 + 1, 1), mix)
        mix = jnp.where(ids == V0, pltpu.roll(v[here_rows, :TILE], V0, 1), mix)
        mix = jnp.where(ids == U0, pltpu.roll(u[inner_rows, :TILE], U0, 1), mix)
        mix = jnp.where(ids == Z0, z[inner_rows, :TILE], mix)
        at = cols + band_row * TILE
        pack[:, at : at + TILE] = jnp.transpose(mix)[:SUB, :]

    at = cols + rows
    pack[:, at:] = zero
    for i, m in enumerate((m0, m1, m2, m3)):
        pack[i : i + 1, at:] = jnp.sum(m, axis=0, keepdims=True)


def sides(own, other, index, stage):
    size = 2**stage
    lower = lax.rem(lax.div(index, size), 2)
    inside = lax.rem(index, size)
    here, there = own[...], other[...]
    first = jnp.where(lower == 0, here, there)
    second = jnp.where(lower == 0, there, here)
    at_end = (lower == 0) & (inside == size - 1)
    at_start = (lower == 1) & (inside == 0)
    return first, second, at_end, at_start


def row_of(pack, i, start, stop):
    return pack[i : i + 1, start:stop]


def add_moments(out, at, first, second, changes):
    width = first.shape[1]
    out[:, at : at + TILE] = first[:, width - TILE :] + second[:, width - TILE :]
    for i, change in enumerate(changes):
        out[i + 1 : i + 2, at : at + TILE] += change


def lat_kernel(stage, final, cols, tabs, own, other, ext_in, out, ext):
    height = own.shape[1] - cols - TILE
    index = lax.axis_index("lat")
    top, bottom, at_end, at_start = sides(own, other, index, stage)
    size = 2**stage
    border = pl.multiple_of((lax.div(index, 2 * size) * 2 * size + size) * (height // size), TILE)
    low = tabs[:, pl.ds(border, TILE)]
    high = tabs[:, pl.ds(border - TILE, TILE)]
    cross = wide(low[UPPER : UPPER + 1, :1], cols)
    ew_b = wide(low[EAST_WEST : EAST_WEST + 1, :1])
    ew_t = wide(high[EAST_WEST : EAST_WEST + 1, TILE - 1 :])
    next_b = wide(low[LOWER : LOWER + 1, :1])
    next_t = wide(high[UPPER : UPPER + 1, TILE - 1 :])

    zt, ut, vt, it = (row_of(top, i, 0, cols) for i in (Z1, U1, V1, I1))
    zb, ub, vb, ib = (row_of(bottom, i, 0, cols) for i in (Z0, U0, V0, I0))
    et, eb = -cross * zb, -cross * zt
    dt, db = it * et, ib * eb
    full_t, full_b = ut + dt, ub + db
    inside = lane_ids(1, cols) < cols - 1
    pair_t = jnp.where(inside, dt * after(dt), 0.0)
    pair_b = jnp.where(inside, db * after(db), 0.0)
    twice = fold(zt * et)
    second = fold((2.0 * ut + dt) * et + (2.0 * ub + db) * eb)
    third = fold(dt * (2.0 * vt + et) + db * (2.0 * vb + eb) - 2.0 * cross * full_t * full_b)
    third = third - 2.0 * (ew_t * fold(pair_t) + ew_b * fold(pair_b))

    base = 0 if final else cols
    if not final:
        top_rows = (lax.broadcasted_iota(jnp.int32, (SUB, cols), 0) < Z1) | (
            lax.broadcasted_iota(jnp.int32, (SUB, cols), 0) == I0
        )
        out[:, :cols] = jnp.where(top_rows, top[:, :cols], bottom[:, :cols])
    out[:, base : base + height] = top[:, cols : cols + height]
    out[:, base + height : base + 2 * height] = bottom[:, cols : cols + height]
    add_moments(out, base + 2 * height, top, bottom, (2.0 * twice, second, third))

    lane = lane_ids(1)
    upper_at = base + height - TILE
    lower_at = base + height
    c = cross[:, :TILE]
    for edge, inner, u_row, v_row in ((0, 1, U0, V0), (cols - 1, cols - 2, U1, V1)):

        def pick(row, place):
            return wide(row[:, place : place + 1])

        d_top, d_bottom = pick(dt, edge), pick(db, edge)
        v_top = pick(et, edge) - ew_t * pick(dt, inner) - c * pick(full_b, edge)
        v_bottom = pick(eb, edge) - ew_b * pick(db, inner) - c * pick(full_t, edge)
        out[u_row : u_row + 1, upper_at : upper_at + TILE] += jnp.where(
            lane == TILE - 1, d_top, 0.0
        )
        out[u_row : u_row + 1, lower_at : lower_at + TILE] += jnp.where(lane == 0, d_bottom, 0.0)
        out[v_row : v_row + 1, upper_at : upper_at + TILE] += jnp.where(
            lane == TILE - 1, v_top, jnp.where(lane == TILE - 2, -next_t * d_top, 0.0)
        )
        out[v_row : v_row + 1, lower_at : lower_at + TILE] += jnp.where(
            lane == 0, v_bottom, jnp.where(lane == 1, -next_b * d_bottom, 0.0)
        )

    if stage == 0:
        ext[...] = jnp.zeros((SUB, cols), jnp.float32)
    else:
        ext[...] = ext_in[...]

    @pl.when(at_start)
    def _():
        ext[0:1, :] = zt
        ext[1:2, :] = full_t
        ext[2:3, :] = it

    @pl.when(at_end)
    def _():
        ext[3:4, :] = zb
        ext[4:5, :] = full_b
        ext[5:6, :] = ib


def column_border(west, east, tabs):
    height = west.shape[1] - TILE
    zw, uw, vw, iw = (row_of(west, i, 0, height) for i in (Z1, U1, V1, I1))
    ze, ue, ve, ie = (row_of(east, i, 0, height) for i in (Z0, U0, V0, I0))
    ew = tabs[EAST_WEST : EAST_WEST + 1, :]
    inner = tabs[INNER : INNER + 1, :]
    to_w, to_e = -ew * ze, -ew * zw
    dw, de = iw * to_w, ie * to_e
    full_w, full_e = uw + dw, ue + de
    first = 2.0 * fold(zw * to_w)
    second = fold((2.0 * uw + dw) * to_w + (2.0 * ue + de) * to_e)
    third = fold(
        dw * (2.0 * vw + to_w)
        + de * (2.0 * ve + to_e)
        - 2.0 * inner * (dw * after(dw) + de * after(de))
        - 2.0 * ew * full_w * full_e
    )
    return (first, second, third), (zw, full_w), (ze, full_e)


def lon_kernel(stage, tabs, own, other, ext_in, out, ext):
    height = own.shape[1] - TILE
    west, east, at_end, at_start = sides(own, other, lax.axis_index("lon"), stage)
    changes, from_west, from_east = column_border(west, east, tabs)
    ids = lax.broadcasted_iota(jnp.int32, (SUB, height), 0)
    out[:, :height] = jnp.where((ids < Z1) | (ids == I0), west[:, :height], east[:, :height])
    add_moments(out, height, west, east, changes)
    if stage == 0:
        ext[...] = jnp.zeros((SUB, height), jnp.float32)
    else:
        ext[...] = ext_in[...]

    @pl.when(at_start)
    def _():
        ext[0:1, :], ext[1:2, :] = from_west

    @pl.when(at_end)
    def _():
        ext[2:3, :], ext[3:4, :] = from_east


def last_kernel(
    stage, chunk, tabs, own, other, ext_in, edges, row_ext, src, z, u, w, v,
    out_x, out_r, mom, ext, field_x, field_r, cols_t, sems,
):
    rows, cols = src.shape
    height = own.shape[1] - TILE
    tiles = cols // TILE
    sectors = lax.axis_size("lon")
    index = lax.axis_index("lon")
    west, east, at_end, at_start = sides(own, other, index, stage)
    changes, from_west, from_east = column_border(west, east, tabs)
    wrap, round_west, round_east = column_border(east, west, tabs)
    add_moments(mom, 0, west, east, [a + b for a, b in zip(changes, wrap)])
    if stage == 0:
        ext[...] = jnp.zeros((SUB, height), jnp.float32)
    else:
        ext[...] = ext_in[...]

    @pl.when(at_start)
    def _():
        ext[0:1, :], ext[1:2, :] = from_west

    @pl.when(at_end)
    def _():
        ext[2:3, :], ext[3:4, :] = from_east

    @pl.when(index == 0)
    def _():
        ext[0:1, :], ext[1:2, :] = round_west

    @pl.when(index == sectors - 1)
    def _():
        ext[2:3, :], ext[3:4, :] = round_east

    sums = jnp.broadcast_to(jnp.sum(mom[...], axis=1, keepdims=True), (SUB, TILE))
    m0, m1, m2, m3 = (sums[i : i + 1, :] for i in range(4))
    alpha = m0 / m1
    fresh = alpha * alpha * m2 - 2.0 * alpha * m1 + m0
    grow = 1.0 + fresh / m0
    bend = grow * grow * m1 - 2.0 * grow * alpha * m2 + alpha * alpha * m3
    beta = fresh / bend
    near1, far1 = alpha + beta * grow, alpha * beta
    near = jnp.broadcast_to(near1, (SUB, TILE))
    far = jnp.broadcast_to(far1, (SUB, TILE))

    lat = lax.axis_index("lat")
    start = pl.multiple_of(lat * rows, rows)
    here = pl.ds(start, rows)
    ew = tabs[EAST_WEST : EAST_WEST + 1, here]
    up = tabs[UPPER : UPPER + 1, here]
    lo = tabs[LOWER : LOWER + 1, here]
    row_lane = lane_ids(1, rows)
    near_r = jnp.concatenate([near1] * (rows // TILE), axis=1)
    far_r = jnp.concatenate([far1] * (rows // TILE), axis=1)
    mods = []
    for z_row, inv_row in ((0, I0), (2, I1)):
        e = -ew * ext[z_row : z_row + 1, here]
        d = edges[inv_row : inv_row + 1, cols : cols + rows] * e
        above = jnp.where(row_lane == 0, 0.0, before(d))
        below = jnp.where(row_lane == rows - 1, 0.0, after(d))
        dv = e - up * above - lo * below - ew * ext[z_row + 1 : z_row + 2, here]
        mods += [-far_r * d, far_r * dv - near_r * e, -far_r * ew * d]
    mods += [jnp.zeros((1, rows), jnp.float32)] * 2
    cols_t[...] = jnp.transpose(jnp.concatenate(mods, axis=0))

    near_c = jnp.concatenate([near1] * tiles, axis=1)
    far_c = jnp.concatenate([far1] * tiles, axis=1)
    col_lane = lane_ids(1, cols)
    first = tabs[:, pl.ds(start, TILE)]
    final = tabs[:, pl.ds(start + rows - TILE, TILE)]
    clamp_n = pl.multiple_of(jnp.maximum(start - TILE, 0), TILE)
    clamp_s = pl.multiple_of(jnp.minimum(start + rows, height - TILE), TILE)
    tab_n, tab_s = tabs[:, pl.ds(clamp_n, TILE)], tabs[:, pl.ds(clamp_s, TILE)]
    ext_n, ext_s = ext[:, pl.ds(clamp_n, TILE)], ext[:, pl.ds(clamp_s, TILE)]
    row_mods = []
    for which in range(2):
        at = 3 * which
        if which == 0:
            lane = 0
            own_tab, next_tab, next_ext, next_lane = first, tab_n, ext_n, TILE - 1
            cross_row, inner_row, inv_row = UPPER, LOWER, I0
        else:
            lane = TILE - 1
            own_tab, next_tab, next_ext, next_lane = final, tab_s, ext_s, 0
            cross_row, inner_row, inv_row = LOWER, UPPER, I1

        def scalar(tab, row, place):
            return wide(tab[row : row + 1, place : place + 1], cols)

        cross = scalar(own_tab, cross_row, lane)
        inner = scalar(own_tab, inner_row, lane)
        ew_own = scalar(own_tab, EAST_WEST, lane)
        ew_next = scalar(next_tab, EAST_WEST, next_lane)
        z_next = row_ext[at : at + 1, :]
        u_next = row_ext[at + 1 : at + 2, :]
        i_next = row_ext[at + 2 : at + 3, :]
        corner = jnp.where(col_lane == 0, scalar(next_ext, 0, next_lane), 0.0)
        corner = jnp.where(col_lane == cols - 1, scalar(next_ext, 2, next_lane), corner)
        u_next = u_next - i_next * ew_next * corner
        e = -cross * z_next
        d = edges[inv_row : inv_row + 1, :cols] * e
        right = jnp.where(col_lane == cols - 1, 0.0, after(d))
        left = jnp.where(col_lane == 0, 0.0, before(d))
        dv = e - ew_own * (right + left) - cross * u_next
        row_mods.append((-far_c * d, far_c * dv - near_c * e, -far_c * inner * d))

    lane = lane_ids(SUB)
    blocks = chunk // SUB

    def copies(i):
        part = pl.ds(pl.multiple_of(i * chunk, SUB), chunk)
        return (
            pltpu.make_async_copy(field_x.at[part, :], out_x.at[part, :], sems.at[0]),
            pltpu.make_async_copy(field_r.at[part, :], out_r.at[part, :], sems.at[1]),
        )

    def step(k, carry):
        at = pl.multiple_of(k * SUB, SUB)
        here = pl.ds(at, SUB)
        lines = cols_t[here, :]
        for c in range(tiles):
            part = pl.ds(c * TILE, TILE)
            x = near * z[pl.ds(at + SUB, SUB), part] - far * u[pl.ds(at + SUB, SUB), part]
            r = src[here, part] - near * w[here, part] + far * v[here, part]
            if c == 0:
                x = x + jnp.where(lane == 0, wide(lines[:, 0:1]), 0.0)
                r = r + jnp.where(
                    lane == 0, wide(lines[:, 1:2]), jnp.where(lane == 1, wide(lines[:, 2:3]), 0.0)
                )
            if c == tiles - 1:
                x = x + jnp.where(lane == TILE - 1, wide(lines[:, 3:4]), 0.0)
                r = r + jnp.where(
                    lane == TILE - 1,
                    wide(lines[:, 4:5]),
                    jnp.where(lane == TILE - 2, wide(lines[:, 5:6]), 0.0),
                )
            field_x[here, part] = x
            field_r[here, part] = r
        return carry

    parts = rows // chunk
    for i in range(parts):
        lax.fori_loop(i * blocks, (i + 1) * blocks, step, 0)
        if i == 0:
            dx, dr, dr_next = row_mods[0]
            field_x[0:1, :] += dx
            field_r[0:1, :] += dr
            field_r[1:2, :] += dr_next
        if i == parts - 1:
            dx, dr, dr_next = row_mods[1]
            field_x[rows - 1 : rows, :] += dx
            field_r[rows - 1 : rows, :] += dr
            field_r[rows - 2 : rows - 1, :] += dr_next
        for copy in copies(i):
            copy.start()
    for i in range(parts):
        for copy in copies(i):
            copy.wait()


def shape(*dims):
    return jax.ShapeDtypeStruct(dims, jnp.float32)


def call(kernel, name, out_shape, n_in, smem=0, out_specs=None, scratch=(), limit=32):
    return pl.pallas_call(
        kernel,
        name=name,
        out_shape=out_shape,
        in_specs=[SMEM_SPEC] * smem + [VMEM_SPEC] * (n_in - smem),
        out_specs=out_specs or [VMEM_SPEC] * len(out_shape),
        scratch_shapes=list(scratch),
        compiler_params=pltpu.CompilerParams(vmem_limit_bytes=limit << 20),
    )


def per_device(source, flags):
    rows, cols = source.shape
    bands, sectors = lax.axis_size("lat"), lax.axis_size("lon")
    height = rows * bands
    tabs = coefficient_table(height)
    z, u, w, v, edges = call(
        local_kernel,
        "local",
        [
            shape(rows + 2 * SUB, cols),
            shape(rows + 2 * SUB, cols),
            shape(rows, cols),
            shape(rows, cols),
            shape(SUB, cols + rows + TILE),
        ],
        3,
        smem=1,
        scratch=[pltpu.VMEM((3, rows, TILE), jnp.float32)]
        + [pltpu.VMEM((rows, TILE), jnp.float32)] * 3,
    )(flags, tabs, source)

    def swap(pack, axis, stage):
        count = lax.axis_size(axis)
        return lax.ppermute(pack, axis, [(i, i ^ (1 << stage)) for i in range(count)])

    lat_stages = bands.bit_length() - 1
    lon_stages = sectors.bit_length() - 1
    pack, row_ext = edges, edges
    for stage in range(lat_stages):
        final = stage == lat_stages - 1
        tall = (rows << (stage + 1)) + TILE + (0 if final else cols)
        pack, row_ext = call(
            functools.partial(lat_kernel, stage, final, cols),
            f"lat_merge{stage}",
            [shape(SUB, tall), shape(SUB, cols)],
            4,
        )(tabs, pack, swap(pack, "lat", stage), row_ext)
    col_ext = pack
    for stage in range(lon_stages - 1):
        pack, col_ext = call(
            functools.partial(lon_kernel, stage),
            f"lon_merge{stage}",
            [shape(SUB, height + TILE), shape(SUB, height)],
            4,
        )(tabs, pack, swap(pack, "lon", stage), col_ext)
    stage = lon_stages - 1
    any_spec = pl.BlockSpec(memory_space=pl.ANY)
    x, r = call(
        functools.partial(last_kernel, stage, 32),
        "combine",
        [shape(rows, cols), shape(rows, cols)],
        11,
        out_specs=[any_spec, any_spec],
        scratch=[
            pltpu.VMEM((SUB, TILE), jnp.float32),
            pltpu.VMEM((SUB, height), jnp.float32),
            pltpu.VMEM((rows, cols), jnp.float32),
            pltpu.VMEM((rows, cols), jnp.float32),
            pltpu.VMEM((rows, SUB), jnp.float32),
            pltpu.SemaphoreType.DMA((2,)),
        ],
    )(tabs, pack, swap(pack, "lon", stage), col_ext, edges, row_ext, source, z, u, w, v)
    return x, r


def solution(mesh):
    in_specs = (P("lat", "lon"), P("lat", "lon"))
    out_specs = (P("lat", "lon"), P("lat", "lon"))
    return jax.shard_map(
        per_device, mesh=mesh, in_specs=in_specs, out_specs=out_specs, check_vma=False
    )
```

```python
import functools
import math

import jax
import jax.numpy as jnp
from jax import lax
from jax.experimental import pallas as pl
from jax.experimental.pallas import tpu as pltpu
from jax.sharding import PartitionSpec as P

ARC_SPAN = 2.0 * math.pi / 3.0
TILE = 128
SUB = 8
VMEM_SPEC = pl.BlockSpec(memory_space=pltpu.VMEM)
HBM_SPEC = pl.BlockSpec(memory_space=pltpu.HBM)
LOADS = 4
Z0, U0, V0, Z1, U1, V1, I0, I1 = range(8)
EAST_WEST, UPPER, LOWER, INNER = range(4)


def coefficient_table(total_rows):
    row_pos = lax.broadcasted_iota(jnp.int32, (SUB, total_rows), 1).astype(jnp.float32)
    kind = lax.broadcasted_iota(jnp.int32, (SUB, total_rows), 0)
    ahead = jnp.where(kind == EAST_WEST, 0.5, jnp.where(kind == UPPER, 0.0, 1.0))
    table = jnp.cos((row_pos + ahead) / total_rows * ARC_SPAN - 0.5 * ARC_SPAN)
    return jnp.where((kind == INNER) & (row_pos == total_rows - 1), 0.0, table)


def fold(row):
    total = row[:, :TILE]
    for start in range(TILE, row.shape[1], TILE):
        total = total + row[:, start : start + TILE]
    return total


def wide(cell, width=TILE):
    return jnp.broadcast_to(cell, (cell.shape[0], width))


def after(row):
    return pltpu.roll(row, row.shape[1] - 1, 1)


def before(row):
    return pltpu.roll(row, 1, 1)


def lane_ids(rows, width=TILE):
    return lax.broadcasted_iota(jnp.int32, (rows, width), 1)


def local_kernel(
    flags_in, source, z, u, w, v, pack, tabs, src, inv, ew_t, up_t, lo_t, flags, sems
):
    rows, cols = src.shape
    tiles = cols // TILE
    blocks = TILE // SUB
    parts = sems.shape[0] - 1
    chunk = rows // parts
    flag_copy = pltpu.make_async_copy(flags_in, flags, sems.at[parts])
    flag_copy.start()
    loads = []
    for i in range(parts):
        part = pl.ds(i * chunk, chunk)
        loads.append(pltpu.make_async_copy(source.at[part, :], src.at[part, :], sems.at[i]))
        loads[-1].start()
    tabs[...] = coefficient_table(tabs.shape[1])
    start = pl.multiple_of(lax.axis_index("lat") * rows, rows)
    band = jnp.transpose(tabs[:, pl.ds(start, rows)])
    ew = wide(band[:, EAST_WEST : EAST_WEST + 1])
    up = wide(band[:, UPPER : UPPER + 1])
    lo = wide(band[:, LOWER : LOWER + 1])
    ew_t[...] = ew
    up_t[...] = up
    lo_t[...] = lo
    for kind, screen in enumerate((0.05, 0.4, 2.0)):
        inv[kind] = 1.0 / (screen + 2.0 * ew + up + lo)
    nothing = jnp.zeros((SUB, cols), jnp.float32)
    for padded in (z, u):
        padded[:SUB] = nothing
        padded[rows + SUB :] = nothing
    zero = jnp.zeros((SUB, TILE), jnp.float32)
    row_id = lax.broadcasted_iota(jnp.int32, (SUB, TILE), 0)
    lane = lane_ids(SUB)
    flag_copy.wait()
    kinds = [
        [
            jnp.where(flags[band_row, c] == 0, 0, jnp.where(flags[band_row, c] == 1, 1, 2))
            for c in range(tiles)
        ]
        for band_row in range(rows // TILE)
    ]

    def columns(c):
        return pl.ds(c * TILE, TILE)

    def around(field, at, c, here, west, east, coeffs):
        prev = field[pl.ds(at, SUB), columns(c)]
        later = field[pl.ds(at + 2 * SUB, SUB), columns(c)]
        above = pltpu.roll(jnp.where(row_id == SUB - 1, prev, here), 1, 0)
        below = pltpu.roll(jnp.where(row_id == 0, later, here), SUB - 1, 0)
        right = pltpu.roll(jnp.where(lane == 0, east, here), TILE - 1, 1)
        left = pltpu.roll(jnp.where(lane == TILE - 1, west, here), 1, 1)
        e, a, b = coeffs
        return e * (right + left) + a * above + b * below

    def first_pass(at, kind, sums):
        part = zero
        for c in range(tiles):
            b = src[pl.ds(at, SUB), columns(c)]
            value = b * inv[kind[c], pl.ds(at, SUB), :]
            z[pl.ds(at + SUB, SUB), columns(c)] = value
            part = part + b * value
        return (sums[0] + part,) + sums[1:]

    def second_pass(at, kind, sums):
        part1, part2 = zero, zero
        here_rows = pl.ds(at, SUB)
        coeffs = ew_t[here_rows, :], up_t[here_rows, :], lo_t[here_rows, :]
        line = [zero] + [z[pl.ds(at + SUB, SUB), columns(c)] for c in range(tiles)] + [zero]
        for c in range(tiles):
            here = line[c + 1]
            near = around(z, at, c, here, line[c], line[c + 2], coeffs)
            image = src[here_rows, columns(c)] - near
            scaled = image * inv[kind[c], here_rows, :]
            w[here_rows, columns(c)] = image
            u[pl.ds(at + SUB, SUB), columns(c)] = scaled
            part1 = part1 + here * image
            part2 = part2 + scaled * image
        return sums[0], sums[1] + part1, sums[2] + part2, sums[3]

    def third_pass(at, kind, sums):
        part = zero
        here_rows = pl.ds(at, SUB)
        coeffs = ew_t[here_rows, :], up_t[here_rows, :], lo_t[here_rows, :]
        line = [zero] + [u[pl.ds(at + SUB, SUB), columns(c)] for c in range(tiles)] + [zero]
        for c in range(tiles):
            here = line[c + 1]
            near = around(u, at, c, here, line[c], line[c + 2], coeffs)
            image = w[here_rows, columns(c)] - near
            v[here_rows, columns(c)] = image
            part = part + here * image
        return sums[:3] + (sums[3] + part,)

    count = rows // SUB
    done = [0, 0, 0]
    sums = (zero,) * 4
    for i in range(parts):
        loads[i].wait()
        ready = (i + 1) * (chunk // SUB)
        for which, body in enumerate((first_pass, second_pass, third_pass)):
            upto = ready - which if i + 1 < parts else count
            while done[which] < upto:
                band_row = done[which] // blocks
                stop = min(upto, (band_row + 1) * blocks)

                def step(k, carry, body=body, band_row=band_row):
                    return body(pl.multiple_of(k * SUB, SUB), kinds[band_row], carry)

                sums = lax.fori_loop(done[which], stop, step, sums, unroll=stop - done[which])
                done[which] = stop
    m0, m1, m2, m3 = sums

    last = rows - 1
    pack[Z0 : Z0 + 1, :cols] = z[SUB : SUB + 1, :]
    pack[U0 : U0 + 1, :cols] = u[SUB : SUB + 1, :]
    pack[V0 : V0 + 1, :cols] = v[:1, :]
    pack[Z1 : Z1 + 1, :cols] = z[last + SUB : last + SUB + 1, :]
    pack[U1 : U1 + 1, :cols] = u[last + SUB : last + SUB + 1, :]
    pack[V1 : V1 + 1, :cols] = v[last:, :]
    for c in range(tiles):
        pack[I0 : I0 + 1, c * TILE : (c + 1) * TILE] = inv[kinds[0][c], :1, :]
        pack[I1 : I1 + 1, c * TILE : (c + 1) * TILE] = inv[kinds[-1][c], last:, :]

    for band_row in range(rows // TILE):
        here_rows = slice(band_row * TILE, (band_row + 1) * TILE)
        inner_rows = slice(band_row * TILE + SUB, (band_row + 1) * TILE + SUB)
        east = slice(cols - TILE, cols)
        ids = lane_ids(TILE)
        mix = inv[kinds[band_row][-1], here_rows, :]
        mix = jnp.where(ids == I0, inv[kinds[band_row][0], here_rows, :], mix)
        mix = jnp.where(ids == V1, pltpu.roll(v[here_rows, east], V1 + 1, 1), mix)
        mix = jnp.where(ids == U1, pltpu.roll(u[inner_rows, east], U1 + 1, 1), mix)
        mix = jnp.where(ids == Z1, pltpu.roll(z[inner_rows, east], Z1 + 1, 1), mix)
        mix = jnp.where(ids == V0, pltpu.roll(v[here_rows, :TILE], V0, 1), mix)
        mix = jnp.where(ids == U0, pltpu.roll(u[inner_rows, :TILE], U0, 1), mix)
        mix = jnp.where(ids == Z0, z[inner_rows, :TILE], mix)
        at = cols + band_row * TILE
        pack[:, at : at + TILE] = jnp.transpose(mix)[:SUB, :]

    at = cols + rows
    pack[:, at:] = zero
    for i, m in enumerate((m0, m1, m2, m3)):
        pack[i : i + 1, at:] = jnp.sum(m, axis=0, keepdims=True)


def sides(own, other, index, stage):
    size = 2**stage
    lower = lax.rem(lax.div(index, size), 2)
    inside = lax.rem(index, size)
    here, there = own[...], other[...]
    first = jnp.where(lower == 0, here, there)
    second = jnp.where(lower == 0, there, here)
    at_end = (lower == 0) & (inside == size - 1)
    at_start = (lower == 1) & (inside == 0)
    return first, second, at_end, at_start


def row_of(pack, i, start, stop):
    return pack[i : i + 1, start:stop]


def add_moments(out, at, first, second, changes):
    width = first.shape[1]
    out[:, at : at + TILE] = first[:, width - TILE :] + second[:, width - TILE :]
    for i, change in enumerate(changes):
        out[i + 1 : i + 2, at : at + TILE] += change


def lat_kernel(stage, stages, cols, tabs, own, other, ext_in, out, ext):
    facing = 0 < stage == stages - 1
    final = stage == stages - 1
    half = cols // 2
    span = half if facing else cols
    height = own.shape[1] - span - TILE
    index = lax.axis_index("lat")
    top, bottom, at_end, at_start = sides(own, other, index, stage)
    size = 2**stage
    border = pl.multiple_of((lax.div(index, 2 * size) * 2 * size + size) * (height // size), TILE)
    low = tabs[:, pl.ds(border, TILE)]
    high = tabs[:, pl.ds(border - TILE, TILE)]
    cross = wide(low[UPPER : UPPER + 1, :1], cols)
    ew_b = wide(low[EAST_WEST : EAST_WEST + 1, :1])
    ew_t = wide(high[EAST_WEST : EAST_WEST + 1, TILE - 1 :])
    next_b = wide(low[LOWER : LOWER + 1, :1])
    next_t = wide(high[UPPER : UPPER + 1, TILE - 1 :])

    if facing:

        def joined(pack, i):
            return jnp.concatenate(
                [row_of(pack, i, 0, half), row_of(pack, i + 4, 0, half)], axis=1
            )

        zt, ut, vt, it = (joined(top, i) for i in range(4))
        zb, ub, vb, ib = (joined(bottom, i) for i in range(4))
    else:
        zt, ut, vt, it = (row_of(top, i, 0, cols) for i in (Z1, U1, V1, I1))
        zb, ub, vb, ib = (row_of(bottom, i, 0, cols) for i in (Z0, U0, V0, I0))
    et, eb = -cross * zb, -cross * zt
    dt, db = it * et, ib * eb
    full_t, full_b = ut + dt, ub + db
    inside = lane_ids(1, cols) < cols - 1
    pair_t = jnp.where(inside, dt * after(dt), 0.0)
    pair_b = jnp.where(inside, db * after(db), 0.0)
    twice = fold(zt * et)
    second = fold((2.0 * ut + dt) * et + (2.0 * ub + db) * eb)
    third = fold(dt * (2.0 * vt + et) + db * (2.0 * vb + eb) - 2.0 * cross * full_t * full_b)
    third = third - 2.0 * (ew_t * fold(pair_t) + ew_b * fold(pair_b))

    if final:
        base = 0
    elif stage + 1 == stages - 1:
        base = half
        up_next = lax.rem(lax.div(index, 2 * size), 2) == 0
        for i, (first_row, last_row) in enumerate(((Z0, Z1), (U0, U1), (V0, V1), (I0, I1))):
            row = jnp.where(
                up_next, row_of(bottom, last_row, 0, cols), row_of(top, first_row, 0, cols)
            )
            out[i : i + 1, :half] = row[:, :half]
            out[i + 4 : i + 5, :half] = row[:, half:]
    else:
        base = cols
        ids = lax.broadcasted_iota(jnp.int32, (SUB, cols), 0)
        out[:, :cols] = jnp.where((ids < Z1) | (ids == I0), top[:, :cols], bottom[:, :cols])
    out[:, base : base + height] = top[:, span : span + height]
    out[:, base + height : base + 2 * height] = bottom[:, span : span + height]
    add_moments(out, base + 2 * height, top, bottom, (2.0 * twice, second, third))

    lane = lane_ids(1)
    upper_at = base + height - TILE
    lower_at = base + height
    c = cross[:, :TILE]
    for edge, inner, u_row, v_row in ((0, 1, U0, V0), (cols - 1, cols - 2, U1, V1)):

        def pick(row, place):
            return wide(row[:, place : place + 1])

        d_top, d_bottom = pick(dt, edge), pick(db, edge)
        v_top = pick(et, edge) - ew_t * pick(dt, inner) - c * pick(full_b, edge)
        v_bottom = pick(eb, edge) - ew_b * pick(db, inner) - c * pick(full_t, edge)
        out[u_row : u_row + 1, upper_at : upper_at + TILE] += jnp.where(
            lane == TILE - 1, d_top, 0.0
        )
        out[u_row : u_row + 1, lower_at : lower_at + TILE] += jnp.where(lane == 0, d_bottom, 0.0)
        out[v_row : v_row + 1, upper_at : upper_at + TILE] += jnp.where(
            lane == TILE - 1, v_top, jnp.where(lane == TILE - 2, -next_t * d_top, 0.0)
        )
        out[v_row : v_row + 1, lower_at : lower_at + TILE] += jnp.where(
            lane == 0, v_bottom, jnp.where(lane == 1, -next_b * d_bottom, 0.0)
        )

    if stage == 0:
        ext[...] = jnp.zeros((SUB, cols), jnp.float32)
    else:
        ext[...] = ext_in[...]

    @pl.when(at_start)
    def _():
        ext[0:1, :] = zt
        ext[1:2, :] = full_t
        ext[2:3, :] = it

    @pl.when(at_end)
    def _():
        ext[3:4, :] = zb
        ext[4:5, :] = full_b
        ext[5:6, :] = ib


def column_border(west, east, tabs):
    height = west.shape[1] - TILE
    zw, uw, vw, iw = (row_of(west, i, 0, height) for i in (Z1, U1, V1, I1))
    ze, ue, ve, ie = (row_of(east, i, 0, height) for i in (Z0, U0, V0, I0))
    ew = tabs[EAST_WEST : EAST_WEST + 1, :]
    inner = tabs[INNER : INNER + 1, :]
    to_w, to_e = -ew * ze, -ew * zw
    dw, de = iw * to_w, ie * to_e
    full_w, full_e = uw + dw, ue + de
    first = 2.0 * fold(zw * to_w)
    second = fold((2.0 * uw + dw) * to_w + (2.0 * ue + de) * to_e)
    third = fold(
        dw * (2.0 * vw + to_w)
        + de * (2.0 * ve + to_e)
        - 2.0 * inner * (dw * after(dw) + de * after(de))
        - 2.0 * ew * full_w * full_e
    )
    return (first, second, third), (zw, full_w), (ze, full_e)


def lon_kernel(stage, tabs, own, other, ext_in, out, ext):
    height = own.shape[1] - TILE
    west, east, at_end, at_start = sides(own, other, lax.axis_index("lon"), stage)
    changes, from_west, from_east = column_border(west, east, tabs)
    ids = lax.broadcasted_iota(jnp.int32, (SUB, height), 0)
    out[:, :height] = jnp.where((ids < Z1) | (ids == I0), west[:, :height], east[:, :height])
    add_moments(out, height, west, east, changes)
    if stage == 0:
        ext[...] = jnp.zeros((SUB, height), jnp.float32)
    else:
        ext[...] = ext_in[...]

    @pl.when(at_start)
    def _():
        ext[0:1, :], ext[1:2, :] = from_west

    @pl.when(at_end)
    def _():
        ext[2:3, :], ext[3:4, :] = from_east


def last_kernel(
    stage, chunk, tabs, own, other, ext_in, edges, row_ext, src, z, u, w, v,
    out_x, out_r, mom, ext, field_x, field_r, cols_t, sems,
):
    rows, cols = src.shape
    height = own.shape[1] - TILE
    tiles = cols // TILE
    sectors = lax.axis_size("lon")
    index = lax.axis_index("lon")
    west, east, at_end, at_start = sides(own, other, index, stage)
    changes, from_west, from_east = column_border(west, east, tabs)
    wrap, round_west, round_east = column_border(east, west, tabs)
    add_moments(mom, 0, west, east, [a + b for a, b in zip(changes, wrap)])
    if stage == 0:
        ext[...] = jnp.zeros((SUB, height), jnp.float32)
    else:
        ext[...] = ext_in[...]

    @pl.when(at_start)
    def _():
        ext[0:1, :], ext[1:2, :] = from_west

    @pl.when(at_end)
    def _():
        ext[2:3, :], ext[3:4, :] = from_east

    @pl.when(index == 0)
    def _():
        ext[0:1, :], ext[1:2, :] = round_west

    @pl.when(index == sectors - 1)
    def _():
        ext[2:3, :], ext[3:4, :] = round_east

    sums = jnp.broadcast_to(jnp.sum(mom[...], axis=1, keepdims=True), (SUB, TILE))
    m0, m1, m2, m3 = (sums[i : i + 1, :] for i in range(4))
    alpha = m0 / m1
    fresh = alpha * alpha * m2 - 2.0 * alpha * m1 + m0
    grow = 1.0 + fresh / m0
    bend = grow * grow * m1 - 2.0 * grow * alpha * m2 + alpha * alpha * m3
    beta = fresh / bend
    near1, far1 = alpha + beta * grow, alpha * beta
    near = jnp.broadcast_to(near1, (SUB, TILE))
    far = jnp.broadcast_to(far1, (SUB, TILE))

    lat = lax.axis_index("lat")
    start = pl.multiple_of(lat * rows, rows)
    here = pl.ds(start, rows)
    ew = tabs[EAST_WEST : EAST_WEST + 1, here]
    up = tabs[UPPER : UPPER + 1, here]
    lo = tabs[LOWER : LOWER + 1, here]
    row_lane = lane_ids(1, rows)
    near_r = jnp.concatenate([near1] * (rows // TILE), axis=1)
    far_r = jnp.concatenate([far1] * (rows // TILE), axis=1)
    mods = []
    for z_row, inv_row in ((0, I0), (2, I1)):
        e = -ew * ext[z_row : z_row + 1, here]
        d = edges[inv_row : inv_row + 1, cols : cols + rows] * e
        above = jnp.where(row_lane == 0, 0.0, before(d))
        below = jnp.where(row_lane == rows - 1, 0.0, after(d))
        dv = e - up * above - lo * below - ew * ext[z_row + 1 : z_row + 2, here]
        mods += [-far_r * d, far_r * dv - near_r * e, -far_r * ew * d]
    mods += [jnp.zeros((1, rows), jnp.float32)] * 2
    cols_t[...] = jnp.transpose(jnp.concatenate(mods, axis=0))

    near_c = jnp.concatenate([near1] * tiles, axis=1)
    far_c = jnp.concatenate([far1] * tiles, axis=1)
    col_lane = lane_ids(1, cols)
    first = tabs[:, pl.ds(start, TILE)]
    final = tabs[:, pl.ds(start + rows - TILE, TILE)]
    clamp_n = pl.multiple_of(jnp.maximum(start - TILE, 0), TILE)
    clamp_s = pl.multiple_of(jnp.minimum(start + rows, height - TILE), TILE)
    tab_n, tab_s = tabs[:, pl.ds(clamp_n, TILE)], tabs[:, pl.ds(clamp_s, TILE)]
    ext_n, ext_s = ext[:, pl.ds(clamp_n, TILE)], ext[:, pl.ds(clamp_s, TILE)]
    row_mods = []
    for which in range(2):
        at = 3 * which
        if which == 0:
            lane = 0
            own_tab, next_tab, next_ext, next_lane = first, tab_n, ext_n, TILE - 1
            cross_row, inner_row, inv_row = UPPER, LOWER, I0
        else:
            lane = TILE - 1
            own_tab, next_tab, next_ext, next_lane = final, tab_s, ext_s, 0
            cross_row, inner_row, inv_row = LOWER, UPPER, I1

        def scalar(tab, row, place):
            return wide(tab[row : row + 1, place : place + 1], cols)

        cross = scalar(own_tab, cross_row, lane)
        inner = scalar(own_tab, inner_row, lane)
        ew_own = scalar(own_tab, EAST_WEST, lane)
        ew_next = scalar(next_tab, EAST_WEST, next_lane)
        z_next = row_ext[at : at + 1, :]
        u_next = row_ext[at + 1 : at + 2, :]
        i_next = row_ext[at + 2 : at + 3, :]
        corner = jnp.where(col_lane == 0, scalar(next_ext, 0, next_lane), 0.0)
        corner = jnp.where(col_lane == cols - 1, scalar(next_ext, 2, next_lane), corner)
        u_next = u_next - i_next * ew_next * corner
        e = -cross * z_next
        d = edges[inv_row : inv_row + 1, :cols] * e
        right = jnp.where(col_lane == cols - 1, 0.0, after(d))
        left = jnp.where(col_lane == 0, 0.0, before(d))
        dv = e - ew_own * (right + left) - cross * u_next
        row_mods.append((-far_c * d, far_c * dv - near_c * e, -far_c * inner * d))

    lane = lane_ids(SUB)
    blocks = chunk // SUB

    def copies(i):
        part = pl.ds(pl.multiple_of(i * chunk, SUB), chunk)
        return (
            pltpu.make_async_copy(field_x.at[part, :], out_x.at[part, :], sems.at[0]),
            pltpu.make_async_copy(field_r.at[part, :], out_r.at[part, :], sems.at[1]),
        )

    def step(k, carry):
        at = pl.multiple_of(k * SUB, SUB)
        here = pl.ds(at, SUB)
        lines = cols_t[here, :]
        for c in range(tiles):
            part = pl.ds(c * TILE, TILE)
            x = near * z[pl.ds(at + SUB, SUB), part] - far * u[pl.ds(at + SUB, SUB), part]
            r = src[here, part] - near * w[here, part] + far * v[here, part]
            if c == 0:
                x = x + jnp.where(lane == 0, wide(lines[:, 0:1]), 0.0)
                r = r + jnp.where(
                    lane == 0, wide(lines[:, 1:2]), jnp.where(lane == 1, wide(lines[:, 2:3]), 0.0)
                )
            if c == tiles - 1:
                x = x + jnp.where(lane == TILE - 1, wide(lines[:, 3:4]), 0.0)
                r = r + jnp.where(
                    lane == TILE - 1,
                    wide(lines[:, 4:5]),
                    jnp.where(lane == TILE - 2, wide(lines[:, 5:6]), 0.0),
                )
            field_x[here, part] = x
            field_r[here, part] = r
        return carry

    parts = rows // chunk
    for i in list(range(1, parts)) + [0]:
        lax.fori_loop(i * blocks, (i + 1) * blocks, step, 0, unroll=blocks)
        if i == 0:
            dx, dr, dr_next = row_mods[0]
            field_x[0:1, :] += dx
            field_r[0:1, :] += dr
            field_r[1:2, :] += dr_next
        if i == parts - 1:
            dx, dr, dr_next = row_mods[1]
            field_x[rows - 1 : rows, :] += dx
            field_r[rows - 1 : rows, :] += dr
            field_r[rows - 2 : rows - 1, :] += dr_next
        for copy in copies(i):
            copy.start()
    for i in range(parts):
        for copy in copies(i):
            copy.wait()


def shape(*dims):
    return jax.ShapeDtypeStruct(dims, jnp.float32)


def call(kernel, name, out_shape, in_specs, out_specs=None, scratch=(), limit=32):
    return pl.pallas_call(
        kernel,
        name=name,
        out_shape=out_shape,
        in_specs=in_specs,
        out_specs=out_specs or [VMEM_SPEC] * len(out_shape),
        scratch_shapes=list(scratch),
        compiler_params=pltpu.CompilerParams(vmem_limit_bytes=limit << 20),
    )


def per_device(source, flags):
    rows, cols = source.shape
    bands, sectors = lax.axis_size("lat"), lax.axis_size("lon")
    height = rows * bands
    z, u, w, v, edges, tabs, src = call(
        local_kernel,
        "local",
        [
            shape(rows + 2 * SUB, cols),
            shape(rows + 2 * SUB, cols),
            shape(rows, cols),
            shape(rows, cols),
            shape(SUB, cols + rows + TILE),
            shape(SUB, height),
            shape(rows, cols),
        ],
        [HBM_SPEC, HBM_SPEC],
        scratch=[pltpu.VMEM((3, rows, TILE), jnp.float32)]
        + [pltpu.VMEM((rows, TILE), jnp.float32)] * 3
        + [pltpu.SMEM(flags.shape, jnp.int32), pltpu.SemaphoreType.DMA((LOADS + 1,))],
    )(*(pltpu.with_memory_space_constraint(a, pltpu.HBM) for a in (flags, source)))

    def swap(pack, axis, stage):
        count = lax.axis_size(axis)
        return lax.ppermute(pack, axis, [(i, i ^ (1 << stage)) for i in range(count)])

    lat_stages = bands.bit_length() - 1
    lon_stages = sectors.bit_length() - 1
    pack, row_ext = edges, edges
    for stage in range(lat_stages):
        left = lat_stages - 1 - stage
        tall = (rows << (stage + 1)) + TILE + (cols, cols // 2, 0)[max(0, 2 - left)]
        pack, row_ext = call(
            functools.partial(lat_kernel, stage, lat_stages, cols),
            f"lat_merge{stage}",
            [shape(SUB, tall), shape(SUB, cols)],
            [VMEM_SPEC] * 4,
        )(tabs, pack, swap(pack, "lat", stage), row_ext)
    col_ext = pack
    for stage in range(lon_stages - 1):
        pack, col_ext = call(
            functools.partial(lon_kernel, stage),
            f"lon_merge{stage}",
            [shape(SUB, height + TILE), shape(SUB, height)],
            [VMEM_SPEC] * 4,
        )(tabs, pack, swap(pack, "lon", stage), col_ext)
    stage = lon_stages - 1
    x, r = call(
        functools.partial(last_kernel, stage, 32),
        "combine",
        [shape(rows, cols), shape(rows, cols)],
        [VMEM_SPEC] * 11,
        out_specs=[HBM_SPEC, HBM_SPEC],
        scratch=[
            pltpu.VMEM((SUB, TILE), jnp.float32),
            pltpu.VMEM((SUB, height), jnp.float32),
            pltpu.VMEM((rows, cols), jnp.float32),
            pltpu.VMEM((rows, cols), jnp.float32),
            pltpu.VMEM((rows, SUB), jnp.float32),
            pltpu.SemaphoreType.DMA((2,)),
        ],
    )(tabs, pack, swap(pack, "lon", stage), col_ext, edges, row_ext, src, z, u, w, v)
    return x, r


def solution(mesh):
    in_specs = (P("lat", "lon"), P("lat", "lon"))
    out_specs = (P("lat", "lon"), P("lat", "lon"))
    return jax.shard_map(
        per_device, mesh=mesh, in_specs=in_specs, out_specs=out_specs, check_vma=False
    )
```

```python
import functools
import math

import jax
import jax.numpy as jnp
from jax import lax
from jax.experimental import pallas as pl
from jax.experimental.pallas import tpu as pltpu
from jax.sharding import PartitionSpec as P

ARC_SPAN = 2.0 * math.pi / 3.0
TILE = 128
SUB = 8
VMEM_SPEC = pl.BlockSpec(memory_space=pltpu.VMEM)
HBM_SPEC = pl.BlockSpec(memory_space=pltpu.HBM)
ANY_SPEC = pl.BlockSpec(memory_space=pl.ANY)
LOADS = 4
Z0, U0, V0, Z1, U1, V1, I0, I1 = range(8)
EAST_WEST, UPPER, LOWER, INNER = range(4)


def coefficient_table(total_rows):
    row_pos = lax.broadcasted_iota(jnp.int32, (SUB, total_rows), 1).astype(jnp.float32)
    kind = lax.broadcasted_iota(jnp.int32, (SUB, total_rows), 0)
    ahead = jnp.where(kind == EAST_WEST, 0.5, jnp.where(kind == UPPER, 0.0, 1.0))
    table = jnp.cos((row_pos + ahead) / total_rows * ARC_SPAN - 0.5 * ARC_SPAN)
    return jnp.where((kind == INNER) & (row_pos == total_rows - 1), 0.0, table)


def fold(row):
    total = row[:, :TILE]
    for start in range(TILE, row.shape[1], TILE):
        total = total + row[:, start : start + TILE]
    return total


def wide(cell, width=TILE):
    return jnp.broadcast_to(cell, (cell.shape[0], width))


def after(row):
    return pltpu.roll(row, row.shape[1] - 1, 1)


def before(row):
    return pltpu.roll(row, 1, 1)


def lane_ids(rows, width=TILE):
    return lax.broadcasted_iota(jnp.int32, (rows, width), 1)


def columns(c):
    return pl.ds(c * TILE, TILE)


def line_of(field, at, tiles):
    zero = jnp.zeros((SUB, TILE), jnp.float32)
    return [zero] + [field[pl.ds(at + SUB, SUB), columns(c)] for c in range(tiles)] + [zero]


def ahead_of(field, at, c, line, coeffs):
    row_id = lax.broadcasted_iota(jnp.int32, (SUB, TILE), 0)
    here = line[c + 1]
    later = field[pl.ds(at + 2 * SUB, SUB), columns(c)]
    below = pltpu.roll(jnp.where(row_id == 0, later, here), SUB - 1, 0)
    right = pltpu.roll(jnp.where(lane_ids(SUB) == 0, line[c + 2], here), TILE - 1, 1)
    return right, coeffs[2] * below


def behind_of(field, at, c, line, coeffs):
    row_id = lax.broadcasted_iota(jnp.int32, (SUB, TILE), 0)
    here = line[c + 1]
    prev = field[pl.ds(at, SUB), columns(c)]
    above = pltpu.roll(jnp.where(row_id == SUB - 1, prev, here), 1, 0)
    left = pltpu.roll(jnp.where(lane_ids(SUB) == TILE - 1, line[c], here), 1, 1)
    return left, coeffs[1] * above


def around(field, at, c, line, coeffs):
    right, below = ahead_of(field, at, c, line, coeffs)
    left, above = behind_of(field, at, c, line, coeffs)
    return coeffs[0] * (right + left) + (above + below)


def local_kernel(
    flags_in, source, z, u, w, pack, tabs, src, coef, inv, v_edge, flags, sems
):
    rows, cols = src.shape
    tiles = cols // TILE
    blocks = TILE // SUB
    parts = sems.shape[0] - 1
    chunk = rows // parts
    flag_copy = pltpu.make_async_copy(flags_in, flags, sems.at[parts])
    flag_copy.start()
    loads = []
    for i in range(parts):
        part = pl.ds(i * chunk, chunk)
        loads.append(pltpu.make_async_copy(source.at[part, :], src.at[part, :], sems.at[i]))
        if i < 2:
            loads[-1].start()
    tabs[...] = coefficient_table(tabs.shape[1])
    start = pl.multiple_of(lax.axis_index("lat") * rows, rows)
    band = jnp.transpose(tabs[:, pl.ds(start, rows)])
    ew = wide(band[:, EAST_WEST : EAST_WEST + 1])
    up = wide(band[:, UPPER : UPPER + 1])
    lo = wide(band[:, LOWER : LOWER + 1])
    for i, values in enumerate((ew, up, lo)):
        coef[i] = values
    for kind, screen in enumerate((0.05, 0.4, 2.0)):
        inv[kind] = 1.0 / (screen + 2.0 * ew + up + lo)
    nothing = jnp.zeros((SUB, cols), jnp.float32)
    for padded in (z, u):
        padded[:SUB] = nothing
        padded[rows + SUB :] = nothing
    zero = jnp.zeros((SUB, TILE), jnp.float32)
    flag_copy.wait()
    kinds = [
        [
            jnp.where(flags[band_row, c] == 0, 0, jnp.where(flags[band_row, c] == 1, 1, 2))
            for c in range(tiles)
        ]
        for band_row in range(rows // TILE)
    ]

    def first_pass(at, kind, sums):
        part = zero
        for c in range(tiles):
            b = src[pl.ds(at, SUB), columns(c)]
            value = b * inv[kind[c], pl.ds(at, SUB), :]
            z[pl.ds(at + SUB, SUB), columns(c)] = value
            part = part + b * value
        return (sums[0] + part,) + sums[1:]

    def second_pass(at, kind, sums):
        part1, part2 = zero, zero
        here_rows = pl.ds(at, SUB)
        coeffs = [coef[i, here_rows, :] for i in range(3)]
        line = line_of(z, at, tiles)
        for c in range(tiles):
            image = src[here_rows, columns(c)] - around(z, at, c, line, coeffs)
            scaled = image * inv[kind[c], here_rows, :]
            w[here_rows, columns(c)] = image
            u[pl.ds(at + SUB, SUB), columns(c)] = scaled
            part1 = part1 + line[c + 1] * image
            part2 = part2 + scaled * image
        return sums[0], sums[1] + part1, sums[2] + part2, sums[3]

    def third_pass(at, kind, sums):
        part = zero
        here_rows = pl.ds(at, SUB)
        coeffs = [coef[i, here_rows, :] for i in range(3)]
        line = line_of(u, at, tiles)
        for c in range(tiles):
            right, below = ahead_of(u, at, c, line, coeffs)
            near = coeffs[0] * right + below
            image = w[here_rows, columns(c)]
            part = part + line[c + 1] * (image - (near + near))
            if c in (0, tiles - 1):
                left, above = behind_of(u, at, c, line, coeffs)
                edge = pl.ds(0 if c == 0 else TILE, TILE)
                v_edge[here_rows, edge] = image - near - (coeffs[0] * left + above)
        return sums[:3] + (sums[3] + part,)

    count = rows // SUB
    done = [0, 0, 0]
    sums = (zero,) * 4
    for i in range(parts):
        loads[i].wait()
        if i + 2 < parts:
            loads[i + 2].start()
        ready = (i + 1) * (chunk // SUB)
        for which, body in enumerate((first_pass, second_pass, third_pass)):
            upto = ready - which if i + 1 < parts else count
            while done[which] < upto:
                band_row = done[which] // blocks
                stop = min(upto, (band_row + 1) * blocks)

                def step(k, carry, body=body, band_row=band_row):
                    return body(pl.multiple_of(k * SUB, SUB), kinds[band_row], carry)

                sums = lax.fori_loop(done[which], stop, step, sums, unroll=stop - done[which])
                done[which] = stop
    m0, m1, m2, m3 = sums

    last = rows - 1
    pack[Z0 : Z0 + 1, :cols] = z[SUB : SUB + 1, :]
    pack[U0 : U0 + 1, :cols] = u[SUB : SUB + 1, :]
    pack[Z1 : Z1 + 1, :cols] = z[last + SUB : last + SUB + 1, :]
    pack[U1 : U1 + 1, :cols] = u[last + SUB : last + SUB + 1, :]
    for at, v_row, place in ((0, V0, 0), (rows - SUB, V1, SUB - 1)):
        line = line_of(u, at, tiles)
        coeffs = [coef[i, at : at + SUB, :] for i in range(3)]
        for c in range(tiles):
            image = w[at : at + SUB, columns(c)] - around(u, at, c, line, coeffs)
            pack[v_row : v_row + 1, columns(c)] = image[place : place + 1, :]
    for c in range(tiles):
        pack[I0 : I0 + 1, c * TILE : (c + 1) * TILE] = inv[kinds[0][c], :1, :]
        pack[I1 : I1 + 1, c * TILE : (c + 1) * TILE] = inv[kinds[-1][c], last:, :]

    for band_row in range(rows // TILE):
        here_rows = slice(band_row * TILE, (band_row + 1) * TILE)
        inner_rows = slice(band_row * TILE + SUB, (band_row + 1) * TILE + SUB)
        east = slice(cols - TILE, cols)
        ids = lane_ids(TILE)
        mix = inv[kinds[band_row][-1], here_rows, :]
        mix = jnp.where(ids == I0, inv[kinds[band_row][0], here_rows, :], mix)
        mix = jnp.where(ids == V1, pltpu.roll(v_edge[here_rows, TILE:], V1 + 1, 1), mix)
        mix = jnp.where(ids == U1, pltpu.roll(u[inner_rows, east], U1 + 1, 1), mix)
        mix = jnp.where(ids == Z1, pltpu.roll(z[inner_rows, east], Z1 + 1, 1), mix)
        mix = jnp.where(ids == V0, pltpu.roll(v_edge[here_rows, :TILE], V0, 1), mix)
        mix = jnp.where(ids == U0, pltpu.roll(u[inner_rows, :TILE], U0, 1), mix)
        mix = jnp.where(ids == Z0, z[inner_rows, :TILE], mix)
        at = cols + band_row * TILE
        pack[:, at : at + TILE] = jnp.transpose(mix)[:SUB, :]

    at = cols + rows
    pack[:, at:] = zero
    for i, m in enumerate((m0, m1, m2, m3)):
        pack[i : i + 1, at:] = jnp.sum(m, axis=0, keepdims=True)


def image_kernel(u, w, coef, after_stage, v):
    del after_stage
    rows, cols = w.shape
    tiles = cols // TILE
    unroll = 8

    def step(k, carry):
        at = pl.multiple_of(k * SUB, SUB)
        here_rows = pl.ds(at, SUB)
        coeffs = [coef[i, here_rows, :] for i in range(3)]
        line = line_of(u, at, tiles)
        for c in range(tiles):
            v[here_rows, columns(c)] = w[here_rows, columns(c)] - around(u, at, c, line, coeffs)
        return carry

    lax.fori_loop(0, rows // SUB, step, 0, unroll=unroll)


def row_kernel(rows, tabs, edges, row_ext, parts, corner):
    cols = row_ext.shape[1]
    height = tabs.shape[1]
    start = pl.multiple_of(lax.axis_index("lat") * rows, rows)
    col_lane = lane_ids(1, cols)
    first = tabs[:, pl.ds(start, TILE)]
    final = tabs[:, pl.ds(start + rows - TILE, TILE)]
    tab_n = tabs[:, pl.ds(pl.multiple_of(jnp.maximum(start - TILE, 0), TILE), TILE)]
    tab_s = tabs[:, pl.ds(pl.multiple_of(jnp.minimum(start + rows, height - TILE), TILE), TILE)]
    for which in range(2):
        at = 3 * which
        if which == 0:
            lane, own_tab, next_tab, next_lane = 0, first, tab_n, TILE - 1
            cross_row, inner_row, inv_row = UPPER, LOWER, I0
        else:
            lane, own_tab, next_tab, next_lane = TILE - 1, final, tab_s, 0
            cross_row, inner_row, inv_row = LOWER, UPPER, I1

        def scalar(tab, row, place):
            return wide(tab[row : row + 1, place : place + 1], cols)

        cross = scalar(own_tab, cross_row, lane)
        inner = scalar(own_tab, inner_row, lane)
        ew_own = scalar(own_tab, EAST_WEST, lane)
        ew_next = scalar(next_tab, EAST_WEST, next_lane)
        e = -cross * row_ext[at : at + 1, :]
        d = edges[inv_row : inv_row + 1, :cols] * e
        right = jnp.where(col_lane == cols - 1, 0.0, after(d))
        left = jnp.where(col_lane == 0, 0.0, before(d))
        dv = e - ew_own * (right + left) - cross * row_ext[at + 1 : at + 2, :]
        for i, row in enumerate((d, e, dv, inner * d)):
            parts[4 * which + i : 4 * which + i + 1, :] = row
        k = cross * ew_next * row_ext[at + 2 : at + 3, :]
        ids = lane_ids(1)
        corner[which : which + 1, :] = jnp.where(ids == 0, k[:, :TILE], k[:, cols - TILE :])


def sides(own, other, index, stage):
    size = 2**stage
    lower = lax.rem(lax.div(index, size), 2)
    inside = lax.rem(index, size)
    here, there = own[...], other[...]
    first = jnp.where(lower == 0, here, there)
    second = jnp.where(lower == 0, there, here)
    at_end = (lower == 0) & (inside == size - 1)
    at_start = (lower == 1) & (inside == 0)
    return first, second, at_end, at_start


def row_of(pack, i, start, stop):
    return pack[i : i + 1, start:stop]


def add_moments(out, at, first, second, changes):
    width = first.shape[1]
    out[:, at : at + TILE] = first[:, width - TILE :] + second[:, width - TILE :]
    for i, change in enumerate(changes):
        out[i + 1 : i + 2, at : at + TILE] += change


def lat_kernel(stage, stages, cols, tabs, own, other, ext_in, out, ext):
    facing = 0 < stage == stages - 1
    final = stage == stages - 1
    half = cols // 2
    span = half if facing else cols
    height = own.shape[1] - span - TILE
    index = lax.axis_index("lat")
    top, bottom, at_end, at_start = sides(own, other, index, stage)
    size = 2**stage
    border = pl.multiple_of((lax.div(index, 2 * size) * 2 * size + size) * (height // size), TILE)
    low = tabs[:, pl.ds(border, TILE)]
    high = tabs[:, pl.ds(border - TILE, TILE)]
    cross = wide(low[UPPER : UPPER + 1, :1], cols)
    ew_b = wide(low[EAST_WEST : EAST_WEST + 1, :1])
    ew_t = wide(high[EAST_WEST : EAST_WEST + 1, TILE - 1 :])
    next_b = wide(low[LOWER : LOWER + 1, :1])
    next_t = wide(high[UPPER : UPPER + 1, TILE - 1 :])

    if facing:

        def joined(pack, i):
            return jnp.concatenate(
                [row_of(pack, i, 0, half), row_of(pack, i + 4, 0, half)], axis=1
            )

        zt, ut, vt, it = (joined(top, i) for i in range(4))
        zb, ub, vb, ib = (joined(bottom, i) for i in range(4))
    else:
        zt, ut, vt, it = (row_of(top, i, 0, cols) for i in (Z1, U1, V1, I1))
        zb, ub, vb, ib = (row_of(bottom, i, 0, cols) for i in (Z0, U0, V0, I0))
    et, eb = -cross * zb, -cross * zt
    dt, db = it * et, ib * eb
    full_t, full_b = ut + dt, ub + db
    inside = lane_ids(1, cols) < cols - 1
    pair_t = jnp.where(inside, dt * after(dt), 0.0)
    pair_b = jnp.where(inside, db * after(db), 0.0)
    twice = fold(zt * et)
    second = fold((2.0 * ut + dt) * et + (2.0 * ub + db) * eb)
    third = fold(dt * (2.0 * vt + et) + db * (2.0 * vb + eb) - 2.0 * cross * full_t * full_b)
    third = third - 2.0 * (ew_t * fold(pair_t) + ew_b * fold(pair_b))

    if final:
        base = 0
    elif stage + 1 == stages - 1:
        base = half
        up_next = lax.rem(lax.div(index, 2 * size), 2) == 0
        for i, (first_row, last_row) in enumerate(((Z0, Z1), (U0, U1), (V0, V1), (I0, I1))):
            row = jnp.where(
                up_next, row_of(bottom, last_row, 0, cols), row_of(top, first_row, 0, cols)
            )
            out[i : i + 1, :half] = row[:, :half]
            out[i + 4 : i + 5, :half] = row[:, half:]
    else:
        base = cols
        ids = lax.broadcasted_iota(jnp.int32, (SUB, cols), 0)
        out[:, :cols] = jnp.where((ids < Z1) | (ids == I0), top[:, :cols], bottom[:, :cols])
    out[:, base : base + height] = top[:, span : span + height]
    out[:, base + height : base + 2 * height] = bottom[:, span : span + height]
    add_moments(out, base + 2 * height, top, bottom, (2.0 * twice, second, third))

    lane = lane_ids(1)
    upper_at = base + height - TILE
    lower_at = base + height
    c = cross[:, :TILE]
    for edge, inner, u_row, v_row in ((0, 1, U0, V0), (cols - 1, cols - 2, U1, V1)):

        def pick(row, place):
            return wide(row[:, place : place + 1])

        d_top, d_bottom = pick(dt, edge), pick(db, edge)
        v_top = pick(et, edge) - ew_t * pick(dt, inner) - c * pick(full_b, edge)
        v_bottom = pick(eb, edge) - ew_b * pick(db, inner) - c * pick(full_t, edge)
        out[u_row : u_row + 1, upper_at : upper_at + TILE] += jnp.where(
            lane == TILE - 1, d_top, 0.0
        )
        out[u_row : u_row + 1, lower_at : lower_at + TILE] += jnp.where(lane == 0, d_bottom, 0.0)
        out[v_row : v_row + 1, upper_at : upper_at + TILE] += jnp.where(
            lane == TILE - 1, v_top, jnp.where(lane == TILE - 2, -next_t * d_top, 0.0)
        )
        out[v_row : v_row + 1, lower_at : lower_at + TILE] += jnp.where(
            lane == 0, v_bottom, jnp.where(lane == 1, -next_b * d_bottom, 0.0)
        )

    if stage == 0:
        ext[...] = jnp.zeros((SUB, cols), jnp.float32)
    else:
        ext[...] = ext_in[...]

    @pl.when(at_start)
    def _():
        ext[0:1, :] = zt
        ext[1:2, :] = full_t
        ext[2:3, :] = it

    @pl.when(at_end)
    def _():
        ext[3:4, :] = zb
        ext[4:5, :] = full_b
        ext[5:6, :] = ib


def column_border(west, east, tabs):
    height = west.shape[1] - TILE
    zw, uw, vw, iw = (row_of(west, i, 0, height) for i in (Z1, U1, V1, I1))
    ze, ue, ve, ie = (row_of(east, i, 0, height) for i in (Z0, U0, V0, I0))
    ew = tabs[EAST_WEST : EAST_WEST + 1, :]
    inner = tabs[INNER : INNER + 1, :]
    to_w, to_e = -ew * ze, -ew * zw
    dw, de = iw * to_w, ie * to_e
    full_w, full_e = uw + dw, ue + de
    first = 2.0 * fold(zw * to_w)
    second = fold((2.0 * uw + dw) * to_w + (2.0 * ue + de) * to_e)
    third = fold(
        dw * (2.0 * vw + to_w)
        + de * (2.0 * ve + to_e)
        - 2.0 * inner * (dw * after(dw) + de * after(de))
        - 2.0 * ew * full_w * full_e
    )
    return (first, second, third), (zw, full_w), (ze, full_e)


def lon_kernel(stage, tabs, own, other, ext_in, out, ext):
    height = own.shape[1] - TILE
    west, east, at_end, at_start = sides(own, other, lax.axis_index("lon"), stage)
    changes, from_west, from_east = column_border(west, east, tabs)
    ids = lax.broadcasted_iota(jnp.int32, (SUB, height), 0)
    out[:, :height] = jnp.where((ids < Z1) | (ids == I0), west[:, :height], east[:, :height])
    add_moments(out, height, west, east, changes)
    if stage == 0:
        ext[...] = jnp.zeros((SUB, height), jnp.float32)
    else:
        ext[...] = ext_in[...]

    @pl.when(at_start)
    def _():
        ext[0:1, :], ext[1:2, :] = from_west

    @pl.when(at_end)
    def _():
        ext[2:3, :], ext[3:4, :] = from_east


def last_kernel(
    stage, chunk, tabs, own, other, ext_in, edges, row_parts, corner, src, z, u, w, v,
    out_x, out_r, mom, ext, field_x, field_r, cols_t, sems,
):
    rows, cols = src.shape
    height = own.shape[1] - TILE
    tiles = cols // TILE
    sectors = lax.axis_size("lon")
    index = lax.axis_index("lon")
    west, east, at_end, at_start = sides(own, other, index, stage)
    changes, from_west, from_east = column_border(west, east, tabs)
    wrap, round_west, round_east = column_border(east, west, tabs)
    add_moments(mom, 0, west, east, [a + b for a, b in zip(changes, wrap)])
    if stage == 0:
        ext[...] = jnp.zeros((SUB, height), jnp.float32)
    else:
        ext[...] = ext_in[...]

    @pl.when(at_start)
    def _():
        ext[0:1, :], ext[1:2, :] = from_west

    @pl.when(at_end)
    def _():
        ext[2:3, :], ext[3:4, :] = from_east

    @pl.when(index == 0)
    def _():
        ext[0:1, :], ext[1:2, :] = round_west

    @pl.when(index == sectors - 1)
    def _():
        ext[2:3, :], ext[3:4, :] = round_east

    sums = jnp.broadcast_to(jnp.sum(mom[...], axis=1, keepdims=True), (SUB, TILE))
    m0, m1, m2, m3 = (sums[i : i + 1, :] for i in range(4))
    alpha = m0 / m1
    fresh = alpha * alpha * m2 - 2.0 * alpha * m1 + m0
    grow = 1.0 + fresh / m0
    bend = grow * grow * m1 - 2.0 * grow * alpha * m2 + alpha * alpha * m3
    beta = fresh / bend
    near1, far1 = alpha + beta * grow, alpha * beta
    near = jnp.broadcast_to(near1, (SUB, TILE))
    far = jnp.broadcast_to(far1, (SUB, TILE))

    lat = lax.axis_index("lat")
    start = pl.multiple_of(lat * rows, rows)
    here = pl.ds(start, rows)
    ew = tabs[EAST_WEST : EAST_WEST + 1, here]
    up = tabs[UPPER : UPPER + 1, here]
    lo = tabs[LOWER : LOWER + 1, here]
    row_lane = lane_ids(1, rows)
    near_r = jnp.concatenate([near1] * (rows // TILE), axis=1)
    far_r = jnp.concatenate([far1] * (rows // TILE), axis=1)
    mods = []
    for z_row, inv_row in ((0, I0), (2, I1)):
        e = -ew * ext[z_row : z_row + 1, here]
        d = edges[inv_row : inv_row + 1, cols : cols + rows] * e
        above = jnp.where(row_lane == 0, 0.0, before(d))
        below = jnp.where(row_lane == rows - 1, 0.0, after(d))
        dv = e - up * above - lo * below - ew * ext[z_row + 1 : z_row + 2, here]
        mods += [-far_r * d, far_r * dv - near_r * e, -far_r * ew * d]
    mods += [jnp.zeros((1, rows), jnp.float32)] * 2
    cols_t[...] = jnp.transpose(jnp.concatenate(mods, axis=0))

    near_c = jnp.concatenate([near1] * tiles, axis=1)
    far_c = jnp.concatenate([far1] * tiles, axis=1)
    col_lane = lane_ids(1, cols)
    clamp_n = pl.multiple_of(jnp.maximum(start - TILE, 0), TILE)
    clamp_s = pl.multiple_of(jnp.minimum(start + rows, height - TILE), TILE)
    row_mods = []
    for which, (clamp, place) in enumerate(((clamp_n, TILE - 1), (clamp_s, 0))):
        next_ext = ext[:, pl.ds(clamp, TILE)]
        d, e, dv, inner_d = (row_parts[4 * which + i : 4 * which + i + 1, :] for i in range(4))

        def corner_of(row, lane):
            cell = corner[which : which + 1, lane : lane + 1] * next_ext[row : row + 1, place : place + 1]
            return wide(cell, cols)

        dv = dv + jnp.where(col_lane == 0, corner_of(0, 0), 0.0)
        dv = dv + jnp.where(col_lane == cols - 1, corner_of(2, TILE - 1), 0.0)
        row_mods.append((-far_c * d, far_c * dv - near_c * e, -far_c * inner_d))

    lane = lane_ids(SUB)
    blocks = chunk // SUB

    def copies(i):
        part = pl.ds(pl.multiple_of(i * chunk, SUB), chunk)
        return (
            pltpu.make_async_copy(field_x.at[part, :], out_x.at[part, :], sems.at[0]),
            pltpu.make_async_copy(field_r.at[part, :], out_r.at[part, :], sems.at[1]),
        )

    def step(k, carry):
        at = pl.multiple_of(k * SUB, SUB)
        here = pl.ds(at, SUB)
        lines = cols_t[here, :]
        for c in range(tiles):
            part = pl.ds(c * TILE, TILE)
            x = near * z[pl.ds(at + SUB, SUB), part] - far * u[pl.ds(at + SUB, SUB), part]
            r = src[here, part] - near * w[here, part] + far * v[here, part]
            if c == 0:
                x = x + jnp.where(lane == 0, wide(lines[:, 0:1]), 0.0)
                r = r + jnp.where(
                    lane == 0, wide(lines[:, 1:2]), jnp.where(lane == 1, wide(lines[:, 2:3]), 0.0)
                )
            if c == tiles - 1:
                x = x + jnp.where(lane == TILE - 1, wide(lines[:, 3:4]), 0.0)
                r = r + jnp.where(
                    lane == TILE - 1,
                    wide(lines[:, 4:5]),
                    jnp.where(lane == TILE - 2, wide(lines[:, 5:6]), 0.0),
                )
            field_x[here, part] = x
            field_r[here, part] = r
        return carry

    parts = rows // chunk
    for i in list(range(1, parts)) + [0]:
        lax.fori_loop(i * blocks, (i + 1) * blocks, step, 0, unroll=blocks)
        if i == 0:
            dx, dr, dr_next = row_mods[0]
            field_x[0:1, :] += dx
            field_r[0:1, :] += dr
            field_r[1:2, :] += dr_next
        if i == parts - 1:
            dx, dr, dr_next = row_mods[1]
            field_x[rows - 1 : rows, :] += dx
            field_r[rows - 1 : rows, :] += dr
            field_r[rows - 2 : rows - 1, :] += dr_next
        for copy in copies(i):
            copy.start()
    for i in range(parts):
        for copy in copies(i):
            copy.wait()


def shape(*dims):
    return jax.ShapeDtypeStruct(dims, jnp.float32)


def call(kernel, name, out_shape, in_specs, out_specs=None, scratch=(), limit=32, cost=None):
    return pl.pallas_call(
        kernel,
        name=name,
        out_shape=out_shape,
        in_specs=in_specs,
        out_specs=out_specs or [VMEM_SPEC] * len(out_shape),
        scratch_shapes=list(scratch),
        cost_estimate=cost,
        compiler_params=pltpu.CompilerParams(vmem_limit_bytes=limit << 20),
    )


def per_device(source, flags):
    rows, cols = source.shape
    bands, sectors = lax.axis_size("lat"), lax.axis_size("lon")
    height = rows * bands
    z, u, w, edges, tabs, src, coef = call(
        local_kernel,
        "local",
        [
            shape(rows + 2 * SUB, cols),
            shape(rows + 2 * SUB, cols),
            shape(rows, cols),
            shape(SUB, cols + rows + TILE),
            shape(SUB, height),
            shape(rows, cols),
            shape(3, rows, TILE),
        ],
        [HBM_SPEC, HBM_SPEC],
        scratch=[pltpu.VMEM((3, rows, TILE), jnp.float32)]
        + [pltpu.VMEM((rows, 2 * TILE), jnp.float32)]
        + [pltpu.SMEM(flags.shape, jnp.int32), pltpu.SemaphoreType.DMA((LOADS + 1,))],
    )(*(pltpu.with_memory_space_constraint(a, pltpu.HBM) for a in (flags, source)))

    def swap(pack, axis, stage):
        count = lax.axis_size(axis)
        return lax.ppermute(pack, axis, [(i, i ^ (1 << stage)) for i in range(count)])

    lat_stages = bands.bit_length() - 1
    lon_stages = sectors.bit_length() - 1
    pack, row_ext = edges, edges
    for stage in range(lat_stages):
        left = lat_stages - 1 - stage
        tall = (rows << (stage + 1)) + TILE + (cols, cols // 2, 0)[max(0, 2 - left)]
        pack, row_ext = call(
            functools.partial(lat_kernel, stage, lat_stages, cols),
            f"lat_merge{stage}",
            [shape(SUB, tall), shape(SUB, cols)],
            [VMEM_SPEC] * 4,
        )(tabs, pack, swap(pack, "lat", stage), row_ext)
        if stage == 0:
            v = call(
                image_kernel,
                "image",
                [shape(rows, cols)],
                [VMEM_SPEC] * 3 + [ANY_SPEC],
                cost=pl.CostEstimate(
                    flops=8 * rows * cols, bytes_accessed=12 * rows * cols, transcendentals=0
                ),
            )(u, w, coef, row_ext)[0]
    row_parts, corner = call(
        functools.partial(row_kernel, rows),
        "row_parts",
        [shape(SUB, cols), shape(SUB, TILE)],
        [VMEM_SPEC] * 3,
        cost=pl.CostEstimate(flops=60 * cols, bytes_accessed=64 * cols, transcendentals=0),
    )(tabs, edges, row_ext)
    col_ext = pack
    for stage in range(lon_stages - 1):
        pack, col_ext = call(
            functools.partial(lon_kernel, stage),
            f"lon_merge{stage}",
            [shape(SUB, height + TILE), shape(SUB, height)],
            [VMEM_SPEC] * 4,
        )(tabs, pack, swap(pack, "lon", stage), col_ext)
    stage = lon_stages - 1
    x, r = call(
        functools.partial(last_kernel, stage, 32),
        "combine",
        [shape(rows, cols), shape(rows, cols)],
        [VMEM_SPEC] * 12,
        out_specs=[HBM_SPEC, HBM_SPEC],
        scratch=[
            pltpu.VMEM((SUB, TILE), jnp.float32),
            pltpu.VMEM((SUB, height), jnp.float32),
            pltpu.VMEM((rows, cols), jnp.float32),
            pltpu.VMEM((rows, cols), jnp.float32),
            pltpu.VMEM((rows, SUB), jnp.float32),
            pltpu.SemaphoreType.DMA((2,)),
        ],
    )(tabs, pack, swap(pack, "lon", stage), col_ext, edges, row_parts, corner, src, z, u, w, v)
    return x, r


def solution(mesh):
    in_specs = (P("lat", "lon"), P("lat", "lon"))
    out_specs = (P("lat", "lon"), P("lat", "lon"))
    return jax.shard_map(
        per_device, mesh=mesh, in_specs=in_specs, out_specs=out_specs, check_vma=False
    )
```

```python
import functools
import math

import jax
import jax.numpy as jnp
from jax import lax
from jax.experimental import pallas as pl
from jax.experimental.pallas import tpu as pltpu
from jax.sharding import PartitionSpec as P

ARC_SPAN = 2.0 * math.pi / 3.0
TILE = 128
SUB = 8
VMEM_SPEC = pl.BlockSpec(memory_space=pltpu.VMEM)
HBM_SPEC = pl.BlockSpec(memory_space=pltpu.HBM)
ANY_SPEC = pl.BlockSpec(memory_space=pl.ANY)
LOADS = 4
Z0, U0, V0, Z1, U1, V1, I0, I1 = range(8)
EAST_WEST, UPPER, LOWER, INNER = range(4)
WEST_KINDS, EAST_KINDS = 4, 5
SCREENS = (0.05, 0.4, 2.0)


def coefficient_table(total_rows):
    row_pos = lax.broadcasted_iota(jnp.int32, (SUB, total_rows), 1).astype(jnp.float32)
    kind = lax.broadcasted_iota(jnp.int32, (SUB, total_rows), 0)
    ahead = jnp.where(kind == EAST_WEST, 0.5, jnp.where(kind == UPPER, 0.0, 1.0))
    table = jnp.cos((row_pos + ahead) / total_rows * ARC_SPAN - 0.5 * ARC_SPAN)
    return jnp.where((kind == INNER) & (row_pos == total_rows - 1), 0.0, table)


def fold(row):
    total = row[:, :TILE]
    for start in range(TILE, row.shape[1], TILE):
        total = total + row[:, start : start + TILE]
    return total


def wide(cell, width=TILE):
    return jnp.broadcast_to(cell, (cell.shape[0], width))


def after(row):
    return pltpu.roll(row, row.shape[1] - 1, 1)


def before(row):
    return pltpu.roll(row, 1, 1)


def lane_ids(rows, width=TILE):
    return lax.broadcasted_iota(jnp.int32, (rows, width), 1)


def columns(c):
    return pl.ds(c * TILE, TILE)


def line_of(field, at, tiles):
    zero = jnp.zeros((SUB, TILE), jnp.float32)
    return [zero] + [field[c, pl.ds(at + SUB, SUB), :] for c in range(tiles)] + [zero]


def ahead_of(field, at, c, line, coeffs):
    here = line[c + 1]
    below = field[c, pl.ds(at + SUB + 1, SUB), :]
    right = pltpu.roll(jnp.where(lane_ids(SUB) == 0, line[c + 2], here), TILE - 1, 1)
    return right, coeffs[2] * below


def behind_of(field, at, c, line, coeffs):
    here = line[c + 1]
    above = field[c, pl.ds(at + SUB - 1, SUB), :]
    left = pltpu.roll(jnp.where(lane_ids(SUB) == TILE - 1, line[c], here), 1, 1)
    return left, coeffs[1] * above


def around(field, at, c, line, coeffs):
    right, below = ahead_of(field, at, c, line, coeffs)
    left, above = behind_of(field, at, c, line, coeffs)
    return coeffs[0] * (right + left) + (above + below)


def folded_tables(tabs, folded):
    quarter = folded.shape[1] // 5
    base = [tabs[i : i + 1, :] for i in (EAST_WEST, UPPER, LOWER)]
    rows = [base[0], tabs[INNER : INNER + 1, :]]
    rows += [1.0 / (screen + 2.0 * base[0] + base[1] + base[2]) for screen in SCREENS]
    for i, row in enumerate(rows):
        for q in range(4):
            piece = row[:, q * quarter : (q + 1) * quarter]
            folded[q : q + 1, i * quarter : (i + 1) * quarter] = piece
            folded[q + 4 : q + 5, i * quarter : (i + 1) * quarter] = piece


def local_kernel(
    flags_in, source, z, u, w, pack, tabs, src, coef, folded, inv, v_edge, flags, sems
):
    rows, cols = src.shape
    tiles = cols // TILE
    blocks = TILE // SUB
    parts = sems.shape[0] - 1
    chunk = rows // parts
    flag_copy = pltpu.make_async_copy(flags_in, flags, sems.at[parts])
    flag_copy.start()
    loads = []
    for i in range(parts):
        part = pl.ds(i * chunk, chunk)
        loads.append(pltpu.make_async_copy(source.at[part, :], src.at[part, :], sems.at[i]))
        if i < 2:
            loads[-1].start()
    tabs[...] = coefficient_table(tabs.shape[1])
    folded_tables(tabs[...], folded)
    start = pl.multiple_of(lax.axis_index("lat") * rows, rows)
    band = jnp.transpose(tabs[:, pl.ds(start, rows)])
    ew = wide(band[:, EAST_WEST : EAST_WEST + 1])
    up = wide(band[:, UPPER : UPPER + 1])
    lo = wide(band[:, LOWER : LOWER + 1])
    for i, values in enumerate((ew, up, lo)):
        coef[i] = values
    for kind, screen in enumerate(SCREENS):
        inv[kind] = 1.0 / (screen + 2.0 * ew + up + lo)
    nothing = jnp.zeros((tiles, SUB, TILE), jnp.float32)
    for padded in (z, u):
        padded[:, :SUB, :] = nothing
        padded[:, rows + SUB :, :] = nothing
    zero = jnp.zeros((SUB, TILE), jnp.float32)
    flag_copy.wait()
    kinds = [
        [
            jnp.where(flags[band_row, c] == 0, 0, jnp.where(flags[band_row, c] == 1, 1, 2))
            for c in range(tiles)
        ]
        for band_row in range(rows // TILE)
    ]

    def first_pass(at, kind, sums):
        part = zero
        for c in range(tiles):
            b = src[pl.ds(at, SUB), columns(c)]
            value = b * inv[kind[c], pl.ds(at, SUB), :]
            z[c, pl.ds(at + SUB, SUB), :] = value
            part = part + b * value
        return (sums[0] + part,) + sums[1:]

    def second_pass(at, kind, sums):
        part1, part2 = zero, zero
        here_rows = pl.ds(at, SUB)
        coeffs = [coef[i, here_rows, :] for i in range(3)]
        line = line_of(z, at, tiles)
        for c in range(tiles):
            image = src[here_rows, columns(c)] - around(z, at, c, line, coeffs)
            scaled = image * inv[kind[c], here_rows, :]
            w[here_rows, columns(c)] = image
            u[c, pl.ds(at + SUB, SUB), :] = scaled
            part1 = part1 + line[c + 1] * image
            part2 = part2 + scaled * image
        return sums[0], sums[1] + part1, sums[2] + part2, sums[3]

    def third_pass(at, kind, sums):
        part = zero
        here_rows = pl.ds(at, SUB)
        coeffs = [coef[i, here_rows, :] for i in range(3)]
        line = line_of(u, at, tiles)
        for c in range(tiles):
            right, below = ahead_of(u, at, c, line, coeffs)
            near = coeffs[0] * right + below
            image = w[here_rows, columns(c)]
            part = part + line[c + 1] * (image - (near + near))
            if c in (0, tiles - 1):
                left, above = behind_of(u, at, c, line, coeffs)
                edge = pl.ds(0 if c == 0 else TILE, TILE)
                v_edge[here_rows, edge] = image - near - (coeffs[0] * left + above)
        return sums[:3] + (sums[3] + part,)

    count = rows // SUB
    done = [0, 0, 0]
    sums = (zero,) * 4
    for i in range(parts):
        loads[i].wait()
        if i + 2 < parts:
            loads[i + 2].start()
        ready = (i + 1) * (chunk // SUB)
        for which, body in enumerate((first_pass, second_pass, third_pass)):
            upto = ready - which if i + 1 < parts else count
            while done[which] < upto:
                band_row = done[which] // blocks
                stop = min(upto, (band_row + 1) * blocks)

                def step(k, carry, body=body, band_row=band_row):
                    return body(pl.multiple_of(k * SUB, SUB), kinds[band_row], carry)

                sums = lax.fori_loop(done[which], stop, step, sums, unroll=stop - done[which])
                done[which] = stop
    m0, m1, m2, m3 = sums

    last = rows - 1
    for c in range(tiles):
        for field, first_row, last_row in ((z, Z0, Z1), (u, U0, U1)):
            pack[first_row : first_row + 1, columns(c)] = field[c, SUB : SUB + 1, :]
            pack[last_row : last_row + 1, columns(c)] = field[c, last + SUB : last + SUB + 1, :]
    for at, v_row, place in ((0, V0, 0), (rows - SUB, V1, SUB - 1)):
        line = line_of(u, at, tiles)
        coeffs = [coef[i, at : at + SUB, :] for i in range(3)]
        for c in range(tiles):
            image = w[at : at + SUB, columns(c)] - around(u, at, c, line, coeffs)
            pack[v_row : v_row + 1, columns(c)] = image[place : place + 1, :]
    for c in range(tiles):
        pack[I0 : I0 + 1, c * TILE : (c + 1) * TILE] = inv[kinds[0][c], :1, :]
        pack[I1 : I1 + 1, c * TILE : (c + 1) * TILE] = inv[kinds[-1][c], last:, :]

    for band_row in range(rows // TILE):
        here_rows = slice(band_row * TILE, (band_row + 1) * TILE)
        inner_rows = slice(band_row * TILE + SUB, (band_row + 1) * TILE + SUB)
        ids = lane_ids(TILE)
        mix = inv[kinds[band_row][-1], here_rows, :]
        mix = jnp.where(ids == I0, inv[kinds[band_row][0], here_rows, :], mix)
        mix = jnp.where(ids == V1, pltpu.roll(v_edge[here_rows, TILE:], V1 + 1, 1), mix)
        mix = jnp.where(ids == U1, pltpu.roll(u[tiles - 1, inner_rows, :], U1 + 1, 1), mix)
        mix = jnp.where(ids == Z1, pltpu.roll(z[tiles - 1, inner_rows, :], Z1 + 1, 1), mix)
        mix = jnp.where(ids == V0, pltpu.roll(v_edge[here_rows, :TILE], V0, 1), mix)
        mix = jnp.where(ids == U0, pltpu.roll(u[0, inner_rows, :], U0, 1), mix)
        mix = jnp.where(ids == Z0, z[0, inner_rows, :], mix)
        at = cols + band_row * TILE
        pack[:, at : at + TILE] = jnp.transpose(mix)[:SUB, :]

    at = cols + rows
    pack[:, at:] = zero
    for i, m in enumerate((m0, m1, m2, m3)):
        pack[i : i + 1, at:] = jnp.sum(m, axis=0, keepdims=True)
    band_start = lax.axis_index("lat") * (rows // TILE)
    for i, c in ((WEST_KINDS, 0), (EAST_KINDS, tiles - 1)):
        line = jnp.zeros((1, TILE), jnp.float32)
        for band_row in range(rows // TILE):
            kind = jnp.full((1, TILE), kinds[band_row][c], jnp.int32).astype(jnp.float32)
            line = jnp.where(lane_ids(1) == band_start + band_row, kind, line)
        pack[i : i + 1, at:] = line


def image_kernel(u, w, coef, after_stage, v):
    del after_stage
    rows, cols = w.shape
    tiles = cols // TILE
    unroll = 8

    def step(k, carry):
        at = pl.multiple_of(k * SUB, SUB)
        here_rows = pl.ds(at, SUB)
        coeffs = [coef[i, here_rows, :] for i in range(3)]
        line = line_of(u, at, tiles)
        for c in range(tiles):
            v[here_rows, columns(c)] = w[here_rows, columns(c)] - around(u, at, c, line, coeffs)
        return carry

    lax.fori_loop(0, rows // SUB, step, 0, unroll=unroll)


def row_kernel(rows, tabs, edges, row_ext, parts, corner):
    cols = row_ext.shape[1]
    height = tabs.shape[1]
    start = pl.multiple_of(lax.axis_index("lat") * rows, rows)
    col_lane = lane_ids(1, cols)
    first = tabs[:, pl.ds(start, TILE)]
    final = tabs[:, pl.ds(start + rows - TILE, TILE)]
    tab_n = tabs[:, pl.ds(pl.multiple_of(jnp.maximum(start - TILE, 0), TILE), TILE)]
    tab_s = tabs[:, pl.ds(pl.multiple_of(jnp.minimum(start + rows, height - TILE), TILE), TILE)]
    for which in range(2):
        at = 3 * which
        if which == 0:
            lane, own_tab, next_tab, next_lane = 0, first, tab_n, TILE - 1
            cross_row, inner_row, inv_row = UPPER, LOWER, I0
        else:
            lane, own_tab, next_tab, next_lane = TILE - 1, final, tab_s, 0
            cross_row, inner_row, inv_row = LOWER, UPPER, I1

        def scalar(tab, row, place):
            return wide(tab[row : row + 1, place : place + 1], cols)

        cross = scalar(own_tab, cross_row, lane)
        inner = scalar(own_tab, inner_row, lane)
        ew_own = scalar(own_tab, EAST_WEST, lane)
        ew_next = scalar(next_tab, EAST_WEST, next_lane)
        e = -cross * row_ext[at : at + 1, :]
        d = edges[inv_row : inv_row + 1, :cols] * e
        right = jnp.where(col_lane == cols - 1, 0.0, after(d))
        left = jnp.where(col_lane == 0, 0.0, before(d))
        dv = e - ew_own * (right + left) - cross * row_ext[at + 1 : at + 2, :]
        for i, row in enumerate((d, e, dv, inner * d)):
            parts[4 * which + i : 4 * which + i + 1, :] = row
        k = cross * ew_next * row_ext[at + 2 : at + 3, :]
        ids = lane_ids(1)
        corner[which : which + 1, :] = jnp.where(ids == 0, k[:, :TILE], k[:, cols - TILE :])


def sides(own, other, index, stage):
    size = 2**stage
    lower = lax.rem(lax.div(index, size), 2)
    inside = lax.rem(index, size)
    here, there = own[...], other[...]
    first = jnp.where(lower == 0, here, there)
    second = jnp.where(lower == 0, there, here)
    at_end = (lower == 0) & (inside == size - 1)
    at_start = (lower == 1) & (inside == 0)
    return first, second, at_end, at_start


def row_of(pack, i, start, stop):
    return pack[i : i + 1, start:stop]


def add_moments(out, at, first, second, changes):
    width = first.shape[1]
    out[:, at : at + TILE] = first[:, width - TILE :] + second[:, width - TILE :]
    for i, change in enumerate(changes):
        out[i + 1 : i + 2, at : at + TILE] += change


def lat_kernel(stage, stages, cols, tabs, own, other, ext_in, result, ext, *scratch):
    out = scratch[0] if scratch else result
    facing = 0 < stage == stages - 1
    final = stage == stages - 1
    half = cols // 2
    span = half if facing else cols
    height = own.shape[1] - span - TILE
    index = lax.axis_index("lat")
    top, bottom, at_end, at_start = sides(own, other, index, stage)
    size = 2**stage
    border = pl.multiple_of((lax.div(index, 2 * size) * 2 * size + size) * (height // size), TILE)
    low = tabs[:, pl.ds(border, TILE)]
    high = tabs[:, pl.ds(border - TILE, TILE)]
    cross = wide(low[UPPER : UPPER + 1, :1], cols)
    ew_b = wide(low[EAST_WEST : EAST_WEST + 1, :1])
    ew_t = wide(high[EAST_WEST : EAST_WEST + 1, TILE - 1 :])
    next_b = wide(low[LOWER : LOWER + 1, :1])
    next_t = wide(high[UPPER : UPPER + 1, TILE - 1 :])

    if facing:

        def joined(pack, i):
            return jnp.concatenate(
                [row_of(pack, i, 0, half), row_of(pack, i + 4, 0, half)], axis=1
            )

        zt, ut, vt, it = (joined(top, i) for i in range(4))
        zb, ub, vb, ib = (joined(bottom, i) for i in range(4))
    else:
        zt, ut, vt, it = (row_of(top, i, 0, cols) for i in (Z1, U1, V1, I1))
        zb, ub, vb, ib = (row_of(bottom, i, 0, cols) for i in (Z0, U0, V0, I0))
    et, eb = -cross * zb, -cross * zt
    dt, db = it * et, ib * eb
    full_t, full_b = ut + dt, ub + db
    inside = lane_ids(1, cols) < cols - 1
    pair_t = jnp.where(inside, dt * after(dt), 0.0)
    pair_b = jnp.where(inside, db * after(db), 0.0)
    twice = fold(zt * et)
    second = fold((2.0 * ut + dt) * et + (2.0 * ub + db) * eb)
    third = fold(dt * (2.0 * vt + et) + db * (2.0 * vb + eb) - 2.0 * cross * full_t * full_b)
    third = third - 2.0 * (ew_t * fold(pair_t) + ew_b * fold(pair_b))

    if final:
        base = 0
    elif stage + 1 == stages - 1:
        base = half
        up_next = lax.rem(lax.div(index, 2 * size), 2) == 0
        for i, (first_row, last_row) in enumerate(((Z0, Z1), (U0, U1), (V0, V1), (I0, I1))):
            row = jnp.where(
                up_next, row_of(bottom, last_row, 0, cols), row_of(top, first_row, 0, cols)
            )
            out[i : i + 1, :half] = row[:, :half]
            out[i + 4 : i + 5, :half] = row[:, half:]
    else:
        base = cols
        ids = lax.broadcasted_iota(jnp.int32, (SUB, cols), 0)
        out[:, :cols] = jnp.where((ids < Z1) | (ids == I0), top[:, :cols], bottom[:, :cols])
    out[:, base : base + height] = top[:, span : span + height]
    out[:, base + height : base + 2 * height] = bottom[:, span : span + height]
    add_moments(out, base + 2 * height, top, bottom, (2.0 * twice, second, third))

    lane = lane_ids(1)
    upper_at = base + height - TILE
    lower_at = base + height
    c = cross[:, :TILE]
    for edge, inner, u_row, v_row in ((0, 1, U0, V0), (cols - 1, cols - 2, U1, V1)):

        def pick(row, place):
            return wide(row[:, place : place + 1])

        d_top, d_bottom = pick(dt, edge), pick(db, edge)
        v_top = pick(et, edge) - ew_t * pick(dt, inner) - c * pick(full_b, edge)
        v_bottom = pick(eb, edge) - ew_b * pick(db, inner) - c * pick(full_t, edge)
        out[u_row : u_row + 1, upper_at : upper_at + TILE] += jnp.where(
            lane == TILE - 1, d_top, 0.0
        )
        out[u_row : u_row + 1, lower_at : lower_at + TILE] += jnp.where(lane == 0, d_bottom, 0.0)
        out[v_row : v_row + 1, upper_at : upper_at + TILE] += jnp.where(
            lane == TILE - 1, v_top, jnp.where(lane == TILE - 2, -next_t * d_top, 0.0)
        )
        out[v_row : v_row + 1, lower_at : lower_at + TILE] += jnp.where(
            lane == 0, v_bottom, jnp.where(lane == 1, -next_b * d_bottom, 0.0)
        )

    if final:
        quarter = 2 * height // 4
        for i, row in enumerate((Z0, U0, V0, Z1, U1, V1)):
            part = slice((i % 3) * quarter, (i % 3 + 1) * quarter)
            for q in range(4):
                to = q + 4 * (i // 3)
                result[to : to + 1, part] = out[row : row + 1, q * quarter : (q + 1) * quarter]
        result[:, 3 * quarter :] = out[:, 2 * height :]

    if stage == 0:
        ext[...] = jnp.zeros((SUB, cols), jnp.float32)
    else:
        ext[...] = ext_in[...]

    @pl.when(at_start)
    def _():
        ext[0:1, :] = zt
        ext[1:2, :] = full_t
        ext[2:3, :] = it

    @pl.when(at_end)
    def _():
        ext[3:4, :] = zb
        ext[4:5, :] = full_b
        ext[5:6, :] = ib


def halves(quarter):
    return lax.broadcasted_iota(jnp.int32, (SUB, quarter), 0) < 4


def column_border(west, east, folded):
    quarter = (west.shape[1] - TILE) // 3
    low = halves(quarter)
    z, u, v = (
        jnp.where(low, east[:, part], west[:, part])
        for part in (slice(i * quarter, (i + 1) * quarter) for i in range(3))
    )
    ew, inner, *inverses = (folded[:, i * quarter : (i + 1) * quarter] for i in range(5))
    tiles = 4 * quarter // TILE
    each = tiles // 4
    east_kinds = jnp.broadcast_to(east[WEST_KINDS : WEST_KINDS + 1, 3 * quarter :], (SUB, TILE))
    west_kinds = jnp.broadcast_to(west[EAST_KINDS : EAST_KINDS + 1, 3 * quarter :], (SUB, TILE))
    kinds = jnp.where(halves(TILE), east_kinds, west_kinds)
    sub = lax.broadcasted_iota(jnp.int32, (SUB, TILE), 0)
    first = each * jnp.where(sub < 4, sub, sub - 4)
    spread = []
    for h in range(each):
        here = jnp.where(lane_ids(SUB) == first + h, kinds, 0.0)
        spread.append(wide(jnp.sum(here, axis=1, keepdims=True)))
    kind = jnp.concatenate(spread, axis=1)
    inv = jnp.where(kind < 0.5, inverses[0], jnp.where(kind < 1.5, inverses[1], inverses[2]))

    def across(x):
        return pltpu.roll(x, 4, 0)

    e = -ew * across(z)
    d = inv * e
    full = u + d
    moved = pltpu.roll(d, quarter - 1, 1)
    along = jnp.where(lane_ids(SUB, quarter) == quarter - 1, pltpu.roll(moved, SUB - 1, 0), moved)
    first_sum = fold(z * e)
    second = fold((u + full) * e)
    third = fold(d * (2.0 * v + e) - 2.0 * inner * d * along - ew * full * across(full))
    changes = [jnp.sum(x, axis=0, keepdims=True) for x in (first_sum, second, third)]
    return changes, jnp.concatenate([z, full], axis=1)


def merge_tiles(west, east):
    at = west.shape[1] - TILE
    ids = lax.broadcasted_iota(jnp.int32, (SUB, TILE), 0)
    kinds = jnp.where(ids == WEST_KINDS, west[:, at:], east[:, at:])
    return jnp.where(ids < WEST_KINDS, west[:, at:] + east[:, at:], kinds)


def keep_ext(ext, found, at_start, at_end):
    @pl.when(at_end)
    def _():
        ext[:4, :] = found[:4, :]

    @pl.when(at_start)
    def _():
        ext[4:, :] = found[4:, :]


def lon_kernel(stage, folded, own, other, ext_in, out, ext):
    at = own.shape[1] - TILE
    west, east, at_end, at_start = sides(own, other, lax.axis_index("lon"), stage)
    changes, found = column_border(west, east, folded)
    out[:, :at] = jnp.where(halves(at), west[:, :at], east[:, :at])
    out[:, at:] = merge_tiles(west, east)
    for i, change in enumerate(changes):
        out[i + 1 : i + 2, at:] += change
    if stage == 0:
        ext[...] = jnp.zeros(ext.shape, jnp.float32)
    else:
        ext[...] = ext_in[...]
    keep_ext(ext, found, at_start, at_end)


def last_kernel(
    stage, chunk, tabs, folded, own, other, ext_in, edges, row_parts, corner, src, z, u, w, v,
    out_x, out_r, mom, ext, field_x, field_r, cols_t, sems,
):
    rows, cols = src.shape
    height = tabs.shape[1]
    tiles = cols // TILE
    sectors = lax.axis_size("lon")
    index = lax.axis_index("lon")
    west, east, at_end, at_start = sides(own, other, index, stage)
    changes, found = column_border(west, east, folded)
    wrap, round_found = column_border(east, west, folded)
    mom[...] = merge_tiles(west, east)
    for i, (change, other_change) in enumerate(zip(changes, wrap)):
        mom[i + 1 : i + 2, :] += change + other_change
    if stage == 0:
        ext[...] = jnp.zeros(ext.shape, jnp.float32)
    else:
        ext[...] = ext_in[...]
    keep_ext(ext, found, at_start, at_end)
    keep_ext(ext, round_found, index == 0, index == sectors - 1)

    sums = jnp.broadcast_to(jnp.sum(mom[...], axis=1, keepdims=True), (SUB, TILE))
    m0, m1, m2, m3 = (sums[i : i + 1, :] for i in range(4))
    alpha = m0 / m1
    fresh = alpha * alpha * m2 - 2.0 * alpha * m1 + m0
    grow = 1.0 + fresh / m0
    bend = grow * grow * m1 - 2.0 * grow * alpha * m2 + alpha * alpha * m3
    beta = fresh / bend
    near1, far1 = alpha + beta * grow, alpha * beta
    near = jnp.broadcast_to(near1, (SUB, TILE))
    far = jnp.broadcast_to(far1, (SUB, TILE))

    lat = lax.axis_index("lat")
    start = pl.multiple_of(lat * rows, rows)
    here = pl.ds(start, rows)
    ew = tabs[EAST_WEST : EAST_WEST + 1, here]
    up = tabs[UPPER : UPPER + 1, here]
    lo = tabs[LOWER : LOWER + 1, here]
    row_lane = lane_ids(1, rows)
    near_r = jnp.concatenate([near1] * (rows // TILE), axis=1)
    far_r = jnp.concatenate([far1] * (rows // TILE), axis=1)
    mods = []
    for ext_row, inv_row in ((4 + lat, I0), (lat, I1)):
        e = -ew * ext[pl.ds(ext_row, 1), :rows]
        d = edges[inv_row : inv_row + 1, cols : cols + rows] * e
        above = jnp.where(row_lane == 0, 0.0, before(d))
        below = jnp.where(row_lane == rows - 1, 0.0, after(d))
        dv = e - up * above - lo * below - ew * ext[pl.ds(ext_row, 1), rows:]
        mods += [-far_r * d, far_r * dv - near_r * e, -far_r * ew * d]
    mods += [jnp.zeros((1, rows), jnp.float32)] * 2
    cols_t[...] = jnp.transpose(jnp.concatenate(mods, axis=0))

    near_c = jnp.concatenate([near1] * tiles, axis=1)
    far_c = jnp.concatenate([far1] * tiles, axis=1)
    col_lane = lane_ids(1, cols)
    row_mods = []
    for which, (band, place) in enumerate(
        ((jnp.maximum(lat - 1, 0), rows - 1), (jnp.minimum(lat + 1, 3), 0))
    ):
        beyond = [ext[pl.ds(4 + band, 1), :rows], ext[pl.ds(band, 1), :rows]]
        d, e, dv, inner_d = (row_parts[4 * which + i : 4 * which + i + 1, :] for i in range(4))

        def corner_of(side, lane):
            cell = corner[which : which + 1, lane : lane + 1] * beyond[side][:, place : place + 1]
            return wide(cell, cols)

        dv = dv + jnp.where(col_lane == 0, corner_of(0, 0), 0.0)
        dv = dv + jnp.where(col_lane == cols - 1, corner_of(1, TILE - 1), 0.0)
        row_mods.append((-far_c * d, far_c * dv - near_c * e, -far_c * inner_d))

    lane = lane_ids(SUB)
    blocks = chunk // SUB

    def copies(i):
        part = pl.ds(pl.multiple_of(i * chunk, SUB), chunk)
        return (
            pltpu.make_async_copy(field_x.at[part, :], out_x.at[part, :], sems.at[0]),
            pltpu.make_async_copy(field_r.at[part, :], out_r.at[part, :], sems.at[1]),
        )

    def step(k, carry):
        at = pl.multiple_of(k * SUB, SUB)
        here = pl.ds(at, SUB)
        lines = cols_t[here, :]
        for c in range(tiles):
            part = pl.ds(c * TILE, TILE)
            x = near * z[c, pl.ds(at + SUB, SUB), :] - far * u[c, pl.ds(at + SUB, SUB), :]
            r = src[here, part] - near * w[here, part] + far * v[here, part]
            if c == 0:
                x = x + jnp.where(lane == 0, wide(lines[:, 0:1]), 0.0)
                r = r + jnp.where(
                    lane == 0, wide(lines[:, 1:2]), jnp.where(lane == 1, wide(lines[:, 2:3]), 0.0)
                )
            if c == tiles - 1:
                x = x + jnp.where(lane == TILE - 1, wide(lines[:, 3:4]), 0.0)
                r = r + jnp.where(
                    lane == TILE - 1,
                    wide(lines[:, 4:5]),
                    jnp.where(lane == TILE - 2, wide(lines[:, 5:6]), 0.0),
                )
            field_x[here, part] = x
            field_r[here, part] = r
        return carry

    parts = rows // chunk
    for i in list(range(1, parts)) + [0]:
        lax.fori_loop(i * blocks, (i + 1) * blocks, step, 0, unroll=blocks)
        if i == 0:
            dx, dr, dr_next = row_mods[0]
            field_x[0:1, :] += dx
            field_r[0:1, :] += dr
            field_r[1:2, :] += dr_next
        if i == parts - 1:
            dx, dr, dr_next = row_mods[1]
            field_x[rows - 1 : rows, :] += dx
            field_r[rows - 1 : rows, :] += dr
            field_r[rows - 2 : rows - 1, :] += dr_next
        for copy in copies(i):
            copy.start()
    for i in range(parts):
        for copy in copies(i):
            copy.wait()


def shape(*dims):
    return jax.ShapeDtypeStruct(dims, jnp.float32)


def call(kernel, name, out_shape, in_specs, out_specs=None, scratch=(), limit=32, cost=None):
    return pl.pallas_call(
        kernel,
        name=name,
        out_shape=out_shape,
        in_specs=in_specs,
        out_specs=out_specs or [VMEM_SPEC] * len(out_shape),
        scratch_shapes=list(scratch),
        cost_estimate=cost,
        compiler_params=pltpu.CompilerParams(vmem_limit_bytes=limit << 20),
    )


def per_device(source, flags):
    rows, cols = source.shape
    bands, sectors = lax.axis_size("lat"), lax.axis_size("lon")
    height = rows * bands
    assert bands == 4
    z, u, w, edges, tabs, src, coef, folded = call(
        local_kernel,
        "local",
        [
            shape(cols // TILE, rows + 2 * SUB, TILE),
            shape(cols // TILE, rows + 2 * SUB, TILE),
            shape(rows, cols),
            shape(SUB, cols + rows + TILE),
            shape(SUB, height),
            shape(rows, cols),
            shape(3, rows, TILE),
            shape(SUB, 5 * rows),
        ],
        [HBM_SPEC, HBM_SPEC],
        scratch=[pltpu.VMEM((3, rows, TILE), jnp.float32)]
        + [pltpu.VMEM((rows, 2 * TILE), jnp.float32)]
        + [pltpu.SMEM(flags.shape, jnp.int32), pltpu.SemaphoreType.DMA((LOADS + 1,))],
    )(*(pltpu.with_memory_space_constraint(a, pltpu.HBM) for a in (flags, source)))

    def swap(pack, axis, stage):
        count = lax.axis_size(axis)
        return lax.ppermute(pack, axis, [(i, i ^ (1 << stage)) for i in range(count)])

    lat_stages = bands.bit_length() - 1
    lon_stages = sectors.bit_length() - 1
    pack, row_ext = edges, edges
    for stage in range(lat_stages):
        left = lat_stages - 1 - stage
        tall = (rows << (stage + 1)) + TILE + (cols, cols // 2, 0)[max(0, 2 - left)]
        pack, row_ext = call(
            functools.partial(lat_kernel, stage, lat_stages, cols),
            f"lat_merge{stage}",
            [shape(SUB, 3 * rows + TILE if left == 0 else tall), shape(SUB, cols)],
            [VMEM_SPEC] * 4,
            scratch=[pltpu.VMEM((SUB, tall), jnp.float32)] if left == 0 else (),
        )(tabs, pack, swap(pack, "lat", stage), row_ext)
        if stage == 0:
            v = call(
                image_kernel,
                "image",
                [shape(rows, cols)],
                [VMEM_SPEC] * 3 + [ANY_SPEC],
                cost=pl.CostEstimate(
                    flops=8 * rows * cols, bytes_accessed=12 * rows * cols, transcendentals=0
                ),
            )(u, w, coef, row_ext)[0]
    row_parts, corner = call(
        functools.partial(row_kernel, rows),
        "row_parts",
        [shape(SUB, cols), shape(SUB, TILE)],
        [VMEM_SPEC] * 3,
        cost=pl.CostEstimate(flops=60 * cols, bytes_accessed=64 * cols, transcendentals=0),
    )(tabs, edges, row_ext)
    col_ext = pack
    for stage in range(lon_stages - 1):
        pack, col_ext = call(
            functools.partial(lon_kernel, stage),
            f"lon_merge{stage}",
            [shape(SUB, 3 * rows + TILE), shape(SUB, 2 * rows)],
            [VMEM_SPEC] * 4,
        )(folded, pack, swap(pack, "lon", stage), col_ext)
    stage = lon_stages - 1
    x, r = call(
        functools.partial(last_kernel, stage, 32),
        "combine",
        [shape(rows, cols), shape(rows, cols)],
        [VMEM_SPEC] * 13,
        out_specs=[HBM_SPEC, HBM_SPEC],
        scratch=[
            pltpu.VMEM((SUB, TILE), jnp.float32),
            pltpu.VMEM((SUB, 2 * rows), jnp.float32),
            pltpu.VMEM((rows, cols), jnp.float32),
            pltpu.VMEM((rows, cols), jnp.float32),
            pltpu.VMEM((rows, SUB), jnp.float32),
            pltpu.SemaphoreType.DMA((2,)),
        ],
    )(tabs, folded, pack, swap(pack, "lon", stage), col_ext, edges, row_parts, corner, src, z, u, w, v)
    return x, r


def solution(mesh):
    in_specs = (P("lat", "lon"), P("lat", "lon"))
    out_specs = (P("lat", "lon"), P("lat", "lon"))
    return jax.shard_map(
        per_device, mesh=mesh, in_specs=in_specs, out_specs=out_specs, check_vma=False
    )
```

```python
import functools
import math

import jax
import jax.numpy as jnp
from jax import lax
from jax.experimental import pallas as pl
from jax.experimental.pallas import tpu as pltpu
from jax.sharding import PartitionSpec as P

ARC_SPAN = 2.0 * math.pi / 3.0
TILE = 128
SUB = 8
VMEM_SPEC = pl.BlockSpec(memory_space=pltpu.VMEM)
HBM_SPEC = pl.BlockSpec(memory_space=pltpu.HBM)
ANY_SPEC = pl.BlockSpec(memory_space=pl.ANY)
LOADS = 4
Z0, U0, V0, Z1, U1, V1, I0, I1 = range(8)
EAST_WEST, UPPER, LOWER, INNER = range(4)
WEST_KINDS, EAST_KINDS = 4, 5
SCREENS = (0.05, 0.4, 2.0)


def coefficient_table(total_rows):
    row_pos = lax.broadcasted_iota(jnp.int32, (SUB, total_rows), 1).astype(jnp.float32)
    kind = lax.broadcasted_iota(jnp.int32, (SUB, total_rows), 0)
    ahead = jnp.where(kind == EAST_WEST, 0.5, jnp.where(kind == UPPER, 0.0, 1.0))
    table = jnp.cos((row_pos + ahead) / total_rows * ARC_SPAN - 0.5 * ARC_SPAN)
    return jnp.where((kind == INNER) & (row_pos == total_rows - 1), 0.0, table)


def fold(row):
    total = row[:, :TILE]
    for start in range(TILE, row.shape[1], TILE):
        total = total + row[:, start : start + TILE]
    return total


def wide(cell, width=TILE):
    return jnp.broadcast_to(cell, (cell.shape[0], width))


def after(row):
    return pltpu.roll(row, row.shape[1] - 1, 1)


def before(row):
    return pltpu.roll(row, 1, 1)


def lane_ids(rows, width=TILE):
    return lax.broadcasted_iota(jnp.int32, (rows, width), 1)


def columns(c):
    return pl.ds(c * TILE, TILE)


def line_of(field, at, tiles):
    zero = jnp.zeros((SUB, TILE), jnp.float32)
    return [zero] + [field[c, pl.ds(at + SUB, SUB), :] for c in range(tiles)] + [zero]


def ahead_of(field, at, c, line, coeffs):
    here = line[c + 1]
    below = field[c, pl.ds(at + SUB + 1, SUB), :]
    right = pltpu.roll(jnp.where(lane_ids(SUB) == 0, line[c + 2], here), TILE - 1, 1)
    return right, coeffs[2] * below


def behind_of(field, at, c, line, coeffs):
    here = line[c + 1]
    above = field[c, pl.ds(at + SUB - 1, SUB), :]
    left = pltpu.roll(jnp.where(lane_ids(SUB) == TILE - 1, line[c], here), 1, 1)
    return left, coeffs[1] * above


def around(field, at, c, line, coeffs):
    right, below = ahead_of(field, at, c, line, coeffs)
    left, above = behind_of(field, at, c, line, coeffs)
    return coeffs[0] * (right + left) + (above + below)


def fold_place(row, c, eighth):
    sub, at = divmod(c * TILE, eighth)
    at += row * eighth
    return slice(sub, sub + 1), slice(at, at + TILE)


def next_cell(row):
    moved = pltpu.roll(row, row.shape[1] - 1, 1)
    ids = lane_ids(SUB, row.shape[1])
    return jnp.where(ids == row.shape[1] - 1, pltpu.roll(moved, SUB - 1, 0), moved)


def last_cell(row):
    moved = pltpu.roll(row, 1, 1)
    return jnp.where(lane_ids(SUB, row.shape[1]) == 0, pltpu.roll(moved, 1, 0), moved)


def cell_ids(width):
    return lax.broadcasted_iota(jnp.int32, (SUB, width), 0) * width + lane_ids(SUB, width)


def folded_tables(tabs, folded):
    quarter = folded.shape[1] // 5
    base = [tabs[i : i + 1, :] for i in (EAST_WEST, UPPER, LOWER)]
    rows = [base[0], tabs[INNER : INNER + 1, :]]
    rows += [1.0 / (screen + 2.0 * base[0] + base[1] + base[2]) for screen in SCREENS]
    for i, row in enumerate(rows):
        for q in range(4):
            piece = row[:, q * quarter : (q + 1) * quarter]
            folded[q : q + 1, i * quarter : (i + 1) * quarter] = piece
            folded[q + 4 : q + 5, i * quarter : (i + 1) * quarter] = piece


def local_kernel(
    flags_in, source, z, u, w, pack, tabs, src, coef, folded, inv, v_edge, flags, sems
):
    rows, cols = src.shape
    tiles = cols // TILE
    blocks = TILE // SUB
    parts = sems.shape[0] - 1
    chunk = rows // parts
    flag_copy = pltpu.make_async_copy(flags_in, flags, sems.at[parts])
    flag_copy.start()
    loads = []
    for i in range(parts):
        part = pl.ds(i * chunk, chunk)
        loads.append(pltpu.make_async_copy(source.at[part, :], src.at[part, :], sems.at[i]))
        if i < 2:
            loads[-1].start()
    tabs[...] = coefficient_table(tabs.shape[1])
    folded_tables(tabs[...], folded)
    start = pl.multiple_of(lax.axis_index("lat") * rows, rows)
    band = jnp.transpose(tabs[:, pl.ds(start, rows)])
    ew = wide(band[:, EAST_WEST : EAST_WEST + 1])
    up = wide(band[:, UPPER : UPPER + 1])
    lo = wide(band[:, LOWER : LOWER + 1])
    for i, values in enumerate((ew, up, lo)):
        coef[i] = values
    for kind, screen in enumerate(SCREENS):
        inv[kind] = 1.0 / (screen + 2.0 * ew + up + lo)
    nothing = jnp.zeros((tiles, SUB, TILE), jnp.float32)
    for padded in (z, u):
        padded[:, :SUB, :] = nothing
        padded[:, rows + SUB :, :] = nothing
    zero = jnp.zeros((SUB, TILE), jnp.float32)
    flag_copy.wait()
    kinds = [
        [
            jnp.where(flags[band_row, c] == 0, 0, jnp.where(flags[band_row, c] == 1, 1, 2))
            for c in range(tiles)
        ]
        for band_row in range(rows // TILE)
    ]

    def first_pass(at, kind, sums):
        part = zero
        for c in range(tiles):
            b = src[pl.ds(at, SUB), columns(c)]
            value = b * inv[kind[c], pl.ds(at, SUB), :]
            z[c, pl.ds(at + SUB, SUB), :] = value
            part = part + b * value
        return (sums[0] + part,) + sums[1:]

    def second_pass(at, kind, sums):
        part1, part2 = zero, zero
        here_rows = pl.ds(at, SUB)
        coeffs = [coef[i, here_rows, :] for i in range(3)]
        line = line_of(z, at, tiles)
        for c in range(tiles):
            image = src[here_rows, columns(c)] - around(z, at, c, line, coeffs)
            scaled = image * inv[kind[c], here_rows, :]
            w[here_rows, columns(c)] = image
            u[c, pl.ds(at + SUB, SUB), :] = scaled
            part1 = part1 + line[c + 1] * image
            part2 = part2 + scaled * image
        return sums[0], sums[1] + part1, sums[2] + part2, sums[3]

    def third_pass(at, kind, sums):
        part = zero
        here_rows = pl.ds(at, SUB)
        coeffs = [coef[i, here_rows, :] for i in range(3)]
        line = line_of(u, at, tiles)
        for c in range(tiles):
            right, below = ahead_of(u, at, c, line, coeffs)
            near = coeffs[0] * right + below
            image = w[here_rows, columns(c)]
            part = part + line[c + 1] * (image - (near + near))
            if c in (0, tiles - 1):
                left, above = behind_of(u, at, c, line, coeffs)
                edge = pl.ds(0 if c == 0 else TILE, TILE)
                v_edge[here_rows, edge] = image - near - (coeffs[0] * left + above)
        return sums[:3] + (sums[3] + part,)

    count = rows // SUB
    done = [0, 0, 0]
    sums = (zero,) * 4
    for i in range(parts):
        loads[i].wait()
        if i + 2 < parts:
            loads[i + 2].start()
        ready = (i + 1) * (chunk // SUB)
        for which, body in enumerate((first_pass, second_pass, third_pass)):
            upto = ready - which if i + 1 < parts else count
            while done[which] < upto:
                band_row = done[which] // blocks
                stop = min(upto, (band_row + 1) * blocks)

                def step(k, carry, body=body, band_row=band_row):
                    return body(pl.multiple_of(k * SUB, SUB), kinds[band_row], carry)

                sums = lax.fori_loop(done[which], stop, step, sums, unroll=stop - done[which])
                done[which] = stop
    m0, m1, m2, m3 = sums

    last = rows - 1
    def put(row, c, value):
        sub, lanes = fold_place(row, c, cols // SUB)
        pack[sub, lanes] = value

    for c in range(tiles):
        for field, first_row, last_row in ((z, Z0, Z1), (u, U0, U1)):
            put(first_row, c, field[c, SUB : SUB + 1, :])
            put(last_row, c, field[c, last + SUB : last + SUB + 1, :])
        put(I0, c, inv[kinds[0][c], :1, :])
        put(I1, c, inv[kinds[-1][c], last:, :])
    for at, v_row, place in ((0, V0, 0), (rows - SUB, V1, SUB - 1)):
        line = line_of(u, at, tiles)
        coeffs = [coef[i, at : at + SUB, :] for i in range(3)]
        for c in range(tiles):
            image = w[at : at + SUB, columns(c)] - around(u, at, c, line, coeffs)
            put(v_row, c, image[place : place + 1, :])

    for band_row in range(rows // TILE):
        here_rows = slice(band_row * TILE, (band_row + 1) * TILE)
        inner_rows = slice(band_row * TILE + SUB, (band_row + 1) * TILE + SUB)
        ids = lane_ids(TILE)
        mix = inv[kinds[band_row][-1], here_rows, :]
        mix = jnp.where(ids == I0, inv[kinds[band_row][0], here_rows, :], mix)
        mix = jnp.where(ids == V1, pltpu.roll(v_edge[here_rows, TILE:], V1 + 1, 1), mix)
        mix = jnp.where(ids == U1, pltpu.roll(u[tiles - 1, inner_rows, :], U1 + 1, 1), mix)
        mix = jnp.where(ids == Z1, pltpu.roll(z[tiles - 1, inner_rows, :], Z1 + 1, 1), mix)
        mix = jnp.where(ids == V0, pltpu.roll(v_edge[here_rows, :TILE], V0, 1), mix)
        mix = jnp.where(ids == U0, pltpu.roll(u[0, inner_rows, :], U0, 1), mix)
        mix = jnp.where(ids == Z0, z[0, inner_rows, :], mix)
        at = cols + band_row * TILE
        pack[:, at : at + TILE] = jnp.transpose(mix)[:SUB, :]

    at = cols + rows
    pack[:, at:] = zero
    for i, m in enumerate((m0, m1, m2, m3)):
        pack[i : i + 1, at:] = jnp.sum(m, axis=0, keepdims=True)
    band_start = lax.axis_index("lat") * (rows // TILE)
    for i, c in ((WEST_KINDS, 0), (EAST_KINDS, tiles - 1)):
        line = jnp.zeros((1, TILE), jnp.float32)
        for band_row in range(rows // TILE):
            kind = jnp.full((1, TILE), kinds[band_row][c], jnp.int32).astype(jnp.float32)
            line = jnp.where(lane_ids(1) == band_start + band_row, kind, line)
        pack[i : i + 1, at:] = line


def image_kernel(u, w, coef, after_stage, v):
    del after_stage
    rows, cols = w.shape
    tiles = cols // TILE
    unroll = 8

    def step(k, carry):
        at = pl.multiple_of(k * SUB, SUB)
        here_rows = pl.ds(at, SUB)
        coeffs = [coef[i, here_rows, :] for i in range(3)]
        line = line_of(u, at, tiles)
        for c in range(tiles):
            v[here_rows, columns(c)] = w[here_rows, columns(c)] - around(u, at, c, line, coeffs)
        return carry

    lax.fori_loop(0, rows // SUB, step, 0, unroll=unroll)


def row_kernel(rows, tabs, edges, row_ext, parts, corner):
    eighth = row_ext.shape[1] // 6
    cols = eighth * SUB
    height = tabs.shape[1]
    start = pl.multiple_of(lax.axis_index("lat") * rows, rows)
    cell = cell_ids(eighth)
    first = tabs[:, pl.ds(start, TILE)]
    final = tabs[:, pl.ds(start + rows - TILE, TILE)]
    tab_n = tabs[:, pl.ds(pl.multiple_of(jnp.maximum(start - TILE, 0), TILE), TILE)]
    tab_s = tabs[:, pl.ds(pl.multiple_of(jnp.minimum(start + rows, height - TILE), TILE), TILE)]
    for which in range(2):
        at = 3 * which
        if which == 0:
            lane, own_tab, next_tab, next_lane = 0, first, tab_n, TILE - 1
            cross_row, inner_row, inv_row = UPPER, LOWER, I0
        else:
            lane, own_tab, next_tab, next_lane = TILE - 1, final, tab_s, 0
            cross_row, inner_row, inv_row = LOWER, UPPER, I1

        def scalar(tab, row, place):
            return jnp.broadcast_to(tab[row : row + 1, place : place + 1], (SUB, eighth))

        def beyond(i):
            return row_ext[:, (at + i) * eighth : (at + i + 1) * eighth]

        cross = scalar(own_tab, cross_row, lane)
        inner = scalar(own_tab, inner_row, lane)
        ew_own = scalar(own_tab, EAST_WEST, lane)
        ew_next = scalar(next_tab, EAST_WEST, next_lane)
        e = -cross * beyond(0)
        d = edges[:, inv_row * eighth : (inv_row + 1) * eighth] * e
        right = jnp.where(cell == cols - 1, 0.0, next_cell(d))
        left = jnp.where(cell == 0, 0.0, last_cell(d))
        dv = e - ew_own * (right + left) - cross * beyond(1)
        for i, row in enumerate((d, e, dv, inner * d)):
            to = 4 * which + i
            for c in range(cols // TILE):
                sub, lanes = fold_place(0, c, eighth)
                parts[to : to + 1, columns(c)] = row[sub, lanes]
        k = cross * ew_next * beyond(2)
        ids = lane_ids(1)
        corner[which : which + 1, :] = jnp.where(
            ids == 0, k[:1, :TILE], k[SUB - 1 :, eighth - TILE :]
        )


def sides(own, other, index, stage):
    size = 2**stage
    lower = lax.rem(lax.div(index, size), 2)
    inside = lax.rem(index, size)
    here, there = own[...], other[...]
    first = jnp.where(lower == 0, here, there)
    second = jnp.where(lower == 0, there, here)
    at_end = (lower == 0) & (inside == size - 1)
    at_start = (lower == 1) & (inside == 0)
    return first, second, at_end, at_start


def row_of(pack, i, start, stop):
    return pack[i : i + 1, start:stop]


def add_moments(out, at, first, second, changes):
    width = first.shape[1]
    out[:, at : at + TILE] = first[:, width - TILE :] + second[:, width - TILE :]
    for i, change in enumerate(changes):
        out[i + 1 : i + 2, at : at + TILE] += change


def lat_kernel(stage, stages, cols, tabs, own, other, ext_in, result, ext, *scratch):
    out = scratch[0] if scratch else result
    facing = 0 < stage == stages - 1
    final = stage == stages - 1
    eighth = cols // SUB
    span = 4 * eighth if facing else cols
    height = own.shape[1] - span - TILE
    index = lax.axis_index("lat")
    top, bottom, at_end, at_start = sides(own, other, index, stage)
    size = 2**stage
    border = pl.multiple_of((lax.div(index, 2 * size) * 2 * size + size) * (height // size), TILE)
    low = tabs[:, pl.ds(border, TILE)]
    high = tabs[:, pl.ds(border - TILE, TILE)]
    cross = jnp.broadcast_to(low[UPPER : UPPER + 1, :1], (SUB, eighth))
    ew_b = wide(low[EAST_WEST : EAST_WEST + 1, :1])
    ew_t = wide(high[EAST_WEST : EAST_WEST + 1, TILE - 1 :])
    next_b = wide(low[LOWER : LOWER + 1, :1])
    next_t = wide(high[UPPER : UPPER + 1, TILE - 1 :])

    def block(pack, i):
        return pack[:, i * eighth : (i + 1) * eighth]

    zt, ut, vt, it = (block(top, i) for i in (range(4) if facing else (Z1, U1, V1, I1)))
    zb, ub, vb, ib = (block(bottom, i) for i in (range(4) if facing else (Z0, U0, V0, I0)))
    et, eb = -cross * zb, -cross * zt
    dt, db = it * et, ib * eb
    full_t, full_b = ut + dt, ub + db
    inside = cell_ids(eighth) < cols - 1
    pair_t = jnp.where(inside, dt * next_cell(dt), 0.0)
    pair_b = jnp.where(inside, db * next_cell(db), 0.0)

    def total(x):
        return jnp.sum(fold(x), axis=0, keepdims=True)

    twice = total(zt * et)
    second = total((2.0 * ut + dt) * et + (2.0 * ub + db) * eb)
    third = total(dt * (2.0 * vt + et) + db * (2.0 * vb + eb) - 2.0 * cross * full_t * full_b)
    third = third - 2.0 * (ew_t * total(pair_t) + ew_b * total(pair_b))

    if final:
        base = 0
    elif stage + 1 == stages - 1:
        base = 4 * eighth
        up_next = lax.rem(lax.div(index, 2 * size), 2) == 0
        for i, (first_row, last_row) in enumerate(((Z0, Z1), (U0, U1), (V0, V1), (I0, I1))):
            out[:, i * eighth : (i + 1) * eighth] = jnp.where(
                up_next, block(bottom, last_row), block(top, first_row)
            )
    else:
        base = cols
        for i in range(8):
            side = top if i in (Z0, U0, V0, I0) else bottom
            out[:, i * eighth : (i + 1) * eighth] = block(side, i)
    out[:, base : base + height] = top[:, span : span + height]
    out[:, base + height : base + 2 * height] = bottom[:, span : span + height]
    add_moments(out, base + 2 * height, top, bottom, (2.0 * twice, second, third))

    lane = lane_ids(1)
    upper_at = base + height - TILE
    lower_at = base + height
    c = cross[:1, :TILE]
    for edge, inner, u_row, v_row in ((0, 1, U0, V0), (cols - 1, cols - 2, U1, V1)):

        def pick(row, place):
            sub, lane_at = divmod(place, eighth)
            return wide(row[sub : sub + 1, lane_at : lane_at + 1])

        d_top, d_bottom = pick(dt, edge), pick(db, edge)
        v_top = pick(et, edge) - ew_t * pick(dt, inner) - c * pick(full_b, edge)
        v_bottom = pick(eb, edge) - ew_b * pick(db, inner) - c * pick(full_t, edge)
        out[u_row : u_row + 1, upper_at : upper_at + TILE] += jnp.where(
            lane == TILE - 1, d_top, 0.0
        )
        out[u_row : u_row + 1, lower_at : lower_at + TILE] += jnp.where(lane == 0, d_bottom, 0.0)
        out[v_row : v_row + 1, upper_at : upper_at + TILE] += jnp.where(
            lane == TILE - 1, v_top, jnp.where(lane == TILE - 2, -next_t * d_top, 0.0)
        )
        out[v_row : v_row + 1, lower_at : lower_at + TILE] += jnp.where(
            lane == 0, v_bottom, jnp.where(lane == 1, -next_b * d_bottom, 0.0)
        )

    if final:
        quarter = 2 * height // 4
        for i, row in enumerate((Z0, U0, V0, Z1, U1, V1)):
            part = slice((i % 3) * quarter, (i % 3 + 1) * quarter)
            for q in range(4):
                to = q + 4 * (i // 3)
                result[to : to + 1, part] = out[row : row + 1, q * quarter : (q + 1) * quarter]
        result[:, 3 * quarter :] = out[:, 2 * height :]

    if stage == 0:
        ext[...] = jnp.zeros(ext.shape, jnp.float32)
    else:
        ext[...] = ext_in[...]

    def keep(first_block, values):
        for i, value in enumerate(values):
            at = (first_block + i) * eighth
            ext[:, at : at + eighth] = value

    @pl.when(at_start)
    def _():
        keep(0, (zt, full_t, it))

    @pl.when(at_end)
    def _():
        keep(3, (zb, full_b, ib))


def halves(quarter):
    return lax.broadcasted_iota(jnp.int32, (SUB, quarter), 0) < 4


def column_border(west, east, folded):
    quarter = (west.shape[1] - TILE) // 3
    low = halves(quarter)
    z, u, v = (
        jnp.where(low, east[:, part], west[:, part])
        for part in (slice(i * quarter, (i + 1) * quarter) for i in range(3))
    )
    ew, inner, *inverses = (folded[:, i * quarter : (i + 1) * quarter] for i in range(5))
    tiles = 4 * quarter // TILE
    each = tiles // 4
    east_kinds = jnp.broadcast_to(east[WEST_KINDS : WEST_KINDS + 1, 3 * quarter :], (SUB, TILE))
    west_kinds = jnp.broadcast_to(west[EAST_KINDS : EAST_KINDS + 1, 3 * quarter :], (SUB, TILE))
    kinds = jnp.where(halves(TILE), east_kinds, west_kinds)
    sub = lax.broadcasted_iota(jnp.int32, (SUB, TILE), 0)
    first = each * jnp.where(sub < 4, sub, sub - 4)
    spread = []
    for h in range(each):
        here = jnp.where(lane_ids(SUB) == first + h, kinds, 0.0)
        spread.append(wide(jnp.sum(here, axis=1, keepdims=True)))
    kind = jnp.concatenate(spread, axis=1)
    inv = jnp.where(kind < 0.5, inverses[0], jnp.where(kind < 1.5, inverses[1], inverses[2]))

    def across(x):
        return pltpu.roll(x, 4, 0)

    e = -ew * across(z)
    d = inv * e
    full = u + d
    along = next_cell(d)
    first_sum = fold(z * e)
    second = fold((u + full) * e)
    third = fold(d * (2.0 * v + e) - 2.0 * inner * d * along - ew * full * across(full))
    changes = [jnp.sum(x, axis=0, keepdims=True) for x in (first_sum, second, third)]
    return changes, jnp.concatenate([z, full], axis=1)


def merge_tiles(west, east):
    at = west.shape[1] - TILE
    ids = lax.broadcasted_iota(jnp.int32, (SUB, TILE), 0)
    kinds = jnp.where(ids == WEST_KINDS, west[:, at:], east[:, at:])
    return jnp.where(ids < WEST_KINDS, west[:, at:] + east[:, at:], kinds)


def keep_ext(ext, found, at_start, at_end):
    @pl.when(at_end)
    def _():
        ext[:4, :] = found[:4, :]

    @pl.when(at_start)
    def _():
        ext[4:, :] = found[4:, :]


def lon_kernel(stage, folded, own, other, ext_in, out, ext):
    at = own.shape[1] - TILE
    west, east, at_end, at_start = sides(own, other, lax.axis_index("lon"), stage)
    changes, found = column_border(west, east, folded)
    out[:, :at] = jnp.where(halves(at), west[:, :at], east[:, :at])
    out[:, at:] = merge_tiles(west, east)
    for i, change in enumerate(changes):
        out[i + 1 : i + 2, at:] += change
    if stage == 0:
        ext[...] = jnp.zeros(ext.shape, jnp.float32)
    else:
        ext[...] = ext_in[...]
    keep_ext(ext, found, at_start, at_end)


def last_kernel(
    stage, chunk, tabs, folded, own, other, ext_in, edges, row_parts, corner, src, z, u, w, v,
    out_x, out_r, mom, ext, field_x, field_r, cols_t, sems,
):
    rows, cols = src.shape
    height = tabs.shape[1]
    tiles = cols // TILE
    sectors = lax.axis_size("lon")
    index = lax.axis_index("lon")
    west, east, at_end, at_start = sides(own, other, index, stage)
    changes, found = column_border(west, east, folded)
    wrap, round_found = column_border(east, west, folded)
    mom[...] = merge_tiles(west, east)
    for i, (change, other_change) in enumerate(zip(changes, wrap)):
        mom[i + 1 : i + 2, :] += change + other_change
    if stage == 0:
        ext[...] = jnp.zeros(ext.shape, jnp.float32)
    else:
        ext[...] = ext_in[...]
    keep_ext(ext, found, at_start, at_end)
    keep_ext(ext, round_found, index == 0, index == sectors - 1)

    sums = jnp.broadcast_to(jnp.sum(mom[...], axis=1, keepdims=True), (SUB, TILE))
    m0, m1, m2, m3 = (sums[i : i + 1, :] for i in range(4))
    alpha = m0 / m1
    fresh = alpha * alpha * m2 - 2.0 * alpha * m1 + m0
    grow = 1.0 + fresh / m0
    bend = grow * grow * m1 - 2.0 * grow * alpha * m2 + alpha * alpha * m3
    beta = fresh / bend
    near1, far1 = alpha + beta * grow, alpha * beta
    near = jnp.broadcast_to(near1, (SUB, TILE))
    far = jnp.broadcast_to(far1, (SUB, TILE))

    lat = lax.axis_index("lat")
    start = pl.multiple_of(lat * rows, rows)
    here = pl.ds(start, rows)
    ew = tabs[EAST_WEST : EAST_WEST + 1, here]
    up = tabs[UPPER : UPPER + 1, here]
    lo = tabs[LOWER : LOWER + 1, here]
    row_lane = lane_ids(1, rows)
    near_r = jnp.concatenate([near1] * (rows // TILE), axis=1)
    far_r = jnp.concatenate([far1] * (rows // TILE), axis=1)
    mods = []
    for ext_row, inv_row in ((4 + lat, I0), (lat, I1)):
        e = -ew * ext[pl.ds(ext_row, 1), :rows]
        d = edges[inv_row : inv_row + 1, cols : cols + rows] * e
        above = jnp.where(row_lane == 0, 0.0, before(d))
        below = jnp.where(row_lane == rows - 1, 0.0, after(d))
        dv = e - up * above - lo * below - ew * ext[pl.ds(ext_row, 1), rows:]
        mods += [-far_r * d, far_r * dv - near_r * e, -far_r * ew * d]
    mods += [jnp.zeros((1, rows), jnp.float32)] * 2
    cols_t[...] = jnp.transpose(jnp.concatenate(mods, axis=0))

    near_c = jnp.concatenate([near1] * tiles, axis=1)
    far_c = jnp.concatenate([far1] * tiles, axis=1)
    col_lane = lane_ids(1, cols)
    row_mods = []
    for which, (band, place) in enumerate(
        ((jnp.maximum(lat - 1, 0), rows - 1), (jnp.minimum(lat + 1, 3), 0))
    ):
        beyond = [ext[pl.ds(4 + band, 1), :rows], ext[pl.ds(band, 1), :rows]]
        d, e, dv, inner_d = (row_parts[4 * which + i : 4 * which + i + 1, :] for i in range(4))

        def corner_of(side, lane):
            cell = corner[which : which + 1, lane : lane + 1] * beyond[side][:, place : place + 1]
            return wide(cell, cols)

        dv = dv + jnp.where(col_lane == 0, corner_of(0, 0), 0.0)
        dv = dv + jnp.where(col_lane == cols - 1, corner_of(1, TILE - 1), 0.0)
        row_mods.append((-far_c * d, far_c * dv - near_c * e, -far_c * inner_d))

    lane = lane_ids(SUB)
    blocks = chunk // SUB

    def copies(i):
        part = pl.ds(pl.multiple_of(i * chunk, SUB), chunk)
        return (
            pltpu.make_async_copy(field_x.at[part, :], out_x.at[part, :], sems.at[0]),
            pltpu.make_async_copy(field_r.at[part, :], out_r.at[part, :], sems.at[1]),
        )

    def step(k, carry):
        at = pl.multiple_of(k * SUB, SUB)
        here = pl.ds(at, SUB)
        lines = cols_t[here, :]
        for c in range(tiles):
            part = pl.ds(c * TILE, TILE)
            x = near * z[c, pl.ds(at + SUB, SUB), :] - far * u[c, pl.ds(at + SUB, SUB), :]
            r = src[here, part] - near * w[here, part] + far * v[here, part]
            if c == 0:
                x = x + jnp.where(lane == 0, wide(lines[:, 0:1]), 0.0)
                r = r + jnp.where(
                    lane == 0, wide(lines[:, 1:2]), jnp.where(lane == 1, wide(lines[:, 2:3]), 0.0)
                )
            if c == tiles - 1:
                x = x + jnp.where(lane == TILE - 1, wide(lines[:, 3:4]), 0.0)
                r = r + jnp.where(
                    lane == TILE - 1,
                    wide(lines[:, 4:5]),
                    jnp.where(lane == TILE - 2, wide(lines[:, 5:6]), 0.0),
                )
            field_x[here, part] = x
            field_r[here, part] = r
        return carry

    parts = rows // chunk
    for i in list(range(1, parts)) + [0]:
        lax.fori_loop(i * blocks, (i + 1) * blocks, step, 0, unroll=blocks)
        if i == 0:
            dx, dr, dr_next = row_mods[0]
            field_x[0:1, :] += dx
            field_r[0:1, :] += dr
            field_r[1:2, :] += dr_next
        if i == parts - 1:
            dx, dr, dr_next = row_mods[1]
            field_x[rows - 1 : rows, :] += dx
            field_r[rows - 1 : rows, :] += dr
            field_r[rows - 2 : rows - 1, :] += dr_next
        for copy in copies(i):
            copy.start()
    for i in range(parts):
        for copy in copies(i):
            copy.wait()


def shape(*dims):
    return jax.ShapeDtypeStruct(dims, jnp.float32)


def call(kernel, name, out_shape, in_specs, out_specs=None, scratch=(), limit=32, cost=None):
    return pl.pallas_call(
        kernel,
        name=name,
        out_shape=out_shape,
        in_specs=in_specs,
        out_specs=out_specs or [VMEM_SPEC] * len(out_shape),
        scratch_shapes=list(scratch),
        cost_estimate=cost,
        compiler_params=pltpu.CompilerParams(vmem_limit_bytes=limit << 20),
    )


def per_device(source, flags):
    rows, cols = source.shape
    bands, sectors = lax.axis_size("lat"), lax.axis_size("lon")
    height = rows * bands
    assert bands == 4
    z, u, w, edges, tabs, src, coef, folded = call(
        local_kernel,
        "local",
        [
            shape(cols // TILE, rows + 2 * SUB, TILE),
            shape(cols // TILE, rows + 2 * SUB, TILE),
            shape(rows, cols),
            shape(SUB, cols + rows + TILE),
            shape(SUB, height),
            shape(rows, cols),
            shape(3, rows, TILE),
            shape(SUB, 5 * rows),
        ],
        [HBM_SPEC, HBM_SPEC],
        scratch=[pltpu.VMEM((3, rows, TILE), jnp.float32)]
        + [pltpu.VMEM((rows, 2 * TILE), jnp.float32)]
        + [pltpu.SMEM(flags.shape, jnp.int32), pltpu.SemaphoreType.DMA((LOADS + 1,))],
    )(*(pltpu.with_memory_space_constraint(a, pltpu.HBM) for a in (flags, source)))

    def swap(pack, axis, stage):
        count = lax.axis_size(axis)
        return lax.ppermute(pack, axis, [(i, i ^ (1 << stage)) for i in range(count)])

    lat_stages = bands.bit_length() - 1
    lon_stages = sectors.bit_length() - 1
    pack, row_ext = edges, edges
    for stage in range(lat_stages):
        left = lat_stages - 1 - stage
        tall = (rows << (stage + 1)) + TILE + (cols, cols // 2, 0)[max(0, 2 - left)]
        pack, row_ext = call(
            functools.partial(lat_kernel, stage, lat_stages, cols),
            f"lat_merge{stage}",
            [shape(SUB, 3 * rows + TILE if left == 0 else tall), shape(SUB, 6 * cols // SUB)],
            [VMEM_SPEC] * 4,
            scratch=[pltpu.VMEM((SUB, tall), jnp.float32)] if left == 0 else (),
        )(tabs, pack, swap(pack, "lat", stage), row_ext)
        if stage == 0:
            v = call(
                image_kernel,
                "image",
                [shape(rows, cols)],
                [VMEM_SPEC] * 3 + [ANY_SPEC],
                cost=pl.CostEstimate(
                    flops=8 * rows * cols, bytes_accessed=12 * rows * cols, transcendentals=0
                ),
            )(u, w, coef, row_ext)[0]
    row_parts, corner = call(
        functools.partial(row_kernel, rows),
        "row_parts",
        [shape(SUB, cols), shape(SUB, TILE)],
        [VMEM_SPEC] * 3,
        cost=pl.CostEstimate(flops=60 * cols, bytes_accessed=64 * cols, transcendentals=0),
    )(tabs, edges, row_ext)
    col_ext = pack
    for stage in range(lon_stages - 1):
        pack, col_ext = call(
            functools.partial(lon_kernel, stage),
            f"lon_merge{stage}",
            [shape(SUB, 3 * rows + TILE), shape(SUB, 2 * rows)],
            [VMEM_SPEC] * 4,
        )(folded, pack, swap(pack, "lon", stage), col_ext)
    stage = lon_stages - 1
    x, r = call(
        functools.partial(last_kernel, stage, 32),
        "combine",
        [shape(rows, cols), shape(rows, cols)],
        [VMEM_SPEC] * 13,
        out_specs=[HBM_SPEC, HBM_SPEC],
        scratch=[
            pltpu.VMEM((SUB, TILE), jnp.float32),
            pltpu.VMEM((SUB, 2 * rows), jnp.float32),
            pltpu.VMEM((rows, cols), jnp.float32),
            pltpu.VMEM((rows, cols), jnp.float32),
            pltpu.VMEM((rows, SUB), jnp.float32),
            pltpu.SemaphoreType.DMA((2,)),
        ],
    )(tabs, folded, pack, swap(pack, "lon", stage), col_ext, edges, row_parts, corner, src, z, u, w, v)
    return x, r


def solution(mesh):
    in_specs = (P("lat", "lon"), P("lat", "lon"))
    out_specs = (P("lat", "lon"), P("lat", "lon"))
    return jax.shard_map(
        per_device, mesh=mesh, in_specs=in_specs, out_specs=out_specs, check_vma=False
    )
```

```python
import functools
import math

import jax
import jax.numpy as jnp
from jax import lax
from jax.experimental import pallas as pl
from jax.experimental.pallas import tpu as pltpu
from jax.sharding import PartitionSpec as P

ARC_SPAN = 2.0 * math.pi / 3.0
TILE = 128
SUB = 8
VMEM_SPEC = pl.BlockSpec(memory_space=pltpu.VMEM)
HBM_SPEC = pl.BlockSpec(memory_space=pltpu.HBM)
ANY_SPEC = pl.BlockSpec(memory_space=pl.ANY)
LOADS = 4
Z0, U0, V0, Z1, U1, V1, I0, I1 = range(8)
EAST_WEST, UPPER, LOWER, INNER = range(4)
WEST_KINDS, EAST_KINDS = 4, 5
SCREENS = (0.05, 0.4, 2.0)


def coefficient_table(total_rows):
    row_pos = lax.broadcasted_iota(jnp.int32, (SUB, total_rows), 1).astype(jnp.float32)
    kind = lax.broadcasted_iota(jnp.int32, (SUB, total_rows), 0)
    ahead = jnp.where(kind == EAST_WEST, 0.5, jnp.where(kind == UPPER, 0.0, 1.0))
    table = jnp.cos((row_pos + ahead) / total_rows * ARC_SPAN - 0.5 * ARC_SPAN)
    return jnp.where((kind == INNER) & (row_pos == total_rows - 1), 0.0, table)


def fold(row):
    total = row[:, :TILE]
    for start in range(TILE, row.shape[1], TILE):
        total = total + row[:, start : start + TILE]
    return total


def wide(cell, width=TILE):
    return jnp.broadcast_to(cell, (cell.shape[0], width))


def after(row):
    return pltpu.roll(row, row.shape[1] - 1, 1)


def before(row):
    return pltpu.roll(row, 1, 1)


def lane_ids(rows, width=TILE):
    return lax.broadcasted_iota(jnp.int32, (rows, width), 1)


def columns(c):
    return pl.ds(c * TILE, TILE)


def line_of(field, at, tiles):
    zero = jnp.zeros((SUB, TILE), jnp.float32)
    return [zero] + [field[c, pl.ds(at + SUB, SUB), :] for c in range(tiles)] + [zero]


def ahead_of(field, at, c, line, coeffs):
    here = line[c + 1]
    below = field[c, pl.ds(at + SUB + 1, SUB), :]
    right = pltpu.roll(jnp.where(lane_ids(SUB) == 0, line[c + 2], here), TILE - 1, 1)
    return right, coeffs[2] * below


def behind_of(field, at, c, line, coeffs):
    here = line[c + 1]
    above = field[c, pl.ds(at + SUB - 1, SUB), :]
    left = pltpu.roll(jnp.where(lane_ids(SUB) == TILE - 1, line[c], here), 1, 1)
    return left, coeffs[1] * above


def around(field, at, c, line, coeffs):
    right, below = ahead_of(field, at, c, line, coeffs)
    left, above = behind_of(field, at, c, line, coeffs)
    return coeffs[0] * (right + left) + (above + below)


def fold_place(row, c, eighth):
    sub, at = divmod(c * TILE, eighth)
    at += row * eighth
    return slice(sub, sub + 1), slice(at, at + TILE)


def next_cell(row):
    moved = pltpu.roll(row, row.shape[1] - 1, 1)
    ids = lane_ids(SUB, row.shape[1])
    return jnp.where(ids == row.shape[1] - 1, pltpu.roll(moved, SUB - 1, 0), moved)


def last_cell(row):
    moved = pltpu.roll(row, 1, 1)
    return jnp.where(lane_ids(SUB, row.shape[1]) == 0, pltpu.roll(moved, 1, 0), moved)


def cell_ids(width):
    return lax.broadcasted_iota(jnp.int32, (SUB, width), 0) * width + lane_ids(SUB, width)


def folded_tables(tabs, folded):
    quarter = folded.shape[1] // 5
    base = [tabs[i : i + 1, :] for i in (EAST_WEST, UPPER, LOWER)]
    rows = [base[0], tabs[INNER : INNER + 1, :]]
    rows += [1.0 / (screen + 2.0 * base[0] + base[1] + base[2]) for screen in SCREENS]
    for i, row in enumerate(rows):
        for q in range(4):
            piece = row[:, q * quarter : (q + 1) * quarter]
            folded[q : q + 1, i * quarter : (i + 1) * quarter] = piece
            folded[q + 4 : q + 5, i * quarter : (i + 1) * quarter] = piece


def local_kernel(
    flags_in, source, z, u, w, pack, tabs, src, coef, folded, inv, v_edge, flags, sems
):
    rows, cols = src.shape
    tiles = cols // TILE
    blocks = TILE // SUB
    parts = sems.shape[0] - 1
    chunk = rows // parts
    flag_copy = pltpu.make_async_copy(flags_in, flags, sems.at[parts])
    flag_copy.start()
    loads = []
    for i in range(parts):
        part = pl.ds(i * chunk, chunk)
        loads.append(pltpu.make_async_copy(source.at[part, :], src.at[part, :], sems.at[i]))
        if i < 2:
            loads[-1].start()
    tabs[...] = coefficient_table(tabs.shape[1])
    folded_tables(tabs[...], folded)
    start = pl.multiple_of(lax.axis_index("lat") * rows, rows)
    band = jnp.transpose(tabs[:, pl.ds(start, rows)])
    ew = wide(band[:, EAST_WEST : EAST_WEST + 1])
    up = wide(band[:, UPPER : UPPER + 1])
    lo = wide(band[:, LOWER : LOWER + 1])
    for i, values in enumerate((ew, up, lo)):
        coef[i] = values
    for kind, screen in enumerate(SCREENS):
        inv[kind] = 1.0 / (screen + 2.0 * ew + up + lo)
    nothing = jnp.zeros((tiles, SUB, TILE), jnp.float32)
    for padded in (z, u):
        padded[:, :SUB, :] = nothing
        padded[:, rows + SUB :, :] = nothing
    zero = jnp.zeros((SUB, TILE), jnp.float32)
    flag_copy.wait()
    kinds = [
        [
            jnp.where(flags[band_row, c] == 0, 0, jnp.where(flags[band_row, c] == 1, 1, 2))
            for c in range(tiles)
        ]
        for band_row in range(rows // TILE)
    ]

    def first_pass(at, kind, sums):
        part = zero
        for c in range(tiles):
            b = src[pl.ds(at, SUB), columns(c)]
            value = b * inv[kind[c], pl.ds(at, SUB), :]
            z[c, pl.ds(at + SUB, SUB), :] = value
            part = part + b * value
        return (sums[0] + part,) + sums[1:]

    def second_pass(at, kind, sums):
        part1, part2 = zero, zero
        here_rows = pl.ds(at, SUB)
        coeffs = [coef[i, here_rows, :] for i in range(3)]
        line = line_of(z, at, tiles)
        for c in range(tiles):
            image = src[here_rows, columns(c)] - around(z, at, c, line, coeffs)
            scaled = image * inv[kind[c], here_rows, :]
            w[here_rows, columns(c)] = image
            u[c, pl.ds(at + SUB, SUB), :] = scaled
            part1 = part1 + line[c + 1] * image
            part2 = part2 + scaled * image
        return sums[0], sums[1] + part1, sums[2] + part2, sums[3]

    def third_pass(at, kind, sums):
        part = zero
        here_rows = pl.ds(at, SUB)
        coeffs = [coef[i, here_rows, :] for i in range(3)]
        line = line_of(u, at, tiles)
        for c in range(tiles):
            right, below = ahead_of(u, at, c, line, coeffs)
            near = coeffs[0] * right + below
            image = w[here_rows, columns(c)]
            part = part + line[c + 1] * (image - (near + near))
            if c in (0, tiles - 1):
                left, above = behind_of(u, at, c, line, coeffs)
                edge = pl.ds(0 if c == 0 else TILE, TILE)
                v_edge[here_rows, edge] = image - near - (coeffs[0] * left + above)
        return sums[:3] + (sums[3] + part,)

    count = rows // SUB
    done = [0, 0, 0]
    sums = (zero,) * 4
    for i in range(parts):
        loads[i].wait()
        if i + 2 < parts:
            loads[i + 2].start()
        ready = (i + 1) * (chunk // SUB)
        for which, body in enumerate((first_pass, second_pass, third_pass)):
            upto = ready - which if i + 1 < parts else count
            while done[which] < upto:
                band_row = done[which] // blocks
                stop = min(upto, (band_row + 1) * blocks)

                def step(k, carry, body=body, band_row=band_row):
                    return body(pl.multiple_of(k * SUB, SUB), kinds[band_row], carry)

                sums = lax.fori_loop(done[which], stop, step, sums, unroll=stop - done[which])
                done[which] = stop
    m0, m1, m2, m3 = sums

    last = rows - 1
    def put(row, c, value):
        sub, lanes = fold_place(row, c, cols // SUB)
        pack[sub, lanes] = value

    for c in range(tiles):
        for field, first_row, last_row in ((z, Z0, Z1), (u, U0, U1)):
            put(first_row, c, field[c, SUB : SUB + 1, :])
            put(last_row, c, field[c, last + SUB : last + SUB + 1, :])
        put(I0, c, inv[kinds[0][c], :1, :])
        put(I1, c, inv[kinds[-1][c], last:, :])
    for at, v_row, place in ((0, V0, 0), (rows - SUB, V1, SUB - 1)):
        line = line_of(u, at, tiles)
        coeffs = [coef[i, at : at + SUB, :] for i in range(3)]
        for c in range(tiles):
            image = w[at : at + SUB, columns(c)] - around(u, at, c, line, coeffs)
            put(v_row, c, image[place : place + 1, :])

    for band_row in range(rows // TILE):
        here_rows = slice(band_row * TILE, (band_row + 1) * TILE)
        inner_rows = slice(band_row * TILE + SUB, (band_row + 1) * TILE + SUB)
        ids = lane_ids(TILE)
        mix = inv[kinds[band_row][-1], here_rows, :]
        mix = jnp.where(ids == I0, inv[kinds[band_row][0], here_rows, :], mix)
        mix = jnp.where(ids == V1, pltpu.roll(v_edge[here_rows, TILE:], V1 + 1, 1), mix)
        mix = jnp.where(ids == U1, pltpu.roll(u[tiles - 1, inner_rows, :], U1 + 1, 1), mix)
        mix = jnp.where(ids == Z1, pltpu.roll(z[tiles - 1, inner_rows, :], Z1 + 1, 1), mix)
        mix = jnp.where(ids == V0, pltpu.roll(v_edge[here_rows, :TILE], V0, 1), mix)
        mix = jnp.where(ids == U0, pltpu.roll(u[0, inner_rows, :], U0, 1), mix)
        mix = jnp.where(ids == Z0, z[0, inner_rows, :], mix)
        at = cols + band_row * TILE
        pack[:, at : at + TILE] = jnp.transpose(mix)[:SUB, :]

    at = cols + rows
    pack[:, at:] = zero
    for i, m in enumerate((m0, m1, m2, m3)):
        pack[i : i + 1, at:] = jnp.sum(m, axis=0, keepdims=True)
    band_start = lax.axis_index("lat") * (rows // TILE)
    for i, c in ((WEST_KINDS, 0), (EAST_KINDS, tiles - 1)):
        line = jnp.zeros((1, TILE), jnp.float32)
        for band_row in range(rows // TILE):
            kind = jnp.full((1, TILE), kinds[band_row][c], jnp.int32).astype(jnp.float32)
            line = jnp.where(lane_ids(1) == band_start + band_row, kind, line)
        pack[i : i + 1, at:] = line


def image_kernel(u, w, coef, after_stage, v):
    del after_stage
    rows, cols = w.shape
    tiles = cols // TILE
    unroll = 8

    def step(k, carry):
        at = pl.multiple_of(k * SUB, SUB)
        here_rows = pl.ds(at, SUB)
        coeffs = [coef[i, here_rows, :] for i in range(3)]
        line = line_of(u, at, tiles)
        for c in range(tiles):
            v[here_rows, columns(c)] = w[here_rows, columns(c)] - around(u, at, c, line, coeffs)
        return carry

    lax.fori_loop(0, rows // SUB, step, 0, unroll=unroll)


def row_kernel(rows, tabs, edges, row_ext, parts, corner):
    eighth = row_ext.shape[1] // 6
    cols = eighth * SUB
    height = tabs.shape[1]
    start = pl.multiple_of(lax.axis_index("lat") * rows, rows)
    cell = cell_ids(eighth)
    first = tabs[:, pl.ds(start, TILE)]
    final = tabs[:, pl.ds(start + rows - TILE, TILE)]
    tab_n = tabs[:, pl.ds(pl.multiple_of(jnp.maximum(start - TILE, 0), TILE), TILE)]
    tab_s = tabs[:, pl.ds(pl.multiple_of(jnp.minimum(start + rows, height - TILE), TILE), TILE)]
    for which in range(2):
        at = 3 * which
        if which == 0:
            lane, own_tab, next_tab, next_lane = 0, first, tab_n, TILE - 1
            cross_row, inner_row, inv_row = UPPER, LOWER, I0
        else:
            lane, own_tab, next_tab, next_lane = TILE - 1, final, tab_s, 0
            cross_row, inner_row, inv_row = LOWER, UPPER, I1

        def scalar(tab, row, place):
            return jnp.broadcast_to(tab[row : row + 1, place : place + 1], (SUB, eighth))

        def beyond(i):
            return row_ext[:, (at + i) * eighth : (at + i + 1) * eighth]

        cross = scalar(own_tab, cross_row, lane)
        inner = scalar(own_tab, inner_row, lane)
        ew_own = scalar(own_tab, EAST_WEST, lane)
        ew_next = scalar(next_tab, EAST_WEST, next_lane)
        e = -cross * beyond(0)
        d = edges[:, inv_row * eighth : (inv_row + 1) * eighth] * e
        right = jnp.where(cell == cols - 1, 0.0, next_cell(d))
        left = jnp.where(cell == 0, 0.0, last_cell(d))
        dv = e - ew_own * (right + left) - cross * beyond(1)
        for i, row in enumerate((d, e, dv, inner * d)):
            to = 4 * which + i
            for c in range(cols // TILE):
                sub, lanes = fold_place(0, c, eighth)
                parts[to : to + 1, columns(c)] = row[sub, lanes]
        k = cross * ew_next * beyond(2)
        ids = lane_ids(1)
        corner[which : which + 1, :] = jnp.where(
            ids == 0, k[:1, :TILE], k[SUB - 1 :, eighth - TILE :]
        )


def sides(own, other, index, stage):
    size = 2**stage
    lower = lax.rem(lax.div(index, size), 2)
    inside = lax.rem(index, size)
    here, there = own[...], other[...]
    first = jnp.where(lower == 0, here, there)
    second = jnp.where(lower == 0, there, here)
    at_end = (lower == 0) & (inside == size - 1)
    at_start = (lower == 1) & (inside == 0)
    return first, second, at_end, at_start


def row_of(pack, i, start, stop):
    return pack[i : i + 1, start:stop]


def add_moments(out, at, first, second, changes):
    width = first.shape[1]
    out[:, at : at + TILE] = first[:, width - TILE :] + second[:, width - TILE :]
    for i, change in enumerate(changes):
        out[i + 1 : i + 2, at : at + TILE] += change


def lat_kernel(stage, stages, cols, tabs, own, other, ext_in, result, ext, *scratch):
    out = scratch[0] if scratch else result
    facing = 0 < stage == stages - 1
    final = stage == stages - 1
    eighth = cols // SUB
    span = 4 * eighth if facing else cols
    height = own.shape[1] - span - TILE
    index = lax.axis_index("lat")
    top, bottom, at_end, at_start = sides(own, other, index, stage)
    size = 2**stage
    border = pl.multiple_of((lax.div(index, 2 * size) * 2 * size + size) * (height // size), TILE)
    low = tabs[:, pl.ds(border, TILE)]
    high = tabs[:, pl.ds(border - TILE, TILE)]
    cross = jnp.broadcast_to(low[UPPER : UPPER + 1, :1], (SUB, eighth))
    ew_b = wide(low[EAST_WEST : EAST_WEST + 1, :1])
    ew_t = wide(high[EAST_WEST : EAST_WEST + 1, TILE - 1 :])
    next_b = wide(low[LOWER : LOWER + 1, :1])
    next_t = wide(high[UPPER : UPPER + 1, TILE - 1 :])

    def block(pack, i):
        return pack[:, i * eighth : (i + 1) * eighth]

    zt, ut, vt, it = (block(top, i) for i in (range(4) if facing else (Z1, U1, V1, I1)))
    zb, ub, vb, ib = (block(bottom, i) for i in (range(4) if facing else (Z0, U0, V0, I0)))
    et, eb = -cross * zb, -cross * zt
    dt, db = it * et, ib * eb
    full_t, full_b = ut + dt, ub + db
    inside = cell_ids(eighth) < cols - 1
    pair_t = jnp.where(inside, dt * next_cell(dt), 0.0)
    pair_b = jnp.where(inside, db * next_cell(db), 0.0)

    def total(x):
        return jnp.sum(fold(x), axis=0, keepdims=True)

    twice = total(zt * et)
    second = total((2.0 * ut + dt) * et + (2.0 * ub + db) * eb)
    third = total(dt * (2.0 * vt + et) + db * (2.0 * vb + eb) - 2.0 * cross * full_t * full_b)
    third = third - 2.0 * (ew_t * total(pair_t) + ew_b * total(pair_b))

    if final:
        base = 0
    elif stage + 1 == stages - 1:
        base = 4 * eighth
        up_next = lax.rem(lax.div(index, 2 * size), 2) == 0
        for i, (first_row, last_row) in enumerate(((Z0, Z1), (U0, U1), (V0, V1), (I0, I1))):
            out[:, i * eighth : (i + 1) * eighth] = jnp.where(
                up_next, block(bottom, last_row), block(top, first_row)
            )
    else:
        base = cols
        for i in range(8):
            side = top if i in (Z0, U0, V0, I0) else bottom
            out[:, i * eighth : (i + 1) * eighth] = block(side, i)
    out[:, base : base + height] = top[:, span : span + height]
    out[:, base + height : base + 2 * height] = bottom[:, span : span + height]
    add_moments(out, base + 2 * height, top, bottom, (2.0 * twice, second, third))

    lane = lane_ids(1)
    upper_at = base + height - TILE
    lower_at = base + height
    c = cross[:1, :TILE]
    for edge, inner, u_row, v_row in ((0, 1, U0, V0), (cols - 1, cols - 2, U1, V1)):

        def pick(row, place):
            sub, lane_at = divmod(place, eighth)
            return wide(row[sub : sub + 1, lane_at : lane_at + 1])

        d_top, d_bottom = pick(dt, edge), pick(db, edge)
        v_top = pick(et, edge) - ew_t * pick(dt, inner) - c * pick(full_b, edge)
        v_bottom = pick(eb, edge) - ew_b * pick(db, inner) - c * pick(full_t, edge)
        out[u_row : u_row + 1, upper_at : upper_at + TILE] += jnp.where(
            lane == TILE - 1, d_top, 0.0
        )
        out[u_row : u_row + 1, lower_at : lower_at + TILE] += jnp.where(lane == 0, d_bottom, 0.0)
        out[v_row : v_row + 1, upper_at : upper_at + TILE] += jnp.where(
            lane == TILE - 1, v_top, jnp.where(lane == TILE - 2, -next_t * d_top, 0.0)
        )
        out[v_row : v_row + 1, lower_at : lower_at + TILE] += jnp.where(
            lane == 0, v_bottom, jnp.where(lane == 1, -next_b * d_bottom, 0.0)
        )

    if final:
        quarter = 2 * height // 4
        for i, row in enumerate((Z0, U0, V0, Z1, U1, V1)):
            part = slice((i % 3) * quarter, (i % 3 + 1) * quarter)
            for q in range(4):
                to = q + 4 * (i // 3)
                result[to : to + 1, part] = out[row : row + 1, q * quarter : (q + 1) * quarter]
        result[:, 3 * quarter :] = out[:, 2 * height :]

    if stage == 0:
        ext[...] = jnp.zeros(ext.shape, jnp.float32)
    else:
        ext[...] = ext_in[...]

    def keep(first_block, values):
        for i, value in enumerate(values):
            at = (first_block + i) * eighth
            ext[:, at : at + eighth] = value

    @pl.when(at_start)
    def _():
        keep(0, (zt, full_t, it))

    @pl.when(at_end)
    def _():
        keep(3, (zb, full_b, ib))


def halves(quarter):
    return lax.broadcasted_iota(jnp.int32, (SUB, quarter), 0) < 4


def column_border(west, east, folded):
    quarter = (west.shape[1] - TILE) // 3
    low = halves(quarter)
    z, u, v = (
        jnp.where(low, east[:, part], west[:, part])
        for part in (slice(i * quarter, (i + 1) * quarter) for i in range(3))
    )
    ew, inner, *inverses = (folded[:, i * quarter : (i + 1) * quarter] for i in range(5))
    tiles = 4 * quarter // TILE
    each = tiles // 4
    east_kinds = jnp.broadcast_to(east[WEST_KINDS : WEST_KINDS + 1, 3 * quarter :], (SUB, TILE))
    west_kinds = jnp.broadcast_to(west[EAST_KINDS : EAST_KINDS + 1, 3 * quarter :], (SUB, TILE))
    kinds = jnp.where(halves(TILE), east_kinds, west_kinds)
    sub = lax.broadcasted_iota(jnp.int32, (SUB, TILE), 0)
    first = each * jnp.where(sub < 4, sub, sub - 4)
    spread = []
    for h in range(each):
        here = jnp.where(lane_ids(SUB) == first + h, kinds, 0.0)
        spread.append(wide(jnp.sum(here, axis=1, keepdims=True)))
    kind = jnp.concatenate(spread, axis=1)
    inv = jnp.where(kind < 0.5, inverses[0], jnp.where(kind < 1.5, inverses[1], inverses[2]))

    def across(x):
        return pltpu.roll(x, 4, 0)

    e = -ew * across(z)
    d = inv * e
    full = u + d
    along = next_cell(d)
    first_sum = fold(z * e)
    second = fold((u + full) * e)
    third = fold(d * (2.0 * v + e) - 2.0 * inner * d * along - ew * full * across(full))
    changes = [jnp.sum(x, axis=0, keepdims=True) for x in (first_sum, second, third)]
    return changes, jnp.concatenate([z, full], axis=1)


def merge_tiles(west, east):
    at = west.shape[1] - TILE
    ids = lax.broadcasted_iota(jnp.int32, (SUB, TILE), 0)
    kinds = jnp.where(ids == WEST_KINDS, west[:, at:], east[:, at:])
    return jnp.where(ids < WEST_KINDS, west[:, at:] + east[:, at:], kinds)


def keep_ext(ext, found, at_start, at_end):
    @pl.when(at_end)
    def _():
        ext[:4, :] = found[:4, :]

    @pl.when(at_start)
    def _():
        ext[4:, :] = found[4:, :]


def lon_kernel(stage, folded, own, other, ext_in, out, ext):
    at = own.shape[1] - TILE
    west, east, at_end, at_start = sides(own, other, lax.axis_index("lon"), stage)
    changes, found = column_border(west, east, folded)
    out[:, :at] = jnp.where(halves(at), west[:, :at], east[:, :at])
    out[:, at:] = merge_tiles(west, east)
    for i, change in enumerate(changes):
        out[i + 1 : i + 2, at:] += change
    if stage == 0:
        ext[...] = jnp.zeros(ext.shape, jnp.float32)
    else:
        ext[...] = ext_in[...]
    keep_ext(ext, found, at_start, at_end)


def last_kernel(
    stage, chunk, tabs, folded, own, other, ext_in, edges, row_parts, corner, src, z, u, w, v,
    out_x, out_r, mom, ext, field_x, field_r, cols_t, sems,
):
    rows, cols = src.shape
    height = tabs.shape[1]
    tiles = cols // TILE
    sectors = lax.axis_size("lon")
    index = lax.axis_index("lon")
    west, east, at_end, at_start = sides(own, other, index, stage)
    changes, found = column_border(west, east, folded)
    wrap, round_found = column_border(east, west, folded)
    mom[...] = merge_tiles(west, east)
    for i, (change, other_change) in enumerate(zip(changes, wrap)):
        mom[i + 1 : i + 2, :] += change + other_change
    sums = jnp.broadcast_to(jnp.sum(mom[...], axis=1, keepdims=True), (SUB, TILE))
    m0, m1, m2, m3 = (sums[i : i + 1, :] for i in range(4))
    alpha = m0 / m1
    fresh = alpha * alpha * m2 - 2.0 * alpha * m1 + m0
    grow = 1.0 + fresh / m0
    bend = grow * grow * m1 - 2.0 * grow * alpha * m2 + alpha * alpha * m3
    beta = fresh / bend
    near1, far1 = alpha + beta * grow, alpha * beta
    near = jnp.broadcast_to(near1, (SUB, TILE))
    far = jnp.broadcast_to(far1, (SUB, TILE))

    lane = lane_ids(SUB)
    blocks = chunk // SUB
    parts = rows // chunk
    early = (1, 2)
    copies = []

    def send(i, first_col, last_col):
        here = pl.ds(i * chunk, chunk), pl.ds(first_col, last_col - first_col)
        for k, (field, out) in enumerate(((field_x, out_x), (field_r, out_r))):
            copies.append(pltpu.make_async_copy(field.at[here], out.at[here], sems.at[k]))
            copies[-1].start()

    def cells(at, c):
        here, part = pl.ds(at, SUB), columns(c)
        x = near * z[c, pl.ds(at + SUB, SUB), :] - far * u[c, pl.ds(at + SUB, SUB), :]
        r = src[here, part] - near * w[here, part] + far * v[here, part]
        return x, r

    def inner(i):
        for at in range(i * chunk, (i + 1) * chunk, SUB):
            for c in range(1, tiles - 1):
                x, r = cells(at, c)
                field_x[at : at + SUB, columns(c)] = x
                field_r[at : at + SUB, columns(c)] = r

    def edge(i):
        for at in range(i * chunk, (i + 1) * chunk, SUB):
            lines = cols_t[at : at + SUB, :]
            for c, k, end, inside in ((0, 0, 0, 1), (tiles - 1, 3, TILE - 1, TILE - 2)):
                x, r = cells(at, c)
                dx, dr, dr_next = (wide(lines[:, k + j : k + j + 1]) for j in range(3))
                field_x[at : at + SUB, columns(c)] = x + jnp.where(lane == end, dx, 0.0)
                field_r[at : at + SUB, columns(c)] = r + jnp.where(
                    lane == end, dr, jnp.where(lane == inside, dr_next, 0.0)
                )

    for i in early:
        inner(i)
        send(i, TILE, cols - TILE)

    if stage == 0:
        ext[...] = jnp.zeros(ext.shape, jnp.float32)
    else:
        ext[...] = ext_in[...]
    keep_ext(ext, found, at_start, at_end)
    keep_ext(ext, round_found, index == 0, index == sectors - 1)

    lat = lax.axis_index("lat")
    start = pl.multiple_of(lat * rows, rows)
    here = pl.ds(start, rows)
    ew = tabs[EAST_WEST : EAST_WEST + 1, here]
    up = tabs[UPPER : UPPER + 1, here]
    lo = tabs[LOWER : LOWER + 1, here]
    row_lane = lane_ids(1, rows)
    near_r = jnp.concatenate([near1] * (rows // TILE), axis=1)
    far_r = jnp.concatenate([far1] * (rows // TILE), axis=1)
    mods = []
    for ext_row, inv_row in ((4 + lat, I0), (lat, I1)):
        e = -ew * ext[pl.ds(ext_row, 1), :rows]
        d = edges[inv_row : inv_row + 1, cols : cols + rows] * e
        above = jnp.where(row_lane == 0, 0.0, before(d))
        below = jnp.where(row_lane == rows - 1, 0.0, after(d))
        dv = e - up * above - lo * below - ew * ext[pl.ds(ext_row, 1), rows:]
        mods += [-far_r * d, far_r * dv - near_r * e, -far_r * ew * d]
    mods += [jnp.zeros((1, rows), jnp.float32)] * 2
    cols_t[...] = jnp.transpose(jnp.concatenate(mods, axis=0))

    near_c = jnp.concatenate([near1] * tiles, axis=1)
    far_c = jnp.concatenate([far1] * tiles, axis=1)
    col_lane = lane_ids(1, cols)
    row_mods = []
    for which, (band, place) in enumerate(
        ((jnp.maximum(lat - 1, 0), rows - 1), (jnp.minimum(lat + 1, 3), 0))
    ):
        beyond = [ext[pl.ds(4 + band, 1), :rows], ext[pl.ds(band, 1), :rows]]
        d, e, dv, inner_d = (row_parts[4 * which + i : 4 * which + i + 1, :] for i in range(4))

        def corner_of(side, lane):
            cell = corner[which : which + 1, lane : lane + 1] * beyond[side][:, place : place + 1]
            return wide(cell, cols)

        dv = dv + jnp.where(col_lane == 0, corner_of(0, 0), 0.0)
        dv = dv + jnp.where(col_lane == cols - 1, corner_of(1, TILE - 1), 0.0)
        row_mods.append((-far_c * d, far_c * dv - near_c * e, -far_c * inner_d))

    for i in [i for i in range(1, parts) if i not in early] + [0]:
        inner(i)
        edge(i)
        if i == 0:
            dx, dr, dr_next = row_mods[0]
            field_x[0:1, :] += dx
            field_r[0:1, :] += dr
            field_r[1:2, :] += dr_next
        if i == parts - 1:
            dx, dr, dr_next = row_mods[1]
            field_x[rows - 1 : rows, :] += dx
            field_r[rows - 1 : rows, :] += dr
            field_r[rows - 2 : rows - 1, :] += dr_next
        send(i, 0, cols)
        if i == parts - 1:
            for k in early:
                edge(k)
                send(k, 0, TILE)
                send(k, cols - TILE, cols)
    for copy in copies:
        copy.wait()


def shape(*dims):
    return jax.ShapeDtypeStruct(dims, jnp.float32)


def call(kernel, name, out_shape, in_specs, out_specs=None, scratch=(), limit=32, cost=None):
    return pl.pallas_call(
        kernel,
        name=name,
        out_shape=out_shape,
        in_specs=in_specs,
        out_specs=out_specs or [VMEM_SPEC] * len(out_shape),
        scratch_shapes=list(scratch),
        cost_estimate=cost,
        compiler_params=pltpu.CompilerParams(vmem_limit_bytes=limit << 20),
    )


def per_device(source, flags):
    rows, cols = source.shape
    bands, sectors = lax.axis_size("lat"), lax.axis_size("lon")
    height = rows * bands
    assert bands == 4
    z, u, w, edges, tabs, src, coef, folded = call(
        local_kernel,
        "local",
        [
            shape(cols // TILE, rows + 2 * SUB, TILE),
            shape(cols // TILE, rows + 2 * SUB, TILE),
            shape(rows, cols),
            shape(SUB, cols + rows + TILE),
            shape(SUB, height),
            shape(rows, cols),
            shape(3, rows, TILE),
            shape(SUB, 5 * rows),
        ],
        [HBM_SPEC, HBM_SPEC],
        scratch=[pltpu.VMEM((3, rows, TILE), jnp.float32)]
        + [pltpu.VMEM((rows, 2 * TILE), jnp.float32)]
        + [pltpu.SMEM(flags.shape, jnp.int32), pltpu.SemaphoreType.DMA((LOADS + 1,))],
    )(*(pltpu.with_memory_space_constraint(a, pltpu.HBM) for a in (flags, source)))

    def swap(pack, axis, stage):
        count = lax.axis_size(axis)
        return lax.ppermute(pack, axis, [(i, i ^ (1 << stage)) for i in range(count)])

    lat_stages = bands.bit_length() - 1
    lon_stages = sectors.bit_length() - 1
    pack, row_ext = edges, edges
    for stage in range(lat_stages):
        left = lat_stages - 1 - stage
        tall = (rows << (stage + 1)) + TILE + (cols, cols // 2, 0)[max(0, 2 - left)]
        pack, row_ext = call(
            functools.partial(lat_kernel, stage, lat_stages, cols),
            f"lat_merge{stage}",
            [shape(SUB, 3 * rows + TILE if left == 0 else tall), shape(SUB, 6 * cols // SUB)],
            [VMEM_SPEC] * 4,
            scratch=[pltpu.VMEM((SUB, tall), jnp.float32)] if left == 0 else (),
        )(tabs, pack, swap(pack, "lat", stage), row_ext)
        if stage == 0:
            v = call(
                image_kernel,
                "image",
                [shape(rows, cols)],
                [VMEM_SPEC] * 3 + [ANY_SPEC],
                cost=pl.CostEstimate(
                    flops=8 * rows * cols, bytes_accessed=12 * rows * cols, transcendentals=0
                ),
            )(u, w, coef, row_ext)[0]
    row_parts, corner = call(
        functools.partial(row_kernel, rows),
        "row_parts",
        [shape(SUB, cols), shape(SUB, TILE)],
        [VMEM_SPEC] * 3,
        cost=pl.CostEstimate(flops=60 * cols, bytes_accessed=64 * cols, transcendentals=0),
    )(tabs, edges, row_ext)
    col_ext = pack
    for stage in range(lon_stages - 1):
        pack, col_ext = call(
            functools.partial(lon_kernel, stage),
            f"lon_merge{stage}",
            [shape(SUB, 3 * rows + TILE), shape(SUB, 2 * rows)],
            [VMEM_SPEC] * 4,
        )(folded, pack, swap(pack, "lon", stage), col_ext)
    stage = lon_stages - 1
    x, r = call(
        functools.partial(last_kernel, stage, 32),
        "combine",
        [shape(rows, cols), shape(rows, cols)],
        [VMEM_SPEC] * 13,
        out_specs=[HBM_SPEC, HBM_SPEC],
        scratch=[
            pltpu.VMEM((SUB, TILE), jnp.float32),
            pltpu.VMEM((SUB, 2 * rows), jnp.float32),
            pltpu.VMEM((rows, cols), jnp.float32),
            pltpu.VMEM((rows, cols), jnp.float32),
            pltpu.VMEM((rows, SUB), jnp.float32),
            pltpu.SemaphoreType.DMA((2,)),
        ],
    )(tabs, folded, pack, swap(pack, "lon", stage), col_ext, edges, row_parts, corner, src, z, u, w, v)
    return x, r


def solution(mesh):
    in_specs = (P("lat", "lon"), P("lat", "lon"))
    out_specs = (P("lat", "lon"), P("lat", "lon"))
    return jax.shard_map(
        per_device, mesh=mesh, in_specs=in_specs, out_specs=out_specs, check_vma=False
    )
```

```python
import functools
import math

import jax
import jax.numpy as jnp
from jax import lax
from jax.experimental import pallas as pl
from jax.experimental.pallas import tpu as pltpu
from jax.sharding import PartitionSpec as P

ARC_SPAN = 2.0 * math.pi / 3.0
TILE = 128
SUB = 8
VMEM_SPEC = pl.BlockSpec(memory_space=pltpu.VMEM)
HBM_SPEC = pl.BlockSpec(memory_space=pltpu.HBM)
ANY_SPEC = pl.BlockSpec(memory_space=pl.ANY)
LOADS = 4
Z0, U0, V0, Z1, U1, V1, I0, I1 = range(8)
EAST_WEST, UPPER, LOWER, INNER = range(4)
WEST_KINDS, EAST_KINDS = 4, 5
SCREENS = (0.05, 0.4, 2.0)


def coefficient_table(total_rows):
    row_pos = lax.broadcasted_iota(jnp.int32, (SUB, total_rows), 1).astype(jnp.float32)
    kind = lax.broadcasted_iota(jnp.int32, (SUB, total_rows), 0)
    ahead = jnp.where(kind == EAST_WEST, 0.5, jnp.where(kind == UPPER, 0.0, 1.0))
    table = jnp.cos((row_pos + ahead) / total_rows * ARC_SPAN - 0.5 * ARC_SPAN)
    return jnp.where((kind == INNER) & (row_pos == total_rows - 1), 0.0, table)


def fold(row):
    total = row[:, :TILE]
    for start in range(TILE, row.shape[1], TILE):
        total = total + row[:, start : start + TILE]
    return total


def wide(cell, width=TILE):
    return jnp.broadcast_to(cell, (cell.shape[0], width))


def after(row):
    return pltpu.roll(row, row.shape[1] - 1, 1)


def before(row):
    return pltpu.roll(row, 1, 1)


def lane_ids(rows, width=TILE):
    return lax.broadcasted_iota(jnp.int32, (rows, width), 1)


def columns(c):
    return pl.ds(c * TILE, TILE)


def line_of(field, at, tiles):
    zero = jnp.zeros((SUB, TILE), jnp.float32)
    return [zero] + [field[c, pl.ds(at + SUB, SUB), :] for c in range(tiles)] + [zero]


def ahead_of(field, at, c, line, coeffs):
    here = line[c + 1]
    below = field[c, pl.ds(at + SUB + 1, SUB), :]
    right = pltpu.roll(jnp.where(lane_ids(SUB) == 0, line[c + 2], here), TILE - 1, 1)
    return right, coeffs[2] * below


def behind_of(field, at, c, line, coeffs):
    here = line[c + 1]
    above = field[c, pl.ds(at + SUB - 1, SUB), :]
    left = pltpu.roll(jnp.where(lane_ids(SUB) == TILE - 1, line[c], here), 1, 1)
    return left, coeffs[1] * above


def around(field, at, c, line, coeffs):
    right, below = ahead_of(field, at, c, line, coeffs)
    left, above = behind_of(field, at, c, line, coeffs)
    return coeffs[0] * (right + left) + (above + below)


def fold_place(row, c, eighth):
    sub, at = divmod(c * TILE, eighth)
    at += row * eighth
    return slice(sub, sub + 1), slice(at, at + TILE)


def next_cell(row):
    moved = pltpu.roll(row, row.shape[1] - 1, 1)
    ids = lane_ids(SUB, row.shape[1])
    return jnp.where(ids == row.shape[1] - 1, pltpu.roll(moved, SUB - 1, 0), moved)


def last_cell(row):
    moved = pltpu.roll(row, 1, 1)
    return jnp.where(lane_ids(SUB, row.shape[1]) == 0, pltpu.roll(moved, 1, 0), moved)


def cell_ids(width):
    return lax.broadcasted_iota(jnp.int32, (SUB, width), 0) * width + lane_ids(SUB, width)


def folded_tables(tabs, folded):
    quarter = folded.shape[1] // 5
    base = [tabs[i : i + 1, :] for i in (EAST_WEST, UPPER, LOWER)]
    rows = [base[0], tabs[INNER : INNER + 1, :]]
    rows += [1.0 / (screen + 2.0 * base[0] + base[1] + base[2]) for screen in SCREENS]
    for i, row in enumerate(rows):
        for q in range(4):
            piece = row[:, q * quarter : (q + 1) * quarter]
            folded[q : q + 1, i * quarter : (i + 1) * quarter] = piece
            folded[q + 4 : q + 5, i * quarter : (i + 1) * quarter] = piece


def local_kernel(
    flags_in, source, z, u, w, pack, tabs, src, coef, folded, inv, v_edge, flags, sems
):
    rows, cols = src.shape
    tiles = cols // TILE
    blocks = TILE // SUB
    parts = sems.shape[0] - 1
    chunk = rows // parts
    flag_copy = pltpu.make_async_copy(flags_in, flags, sems.at[parts])
    flag_copy.start()
    loads = []
    for i in range(parts):
        part = pl.ds(i * chunk, chunk)
        loads.append(pltpu.make_async_copy(source.at[part, :], src.at[part, :], sems.at[i]))
        if i < 2:
            loads[-1].start()
    tabs[...] = coefficient_table(tabs.shape[1])
    folded_tables(tabs[...], folded)
    start = pl.multiple_of(lax.axis_index("lat") * rows, rows)
    band = jnp.transpose(tabs[:, pl.ds(start, rows)])
    ew = wide(band[:, EAST_WEST : EAST_WEST + 1])
    up = wide(band[:, UPPER : UPPER + 1])
    lo = wide(band[:, LOWER : LOWER + 1])
    for i, values in enumerate((ew, up, lo)):
        coef[i] = values
    for kind, screen in enumerate(SCREENS):
        inv[kind] = 1.0 / (screen + 2.0 * ew + up + lo)
    nothing = jnp.zeros((tiles, SUB, TILE), jnp.float32)
    for padded in (z, u):
        padded[:, :SUB, :] = nothing
        padded[:, rows + SUB :, :] = nothing
    zero = jnp.zeros((SUB, TILE), jnp.float32)
    flag_copy.wait()
    kinds = [
        [
            jnp.where(flags[band_row, c] == 0, 0, jnp.where(flags[band_row, c] == 1, 1, 2))
            for c in range(tiles)
        ]
        for band_row in range(rows // TILE)
    ]

    def first_pass(at, kind, sums):
        part = zero
        for c in range(tiles):
            b = src[pl.ds(at, SUB), columns(c)]
            value = b * inv[kind[c], pl.ds(at, SUB), :]
            z[c, pl.ds(at + SUB, SUB), :] = value
            part = part + b * value
        return (sums[0] + part,) + sums[1:]

    def second_pass(at, kind, sums):
        part1, part2 = zero, zero
        here_rows = pl.ds(at, SUB)
        coeffs = [coef[i, here_rows, :] for i in range(3)]
        line = line_of(z, at, tiles)
        for c in range(tiles):
            image = src[here_rows, columns(c)] - around(z, at, c, line, coeffs)
            scaled = image * inv[kind[c], here_rows, :]
            w[here_rows, columns(c)] = image
            u[c, pl.ds(at + SUB, SUB), :] = scaled
            part1 = part1 + line[c + 1] * image
            part2 = part2 + scaled * image
        return sums[0], sums[1] + part1, sums[2] + part2, sums[3]

    def third_pass(at, kind, sums):
        part = zero
        here_rows = pl.ds(at, SUB)
        coeffs = [coef[i, here_rows, :] for i in range(3)]
        line = line_of(u, at, tiles)
        for c in range(tiles):
            right, below = ahead_of(u, at, c, line, coeffs)
            near = coeffs[0] * right + below
            image = w[here_rows, columns(c)]
            part = part + line[c + 1] * (image - (near + near))
            if c in (0, tiles - 1):
                left, above = behind_of(u, at, c, line, coeffs)
                edge = pl.ds(0 if c == 0 else TILE, TILE)
                v_edge[here_rows, edge] = image - near - (coeffs[0] * left + above)
        return sums[:3] + (sums[3] + part,)

    count = rows // SUB
    done = [0, 0, 0]
    sums = (zero,) * 4
    for i in range(parts):
        loads[i].wait()
        if i + 2 < parts:
            loads[i + 2].start()
        ready = (i + 1) * (chunk // SUB)
        for which, body in enumerate((first_pass, second_pass, third_pass)):
            upto = ready - which if i + 1 < parts else count
            while done[which] < upto:
                band_row = done[which] // blocks
                stop = min(upto, (band_row + 1) * blocks)

                def step(k, carry, body=body, band_row=band_row):
                    return body(pl.multiple_of(k * SUB, SUB), kinds[band_row], carry)

                sums = lax.fori_loop(done[which], stop, step, sums, unroll=stop - done[which])
                done[which] = stop
    m0, m1, m2, m3 = sums

    last = rows - 1
    def put(row, c, value):
        sub, lanes = fold_place(row, c, cols // SUB)
        pack[sub, lanes] = value

    for c in range(tiles):
        for field, first_row, last_row in ((z, Z0, Z1), (u, U0, U1)):
            put(first_row, c, field[c, SUB : SUB + 1, :])
            put(last_row, c, field[c, last + SUB : last + SUB + 1, :])
        put(I0, c, inv[kinds[0][c], :1, :])
        put(I1, c, inv[kinds[-1][c], last:, :])
    for at, v_row, place in ((0, V0, 0), (rows - SUB, V1, SUB - 1)):
        line = line_of(u, at, tiles)
        coeffs = [coef[i, at : at + SUB, :] for i in range(3)]
        for c in range(tiles):
            image = w[at : at + SUB, columns(c)] - around(u, at, c, line, coeffs)
            put(v_row, c, image[place : place + 1, :])

    for band_row in range(rows // TILE):
        here_rows = slice(band_row * TILE, (band_row + 1) * TILE)
        inner_rows = slice(band_row * TILE + SUB, (band_row + 1) * TILE + SUB)
        ids = lane_ids(TILE)
        mix = inv[kinds[band_row][-1], here_rows, :]
        mix = jnp.where(ids == I0, inv[kinds[band_row][0], here_rows, :], mix)
        mix = jnp.where(ids == V1, pltpu.roll(v_edge[here_rows, TILE:], V1 + 1, 1), mix)
        mix = jnp.where(ids == U1, pltpu.roll(u[tiles - 1, inner_rows, :], U1 + 1, 1), mix)
        mix = jnp.where(ids == Z1, pltpu.roll(z[tiles - 1, inner_rows, :], Z1 + 1, 1), mix)
        mix = jnp.where(ids == V0, pltpu.roll(v_edge[here_rows, :TILE], V0, 1), mix)
        mix = jnp.where(ids == U0, pltpu.roll(u[0, inner_rows, :], U0, 1), mix)
        mix = jnp.where(ids == Z0, z[0, inner_rows, :], mix)
        at = cols + band_row * TILE
        pack[:, at : at + TILE] = jnp.transpose(mix)[:SUB, :]

    at = cols + rows
    pack[:, at:] = zero
    for i, m in enumerate((m0, m1, m2, m3)):
        pack[i : i + 1, at:] = jnp.sum(m, axis=0, keepdims=True)
    band_start = lax.axis_index("lat") * (rows // TILE)
    for i, c in ((WEST_KINDS, 0), (EAST_KINDS, tiles - 1)):
        line = jnp.zeros((1, TILE), jnp.float32)
        for band_row in range(rows // TILE):
            kind = jnp.full((1, TILE), kinds[band_row][c], jnp.int32).astype(jnp.float32)
            line = jnp.where(lane_ids(1) == band_start + band_row, kind, line)
        pack[i : i + 1, at:] = line


def image_kernel(u, w, coef, after_stage, v):
    del after_stage
    rows, cols = w.shape
    tiles = cols // TILE
    unroll = 8

    def step(k, carry):
        at = pl.multiple_of(k * SUB, SUB)
        here_rows = pl.ds(at, SUB)
        coeffs = [coef[i, here_rows, :] for i in range(3)]
        line = line_of(u, at, tiles)
        for c in range(tiles):
            v[here_rows, columns(c)] = w[here_rows, columns(c)] - around(u, at, c, line, coeffs)
        return carry

    lax.fori_loop(0, rows // SUB, step, 0, unroll=unroll)


def row_kernel(rows, tabs, edges, row_ext, parts, corner):
    eighth = row_ext.shape[1] // 6
    cols = eighth * SUB
    height = tabs.shape[1]
    start = pl.multiple_of(lax.axis_index("lat") * rows, rows)
    cell = cell_ids(eighth)
    first = tabs[:, pl.ds(start, TILE)]
    final = tabs[:, pl.ds(start + rows - TILE, TILE)]
    tab_n = tabs[:, pl.ds(pl.multiple_of(jnp.maximum(start - TILE, 0), TILE), TILE)]
    tab_s = tabs[:, pl.ds(pl.multiple_of(jnp.minimum(start + rows, height - TILE), TILE), TILE)]
    for which in range(2):
        at = 3 * which
        if which == 0:
            lane, own_tab, next_tab, next_lane = 0, first, tab_n, TILE - 1
            cross_row, inner_row, inv_row = UPPER, LOWER, I0
        else:
            lane, own_tab, next_tab, next_lane = TILE - 1, final, tab_s, 0
            cross_row, inner_row, inv_row = LOWER, UPPER, I1

        def scalar(tab, row, place):
            return jnp.broadcast_to(tab[row : row + 1, place : place + 1], (SUB, eighth))

        def beyond(i):
            return row_ext[:, (at + i) * eighth : (at + i + 1) * eighth]

        cross = scalar(own_tab, cross_row, lane)
        inner = scalar(own_tab, inner_row, lane)
        ew_own = scalar(own_tab, EAST_WEST, lane)
        ew_next = scalar(next_tab, EAST_WEST, next_lane)
        e = -cross * beyond(0)
        d = edges[:, inv_row * eighth : (inv_row + 1) * eighth] * e
        right = jnp.where(cell == cols - 1, 0.0, next_cell(d))
        left = jnp.where(cell == 0, 0.0, last_cell(d))
        dv = e - ew_own * (right + left) - cross * beyond(1)
        for i, row in enumerate((d, e, dv, inner * d)):
            to = 4 * which + i
            for c in range(cols // TILE):
                sub, lanes = fold_place(0, c, eighth)
                parts[to : to + 1, columns(c)] = row[sub, lanes]
        k = cross * ew_next * beyond(2)
        ids = lane_ids(1)
        corner[which : which + 1, :] = jnp.where(
            ids == 0, k[:1, :TILE], k[SUB - 1 :, eighth - TILE :]
        )


def sides(own, other, index, stage):
    size = 2**stage
    lower = lax.rem(lax.div(index, size), 2)
    inside = lax.rem(index, size)
    here, there = own[...], other[...]
    first = jnp.where(lower == 0, here, there)
    second = jnp.where(lower == 0, there, here)
    at_end = (lower == 0) & (inside == size - 1)
    at_start = (lower == 1) & (inside == 0)
    return first, second, at_end, at_start


def row_of(pack, i, start, stop):
    return pack[i : i + 1, start:stop]


def add_moments(out, at, first, second, changes):
    width = first.shape[1]
    out[:, at : at + TILE] = first[:, width - TILE :] + second[:, width - TILE :]
    for i, change in enumerate(changes):
        out[i + 1 : i + 2, at : at + TILE] += change


def lat_kernel(stage, stages, cols, tabs, own, other, ext_in, result, ext, *scratch):
    out = scratch[0] if scratch else result
    facing = 0 < stage == stages - 1
    final = stage == stages - 1
    eighth = cols // SUB
    span = 4 * eighth if facing else cols
    height = own.shape[1] - span - TILE
    index = lax.axis_index("lat")
    top, bottom, at_end, at_start = sides(own, other, index, stage)
    size = 2**stage
    border = pl.multiple_of((lax.div(index, 2 * size) * 2 * size + size) * (height // size), TILE)
    low = tabs[:, pl.ds(border, TILE)]
    high = tabs[:, pl.ds(border - TILE, TILE)]
    cross = jnp.broadcast_to(low[UPPER : UPPER + 1, :1], (SUB, eighth))
    ew_b = wide(low[EAST_WEST : EAST_WEST + 1, :1])
    ew_t = wide(high[EAST_WEST : EAST_WEST + 1, TILE - 1 :])
    next_b = wide(low[LOWER : LOWER + 1, :1])
    next_t = wide(high[UPPER : UPPER + 1, TILE - 1 :])

    def block(pack, i):
        return pack[:, i * eighth : (i + 1) * eighth]

    zt, ut, vt, it = (block(top, i) for i in (range(4) if facing else (Z1, U1, V1, I1)))
    zb, ub, vb, ib = (block(bottom, i) for i in (range(4) if facing else (Z0, U0, V0, I0)))
    et, eb = -cross * zb, -cross * zt
    dt, db = it * et, ib * eb
    full_t, full_b = ut + dt, ub + db
    inside = cell_ids(eighth) < cols - 1
    pair_t = jnp.where(inside, dt * next_cell(dt), 0.0)
    pair_b = jnp.where(inside, db * next_cell(db), 0.0)

    def total(x):
        return jnp.sum(fold(x), axis=0, keepdims=True)

    twice = total(zt * et)
    second = total((2.0 * ut + dt) * et + (2.0 * ub + db) * eb)
    third = total(dt * (2.0 * vt + et) + db * (2.0 * vb + eb) - 2.0 * cross * full_t * full_b)
    third = third - 2.0 * (ew_t * total(pair_t) + ew_b * total(pair_b))

    if final:
        base = 0
    elif stage + 1 == stages - 1:
        base = 4 * eighth
        up_next = lax.rem(lax.div(index, 2 * size), 2) == 0
        for i, (first_row, last_row) in enumerate(((Z0, Z1), (U0, U1), (V0, V1), (I0, I1))):
            out[:, i * eighth : (i + 1) * eighth] = jnp.where(
                up_next, block(bottom, last_row), block(top, first_row)
            )
    else:
        base = cols
        for i in range(8):
            side = top if i in (Z0, U0, V0, I0) else bottom
            out[:, i * eighth : (i + 1) * eighth] = block(side, i)
    out[:, base : base + height] = top[:, span : span + height]
    out[:, base + height : base + 2 * height] = bottom[:, span : span + height]
    add_moments(out, base + 2 * height, top, bottom, (2.0 * twice, second, third))

    lane = lane_ids(1)
    upper_at = base + height - TILE
    lower_at = base + height
    c = cross[:1, :TILE]
    for edge, inner, u_row, v_row in ((0, 1, U0, V0), (cols - 1, cols - 2, U1, V1)):

        def pick(row, place):
            sub, lane_at = divmod(place, eighth)
            return wide(row[sub : sub + 1, lane_at : lane_at + 1])

        d_top, d_bottom = pick(dt, edge), pick(db, edge)
        v_top = pick(et, edge) - ew_t * pick(dt, inner) - c * pick(full_b, edge)
        v_bottom = pick(eb, edge) - ew_b * pick(db, inner) - c * pick(full_t, edge)
        out[u_row : u_row + 1, upper_at : upper_at + TILE] += jnp.where(
            lane == TILE - 1, d_top, 0.0
        )
        out[u_row : u_row + 1, lower_at : lower_at + TILE] += jnp.where(lane == 0, d_bottom, 0.0)
        out[v_row : v_row + 1, upper_at : upper_at + TILE] += jnp.where(
            lane == TILE - 1, v_top, jnp.where(lane == TILE - 2, -next_t * d_top, 0.0)
        )
        out[v_row : v_row + 1, lower_at : lower_at + TILE] += jnp.where(
            lane == 0, v_bottom, jnp.where(lane == 1, -next_b * d_bottom, 0.0)
        )

    if final:
        quarter = 2 * height // 4
        for i, row in enumerate((Z0, U0, V0, Z1, U1, V1)):
            part = slice((i % 3) * quarter, (i % 3 + 1) * quarter)
            for q in range(4):
                to = q + 4 * (i // 3)
                result[to : to + 1, part] = out[row : row + 1, q * quarter : (q + 1) * quarter]
        result[:, 3 * quarter :] = out[:, 2 * height :]

    if stage == 0:
        ext[...] = jnp.zeros(ext.shape, jnp.float32)
    else:
        ext[...] = ext_in[...]

    def keep(first_block, values):
        for i, value in enumerate(values):
            at = (first_block + i) * eighth
            ext[:, at : at + eighth] = value

    @pl.when(at_start)
    def _():
        keep(0, (zt, full_t, it))

    @pl.when(at_end)
    def _():
        keep(3, (zb, full_b, ib))


def halves(quarter):
    return lax.broadcasted_iota(jnp.int32, (SUB, quarter), 0) < 4


def column_border(west, east, folded):
    quarter = (west.shape[1] - TILE) // 3
    low = halves(quarter)
    z, u, v = (
        jnp.where(low, east[:, part], west[:, part])
        for part in (slice(i * quarter, (i + 1) * quarter) for i in range(3))
    )
    ew, inner, *inverses = (folded[:, i * quarter : (i + 1) * quarter] for i in range(5))
    tiles = 4 * quarter // TILE
    each = tiles // 4
    east_kinds = jnp.broadcast_to(east[WEST_KINDS : WEST_KINDS + 1, 3 * quarter :], (SUB, TILE))
    west_kinds = jnp.broadcast_to(west[EAST_KINDS : EAST_KINDS + 1, 3 * quarter :], (SUB, TILE))
    kinds = jnp.where(halves(TILE), east_kinds, west_kinds)
    sub = lax.broadcasted_iota(jnp.int32, (SUB, TILE), 0)
    first = each * jnp.where(sub < 4, sub, sub - 4)
    spread = []
    for h in range(each):
        here = jnp.where(lane_ids(SUB) == first + h, kinds, 0.0)
        spread.append(wide(jnp.sum(here, axis=1, keepdims=True)))
    kind = jnp.concatenate(spread, axis=1)
    inv = jnp.where(kind < 0.5, inverses[0], jnp.where(kind < 1.5, inverses[1], inverses[2]))

    def across(x):
        return pltpu.roll(x, 4, 0)

    e = -ew * across(z)
    d = inv * e
    full = u + d
    along = next_cell(d)
    first_sum = fold(z * e)
    second = fold((u + full) * e)
    third = fold(d * (2.0 * v + e) - 2.0 * inner * d * along - ew * full * across(full))
    changes = [jnp.sum(x, axis=0, keepdims=True) for x in (first_sum, second, third)]
    return changes, jnp.concatenate([z, full], axis=1)


def merge_tiles(west, east):
    at = west.shape[1] - TILE
    ids = lax.broadcasted_iota(jnp.int32, (SUB, TILE), 0)
    kinds = jnp.where(ids == WEST_KINDS, west[:, at:], east[:, at:])
    return jnp.where(ids < WEST_KINDS, west[:, at:] + east[:, at:], kinds)


def keep_ext(ext, found, at_start, at_end):
    @pl.when(at_end)
    def _():
        ext[:4, :] = found[:4, :]

    @pl.when(at_start)
    def _():
        ext[4:, :] = found[4:, :]


def lon_kernel(stage, folded, own, other, ext_in, out, ext):
    at = own.shape[1] - TILE
    west, east, at_end, at_start = sides(own, other, lax.axis_index("lon"), stage)
    changes, found = column_border(west, east, folded)
    out[:, :at] = jnp.where(halves(at), west[:, :at], east[:, :at])
    out[:, at:] = merge_tiles(west, east)
    for i, change in enumerate(changes):
        out[i + 1 : i + 2, at:] += change
    if stage == 0:
        ext[...] = jnp.zeros(ext.shape, jnp.float32)
    else:
        ext[...] = ext_in[...]
    keep_ext(ext, found, at_start, at_end)


def last_kernel(
    stage, chunk, tabs, folded, own, other, ext_in, edges, row_parts, corner, src, z, u, w, v,
    out_x, out_r, mom, ext, field_x, field_r, cols_t, sems,
):
    rows, cols = src.shape
    height = tabs.shape[1]
    tiles = cols // TILE
    sectors = lax.axis_size("lon")
    index = lax.axis_index("lon")
    west, east, at_end, at_start = sides(own, other, index, stage)
    changes, found = column_border(west, east, folded)
    wrap, round_found = column_border(east, west, folded)
    mom[...] = merge_tiles(west, east)
    for i, (change, other_change) in enumerate(zip(changes, wrap)):
        mom[i + 1 : i + 2, :] += change + other_change
    if stage == 0:
        ext[...] = jnp.zeros(ext.shape, jnp.float32)
    else:
        ext[...] = ext_in[...]
    keep_ext(ext, found, at_start, at_end)
    keep_ext(ext, round_found, index == 0, index == sectors - 1)

    sums = jnp.broadcast_to(jnp.sum(mom[...], axis=1, keepdims=True), (SUB, TILE))
    m0, m1, m2, m3 = (sums[i : i + 1, :] for i in range(4))
    alpha = m0 / m1
    fresh = alpha * alpha * m2 - 2.0 * alpha * m1 + m0
    grow = 1.0 + fresh / m0
    bend = grow * grow * m1 - 2.0 * grow * alpha * m2 + alpha * alpha * m3
    beta = fresh / bend
    near1, far1 = alpha + beta * grow, alpha * beta
    near = jnp.broadcast_to(near1, (SUB, TILE))
    far = jnp.broadcast_to(far1, (SUB, TILE))

    lat = lax.axis_index("lat")
    start = pl.multiple_of(lat * rows, rows)
    here = pl.ds(start, rows)
    ew = tabs[EAST_WEST : EAST_WEST + 1, here]
    up = tabs[UPPER : UPPER + 1, here]
    lo = tabs[LOWER : LOWER + 1, here]
    row_lane = lane_ids(1, rows)
    near_r = jnp.concatenate([near1] * (rows // TILE), axis=1)
    far_r = jnp.concatenate([far1] * (rows // TILE), axis=1)
    mods = []
    for ext_row, inv_row in ((4 + lat, I0), (lat, I1)):
        e = -ew * ext[pl.ds(ext_row, 1), :rows]
        d = edges[inv_row : inv_row + 1, cols : cols + rows] * e
        above = jnp.where(row_lane == 0, 0.0, before(d))
        below = jnp.where(row_lane == rows - 1, 0.0, after(d))
        dv = e - up * above - lo * below - ew * ext[pl.ds(ext_row, 1), rows:]
        mods += [-far_r * d, far_r * dv - near_r * e, -far_r * ew * d]
    mods += [jnp.zeros((1, rows), jnp.float32)] * 2
    cols_t[...] = jnp.transpose(jnp.concatenate(mods, axis=0))

    near_c = jnp.concatenate([near1] * tiles, axis=1)
    far_c = jnp.concatenate([far1] * tiles, axis=1)
    col_lane = lane_ids(1, cols)
    row_mods = []
    for which, (band, place) in enumerate(
        ((jnp.maximum(lat - 1, 0), rows - 1), (jnp.minimum(lat + 1, 3), 0))
    ):
        beyond = [ext[pl.ds(4 + band, 1), :rows], ext[pl.ds(band, 1), :rows]]
        d, e, dv, inner_d = (row_parts[4 * which + i : 4 * which + i + 1, :] for i in range(4))

        def corner_of(side, lane):
            cell = corner[which : which + 1, lane : lane + 1] * beyond[side][:, place : place + 1]
            return wide(cell, cols)

        dv = dv + jnp.where(col_lane == 0, corner_of(0, 0), 0.0)
        dv = dv + jnp.where(col_lane == cols - 1, corner_of(1, TILE - 1), 0.0)
        row_mods.append((-far_c * d, far_c * dv - near_c * e, -far_c * inner_d))

    lane = lane_ids(SUB)
    blocks = chunk // SUB

    def copies(i):
        part = pl.ds(pl.multiple_of(i * chunk, SUB), chunk)
        return (
            pltpu.make_async_copy(field_x.at[part, :], out_x.at[part, :], sems.at[0]),
            pltpu.make_async_copy(field_r.at[part, :], out_r.at[part, :], sems.at[1]),
        )

    def step(k, carry):
        at = pl.multiple_of(k * SUB, SUB)
        here = pl.ds(at, SUB)
        lines = cols_t[here, :]
        for c in range(tiles):
            part = pl.ds(c * TILE, TILE)
            x = near * z[c, pl.ds(at + SUB, SUB), :] - far * u[c, pl.ds(at + SUB, SUB), :]
            r = src[here, part] - near * w[here, part] + far * v[here, part]
            if c == 0:
                x = x + jnp.where(lane == 0, wide(lines[:, 0:1]), 0.0)
                r = r + jnp.where(
                    lane == 0, wide(lines[:, 1:2]), jnp.where(lane == 1, wide(lines[:, 2:3]), 0.0)
                )
            if c == tiles - 1:
                x = x + jnp.where(lane == TILE - 1, wide(lines[:, 3:4]), 0.0)
                r = r + jnp.where(
                    lane == TILE - 1,
                    wide(lines[:, 4:5]),
                    jnp.where(lane == TILE - 2, wide(lines[:, 5:6]), 0.0),
                )
            field_x[here, part] = x
            field_r[here, part] = r
        return carry

    parts = rows // chunk
    for i in range(parts):
        lax.fori_loop(i * blocks, (i + 1) * blocks, step, 0, unroll=blocks)
        if i == 0:
            dx, dr, dr_next = row_mods[0]
            field_x[0:1, :] += dx
            field_r[0:1, :] += dr
            field_r[1:2, :] += dr_next
        if i == parts - 1:
            dx, dr, dr_next = row_mods[1]
            field_x[rows - 1 : rows, :] += dx
            field_r[rows - 1 : rows, :] += dr
            field_r[rows - 2 : rows - 1, :] += dr_next
        for copy in copies(i):
            copy.start()
    for i in range(parts):
        for copy in copies(i):
            copy.wait()


def shape(*dims):
    return jax.ShapeDtypeStruct(dims, jnp.float32)


def call(kernel, name, out_shape, in_specs, out_specs=None, scratch=(), limit=32, cost=None):
    return pl.pallas_call(
        kernel,
        name=name,
        out_shape=out_shape,
        in_specs=in_specs,
        out_specs=out_specs or [VMEM_SPEC] * len(out_shape),
        scratch_shapes=list(scratch),
        cost_estimate=cost,
        compiler_params=pltpu.CompilerParams(vmem_limit_bytes=limit << 20),
    )


def per_device(source, flags):
    rows, cols = source.shape
    bands, sectors = lax.axis_size("lat"), lax.axis_size("lon")
    height = rows * bands
    assert bands == 4
    z, u, w, edges, tabs, src, coef, folded = call(
        local_kernel,
        "local",
        [
            shape(cols // TILE, rows + 2 * SUB, TILE),
            shape(cols // TILE, rows + 2 * SUB, TILE),
            shape(rows, cols),
            shape(SUB, cols + rows + TILE),
            shape(SUB, height),
            shape(rows, cols),
            shape(3, rows, TILE),
            shape(SUB, 5 * rows),
        ],
        [HBM_SPEC, HBM_SPEC],
        scratch=[pltpu.VMEM((3, rows, TILE), jnp.float32)]
        + [pltpu.VMEM((rows, 2 * TILE), jnp.float32)]
        + [pltpu.SMEM(flags.shape, jnp.int32), pltpu.SemaphoreType.DMA((LOADS + 1,))],
    )(*(pltpu.with_memory_space_constraint(a, pltpu.HBM) for a in (flags, source)))

    def swap(pack, axis, stage):
        count = lax.axis_size(axis)
        return lax.ppermute(pack, axis, [(i, i ^ (1 << stage)) for i in range(count)])

    lat_stages = bands.bit_length() - 1
    lon_stages = sectors.bit_length() - 1
    pack, row_ext = edges, edges
    for stage in range(lat_stages):
        left = lat_stages - 1 - stage
        tall = (rows << (stage + 1)) + TILE + (cols, cols // 2, 0)[max(0, 2 - left)]
        pack, row_ext = call(
            functools.partial(lat_kernel, stage, lat_stages, cols),
            f"lat_merge{stage}",
            [shape(SUB, 3 * rows + TILE if left == 0 else tall), shape(SUB, 6 * cols // SUB)],
            [VMEM_SPEC] * 4,
            scratch=[pltpu.VMEM((SUB, tall), jnp.float32)] if left == 0 else (),
        )(tabs, pack, swap(pack, "lat", stage), row_ext)
        if stage == 0:
            v = call(
                image_kernel,
                "image",
                [shape(rows, cols)],
                [VMEM_SPEC] * 3 + [ANY_SPEC],
                cost=pl.CostEstimate(
                    flops=8 * rows * cols, bytes_accessed=12 * rows * cols, transcendentals=0
                ),
            )(u, w, coef, row_ext)[0]
    row_parts, corner = call(
        functools.partial(row_kernel, rows),
        "row_parts",
        [shape(SUB, cols), shape(SUB, TILE)],
        [VMEM_SPEC] * 3,
        cost=pl.CostEstimate(flops=60 * cols, bytes_accessed=64 * cols, transcendentals=0),
    )(tabs, edges, row_ext)
    col_ext = pack
    for stage in range(lon_stages - 1):
        pack, col_ext = call(
            functools.partial(lon_kernel, stage),
            f"lon_merge{stage}",
            [shape(SUB, 3 * rows + TILE), shape(SUB, 2 * rows)],
            [VMEM_SPEC] * 4,
        )(folded, pack, swap(pack, "lon", stage), col_ext)
    stage = lon_stages - 1
    x, r = call(
        functools.partial(last_kernel, stage, 32),
        "combine",
        [shape(rows, cols), shape(rows, cols)],
        [VMEM_SPEC] * 13,
        out_specs=[HBM_SPEC, HBM_SPEC],
        scratch=[
            pltpu.VMEM((SUB, TILE), jnp.float32),
            pltpu.VMEM((SUB, 2 * rows), jnp.float32),
            pltpu.VMEM((rows, cols), jnp.float32),
            pltpu.VMEM((rows, cols), jnp.float32),
            pltpu.VMEM((rows, SUB), jnp.float32),
            pltpu.SemaphoreType.DMA((2,)),
        ],
    )(tabs, folded, pack, swap(pack, "lon", stage), col_ext, edges, row_parts, corner, src, z, u, w, v)
    return x, r


def solution(mesh):
    in_specs = (P("lat", "lon"), P("lat", "lon"))
    out_specs = (P("lat", "lon"), P("lat", "lon"))
    return jax.shard_map(
        per_device, mesh=mesh, in_specs=in_specs, out_specs=out_specs, check_vma=False
    )
```
